256 devices in a mesh: seq: 32 (over x, y, core), ch: 8 (over z).
Axes of the slice: x: 4, y: 4, z: 8, core: 2. Of those that a mesh axis runs over, the one named last changes fastest.
Arguments:
- inputs: bfloat16 [256, 131072], P('ch', 'seq'), may hold values from -6 to 6
- w_in: bfloat16 [3, 256, 256], P(None, 'ch'), may hold values from -0.375 to 0.375
- b_in: float32 [3, 256], P(None, 'ch'), may hold values from -3 to 3
- short_kernel: float32 [3, 256, 3], P(None, 'ch'), may hold values from -1 to 1
- positional: float32 [5, 131072], P(None, 'seq'), may hold values from -3.5 to 3.5
- filter_in: float32 [64, 5], replicated, may hold values from -4 to 4
- filter_bias: float32 [3, 64], replicated, may hold values from -4 to 4
- filter_freq: float32 [3, 64], replicated, may hold values from 0.5 to 2
- filter_hidden: float32 [2, 64, 64], replicated, may hold values from -0.75 to 0.75
- filter_out: float32 [256, 64], P('ch'), may hold values from -0.01171875 to 0.01171875
- decay: float32 [256], P('ch'), may hold values from 0.05 to 8
- conv_bias: float32 [256], P('ch'), may hold values from -1.5 to 1.5
- w_out: bfloat16 [256, 256], replicated, may hold values from -0.375 to 0.375
- b_out: float32 [256], P('ch'), may hold values from -3 to 3
Outputs:
- outputs: bfloat16 [256, 131072], P('ch', 'seq')
The draws below stay inside these ranges and needn't reach their ends.
All inputs are finite; a program needn't handle non-finite values.
Results may differ from the reference program's by a relative error of at most 0.005.
Values may be sent and summed in bfloat16 or wider, within the bound.
A program may use at most 64 MiB of HBM per device.

```python
import math
import jax
import jax.numpy as jnp
from jax import lax

D = 256
ORDER = 64
EMB = 5
TOK_DEV = 4096
LENGTH = 131072


def draw_positional(key, part):
    places = jnp.arange(LENGTH).astype(jnp.float32)
    phases = places * (2.0 * math.pi / LENGTH)
    smooth_part = jnp.stack([places / (LENGTH - 1), jnp.cos(0.0001 * phases), jnp.cos(phases), -jnp.sin(0.0001 * phases), -jnp.sin(phases)])
    jitter = 0.8 * jax.random.truncated_normal(key, -3.0, 3.0, (EMB, LENGTH), jnp.float32)
    return smooth_part + jitter


def block_scale(stream_key, shape, pieces, low, top_value):
    factor_of = 1.0
    for axis_at, parts in pieces:
        steps = jax.random.uniform(jax.random.fold_in(jax.random.fold_in(stream_key, 6), axis_at), (parts,), jnp.float32, low / len(pieces), top_value / len(pieces))
        factor_of = factor_of * jnp.repeat(jnp.exp(steps), shape[axis_at] // parts).reshape((-1,) + (1,) * (len(shape) - 1 - axis_at))
    return factor_of


def gaussian(stream_key, dims, spread, most, cuts=(), kind=jnp.bfloat16):
    gain = block_scale(stream_key, dims, cuts, -0.22, 0.18) if cuts else 1.0
    array = jax.random.normal(stream_key, dims, jnp.float32) * spread * gain
    return jnp.minimum(jnp.maximum(array, -most), most).astype(kind)


def setup_inputs(seed: int = 0) -> dict:
    arg_keys = jax.random.split(jax.random.key(seed), 15)
    return {
        "inputs": gaussian(arg_keys[0], (D, LENGTH), 1.0, 6.0, ((0, 8), (1, 32))),
        "w_in": gaussian(arg_keys[1], (3, D, D), D ** -0.5, 0.375, ((1, 8),)),
        "b_in": gaussian(arg_keys[2], (3, D), 0.5, 3.0, ((1, 8),), jnp.float32),
        "short_kernel": jnp.clip(jax.random.uniform(arg_keys[3], (3, D, 3), jnp.float32, -1.0, 1.0) * block_scale(arg_keys[3], (3, D, 3), ((1, 8),), -0.4, 0.0), -1.0, 1.0),
        "positional": draw_positional(jax.random.fold_in(arg_keys[14], 71), 0),
        "filter_in": gaussian(arg_keys[5], (ORDER, EMB), 1.0, 4.0, (), jnp.float32),
        "filter_bias": gaussian(arg_keys[6], (3, ORDER), 1.0, 4.0, (), jnp.float32),
        "filter_freq": jnp.clip(jnp.exp(jax.random.uniform(arg_keys[7], (3, ORDER), jnp.float32, math.log(0.5), math.log(2.0))), 0.5, 2.0),
        "filter_hidden": gaussian(arg_keys[8], (2, ORDER, ORDER), ORDER ** -0.5, 0.75, (), jnp.float32),
        "filter_out": gaussian(arg_keys[9], (D, ORDER), (ORDER * TOK_DEV) ** -0.5, 0.01171875, ((0, 8),), jnp.float32),
        "decay": jnp.clip(jnp.exp(math.log(8.0) - 5.075174 * jax.random.uniform(arg_keys[10], (D,), jnp.float32) ** block_scale(arg_keys[10], (D,), ((0, 8),), -0.2, 0.2)), 0.05, 8.0),
        "conv_bias": gaussian(arg_keys[11], (D,), 0.3, 1.5, ((0, 8),), jnp.float32),
        "w_out": gaussian(arg_keys[12], (D, D), D ** -0.5, 0.375),
        "b_out": gaussian(arg_keys[13], (D,), 0.5, 3.0, ((0, 8),), jnp.float32),
    }


HIGHEST = lax.Precision.HIGHEST


def filter_values(positional, positions, length, filter_in, filter_bias, filter_freq, filter_hidden, filter_out, decay):
    activity = jnp.sin(filter_freq[0][:, None] * (jnp.dot(filter_in, positional, precision=HIGHEST) + filter_bias[0][:, None]))
    for hidden_layer in range(2):
        inner = jnp.dot(filter_hidden[hidden_layer], activity, precision=HIGHEST) + filter_bias[hidden_layer + 1][:, None]
        activity = jnp.sin(filter_freq[hidden_layer + 1][:, None] * inner)
    scaled = positions / (length - 1)
    return jnp.dot(filter_out, activity, precision=HIGHEST) * jnp.exp(-(scaled[None, :] * decay[:, None]))


def long_conv(gated, kernel):
    channels, length = gated.shape
    block = min(32, channels)

    def one_block(pair):
        spectrum = jnp.fft.rfft(pair[0], n=2 * length) * jnp.fft.rfft(pair[1], n=2 * length)
        return jnp.fft.irfft(spectrum, n=2 * length)[:, :length]

    shaped = (gated.reshape(channels // block, block, length), kernel.reshape(channels // block, block, length))
    return lax.map(one_block, shaped).reshape(channels, length)


def reference(inputs, w_in, b_in, short_kernel, positional, filter_in, filter_bias, filter_freq, filter_hidden, filter_out, decay, conv_bias, w_out, b_out):
    length = inputs.shape[1]
    streams = []
    for stream_index in range(3):
        projected = jnp.dot(w_in[stream_index], inputs, preferred_element_type=jnp.float32) + b_in[stream_index][:, None]
        padded = jnp.pad(projected, ((0, 0), (2, 0)))
        taps = short_kernel[stream_index]
        shorted = taps[:, 0:1] * padded[:, 0:length] + taps[:, 1:2] * padded[:, 1:length + 1] + taps[:, 2:3] * padded[:, 2:length + 2]
        streams.append(shorted)
    gated = streams[2] * streams[1]
    positions = jnp.arange(length).astype(jnp.float32)
    kernel = filter_values(positional, positions, length, filter_in, filter_bias, filter_freq, filter_hidden, filter_out, decay)
    convolved = long_conv(gated, kernel) + conv_bias[:, None] * gated
    mixed = (streams[0] * convolved).astype(jnp.bfloat16)
    summed = jnp.dot(w_out, mixed, preferred_element_type=jnp.float32)
    return (summed + b_out[:, None]).astype(jnp.bfloat16)
```

```python
import math

import jax
import jax.numpy as jnp
import numpy as np
from jax import lax
from jax.experimental import pallas as pl
from jax.experimental.pallas import tpu as pltpu
from jax.sharding import PartitionSpec as P

MESH = pl.DeviceIdType.MESH
F32 = jnp.float32
BF16 = jnp.bfloat16
HIGHEST = lax.Precision.HIGHEST

SEQ, CH = 32, 8
DEV = SEQ * CH
D = 256
OWN = D // CH
SPAN = 4096
CHUNK = SPAN // CH
LENGTH = SPAN * SEQ
HALO = 128
LANES = 128
RADIX = CHUNK // LANES
ORDER = 64
BIAS, TAPS, DECAY, DIRECT, OUTB = 64, 67, 76, 77, 78


def halves(table):
    high = np.asarray(table, np.float64).astype(jnp.bfloat16)
    low = (np.asarray(table, np.float64) - high.astype(np.float64)).astype(jnp.bfloat16)
    return high, low


def tables():
    rows = np.arange(D)
    f1 = np.arange(D) + 0.25
    angle = 2.0 * np.pi * ((np.outer(4 * f1, rows) % (4 * D)) / (4 * D))
    first = np.concatenate([np.cos(angle), -np.sin(angle)], axis=0)
    first_stack = np.concatenate(halves(first), axis=0)
    last_stack = np.concatenate(halves(first.T / LENGTH), axis=0)
    lanes = np.arange(LANES)
    inner = 2.0 * np.pi * (np.outer(lanes, lanes) % LANES) / LANES
    c, s = np.cos(inner), np.sin(inner)
    forward = np.stack(halves(np.block([[c, -s], [s, c]])))
    inverse = np.stack(halves(np.block([[c, s], [-s, c]])))
    shift = f1[:, None] + D * np.arange(RADIX)[None, :]
    turn = 2.0 * np.pi / LENGTH * shift[:, :, None] * lanes[None, None, :]
    turn = turn.reshape(D, CHUNK)
    twiddle = np.stack([np.cos(turn), np.sin(turn)]).astype(np.float32)
    spin = 2.0 * np.pi / (RADIX * D) * f1[:, None] * np.arange(RADIX)[None, :]
    spins = np.zeros((D, LANES), np.float32)
    spins[:, 0:RADIX] = np.cos(spin)
    spins[:, RADIX : 2 * RADIX] = np.sin(spin)
    return first_stack, last_stack, forward, inverse, twiddle, spins


def split(x):
    high = x.astype(BF16)
    return high, (x - high.astype(F32)).astype(BF16)


def mm(a, b):
    return jnp.dot(a, b, preferred_element_type=F32)


def kernel(
    x_ref,
    w_ref,
    prm_ref,
    pos_ref,
    net_ref,
    hid_ref,
    wout_ref,
    first_ref,
    last_ref,
    fwd_ref,
    inv_ref,
    twid_ref,
    spin_ref,
    out_ref,
    xc,
    wbuf,
    pbuf,
    proj,
    stage,
    keep0,
    keepg,
    snd,
    rcv,
    first_v,
    last_v,
    fwd_v,
    inv_v,
    twid_v,
    spin_v,
    sect,
    chi,
    clo,
    back,
    dhi,
    dlo,
    ystage,
    ysnd,
    yrcv,
    osnd,
    const_sem,
    s1,
    rx,
    rh,
    rw,
    rp,
    s3,
    r3,
    s5,
    r5,
    s6,
    r6,
    ):
    s = lax.axis_index("seq")
    c = lax.axis_index("ch")
    me = s * CH + c
    own = pl.multiple_of(c * OWN, OWN)
    rows_own = pl.ds(own, OWN)

    consts = [
        pltpu.make_async_copy(src, dst, const_sem.at[i])
        for i, (src, dst) in enumerate(
            [
                (first_ref, first_v),
                (last_ref, last_v),
                (fwd_ref, fwd_v),
                (inv_ref, inv_v),
                (twid_ref, twid_v),
                (spin_ref, spin_v),
            ]
        )
    ]

    def put(src, dst, send, recv, to):
        pltpu.make_async_remote_copy(
            src_ref=src, dst_ref=dst, send_sem=send, recv_sem=recv, device_id=to, device_id_type=MESH
        ).start()

    x_dst = xc.at[rows_own, pl.ds(HALO, CHUNK)]
    h_dst = xc.at[rows_own, pl.ds(0, HALO)]
    w_dst = wbuf.at[:, rows_own, :]
    p_dst = pbuf.at[rows_own, :]
    for i in range(1, CH):
        j = lax.rem(c + i, CH)
        put(prm_ref, p_dst, s1.at[3], rp, (s, j))
    for i in range(1, CH):
        j = lax.rem(c + i, CH)
        put(
            x_ref.at[:, pl.ds(pl.multiple_of(j * CHUNK, CHUNK), CHUNK)], x_dst, s1.at[0], rx, (s, j)
        )
        put(w_ref, w_dst, s1.at[2], rw, (s, j))

    def tail(j):
        return x_ref.at[:, pl.ds(pl.multiple_of(j * CHUNK + CHUNK - HALO, HALO), HALO)]

    for i in range(1, CH):
        j = lax.rem(c + i, CH)

        @pl.when(j > 0)
        def _():
            put(tail(j - 1), h_dst, s1.at[1], rh, (s, j))

    @pl.when(s < SEQ - 1)
    def _():
        put(tail(CH - 1), h_dst, s1.at[1], rh, (s + 1, 0))

    pltpu.make_async_copy(
        x_ref.at[:, pl.ds(pl.multiple_of(c * CHUNK, CHUNK), CHUNK)], x_dst, rx
    ).start()
    pltpu.make_async_copy(w_ref, w_dst, rw).start()
    pltpu.make_async_copy(prm_ref, p_dst, rp).start()

    @pl.when(c > 0)
    def _():
        pltpu.make_async_copy(tail(c - 1), h_dst, rh).start()

    @pl.when(me == 0)
    def _():
        xc[:, 0:HALO] = jnp.zeros((D, HALO), BF16)

    for copy in consts:
        copy.start()

    here = pl.ds(pl.multiple_of(c * CHUNK, CHUNK), CHUNK)
    net = net_ref[...]
    inner = net[:, 0:1] * pos_ref[0:1, here]
    for i in range(1, 5):
        inner = inner + net[:, i : i + 1] * pos_ref[i : i + 1, here]
    activity = jnp.sin(net[:, 8:9] * (inner + net[:, 5:6]))
    for layer in range(2):
        inner = (
            jnp.dot(hid_ref[layer], activity, precision=HIGHEST, preferred_element_type=F32)
            + net[:, 6 + layer : 7 + layer]
        )
        activity = jnp.sin(net[:, 9 + layer : 10 + layer] * inner)
    places = me * CHUNK + lax.broadcasted_iota(jnp.int32, (1, CHUNK), 1)
    scaled = places.astype(F32) / (LENGTH - 1)

    def wait(ref, sem):
        pltpu.make_async_copy(ref, ref, sem).wait()

    wait(pbuf, rp)
    for lo in range(0, D, 64):
        pm = pbuf[lo : lo + 64, :]
        values = jnp.dot(pm[:, 0:ORDER], activity, precision=HIGHEST, preferred_element_type=F32)
        values = values * jnp.exp(-(scaled * pm[:, DECAY : DECAY + 1]))
        for r in range(RADIX):
            stage[pl.ds(8 * lo + RADIX + r, 64, stride=8), :] = values[
                :, r * LANES : (r + 1) * LANES
            ]

    wait(xc.at[:, pl.ds(HALO, CHUNK)], rx)
    wait(wbuf, rw)

    @pl.when(me > 0)
    def _():
        wait(xc.at[:, pl.ds(0, HALO)], rh)

    for j in range(3):
        proj[j] = mm(wbuf[j], xc[...])
    column = lax.broadcasted_iota(jnp.int32, (1, HALO + CHUNK), 1)
    inside = jnp.logical_or(column >= HALO, me > 0)

    def shorts(step, carry):
        lo = pl.multiple_of(step * 32, 32)
        pm = pbuf[pl.ds(lo, 32), :]
        streams = []
        for j in range(3):
            p = jnp.where(inside, proj[j, pl.ds(lo, 32), :] + pm[:, BIAS + j : BIAS + j + 1], 0.0)
            taps = [pm[:, TAPS + 3 * j + i : TAPS + 3 * j + i + 1] for i in range(3)]
            streams.append(
                taps[0] * pltpu.roll(p, 2, 1)[:, HALO:]
                + taps[1] * pltpu.roll(p, 1, 1)[:, HALO:]
                + taps[2] * p[:, HALO:]
            )
        gated = streams[2] * streams[1]
        keep0[pl.ds(lo, 32), :] = streams[0]
        keepg[pl.ds(lo, 32), :] = gated
        for r in range(RADIX):
            stage[pl.ds(8 * lo + r, 32, stride=8), :] = gated[:, r * LANES : (r + 1) * LANES]
        return carry

    lax.fori_loop(0, D // 32, shorts, 0)
    snd[...] = stage[...].reshape(D, 8, LANES).astype(BF16)

    def scatter(src, dst, send, recv):
        def one(i, carry):
            to = lax.rem(me + i, DEV)
            put(src.at[to], dst.at[me], send, recv, (to // CH, lax.rem(to, CH)))
            return carry

        lax.fori_loop(1, DEV, one, 0)
        pltpu.make_async_copy(src.at[me], dst.at[me], recv).start()

    scatter(snd, rcv, s3, r3)
    for copy in consts:
        copy.wait()
    wait(rcv, r3)

    stage[...] = rcv[...].astype(F32).reshape(D * 8, LANES)
    for r in range(RADIX):
        x = jnp.concatenate(
            [stage[pl.ds(r, D, stride=8), :], stage[pl.ds(RADIX + r, D, stride=8), :]], axis=1
        ).astype(BF16)
        for part in range(2):
            sect[r, part] = mm(first_v[part * D : (part + 1) * D, :], x) + mm(
                first_v[(2 + part) * D : (3 + part) * D, :], x
            )

    def ahead(step, carry):
        lo = pl.multiple_of(step * 16, 16)
        rows = pl.ds(lo, 16)
        spins = spin_v[rows, :]
        re, im = [], []
        for r in range(RADIX):
            a, b = sect[r, 0, rows, :], sect[r, 1, rows, :]
            if r:
                cs, sn = spins[:, r : r + 1], spins[:, RADIX + r : RADIX + r + 1]
                a, b = a * cs + b * sn, b * cs - a * sn
            re.append(a)
            im.append(b)
        e0r, e0i, e1r, e1i = re[0] + re[2], im[0] + im[2], re[0] - re[2], im[0] - im[2]
        o0r, o0i, o1r, o1i = re[1] + re[3], im[1] + im[3], re[1] - re[3], im[1] - im[3]
        outs = [
            (e0r + o0r, e0i + o0i),
            (e1r + o1i, e1i - o1r),
            (e0r - o0r, e0i - o0i),
            (e1r - o1i, e1i + o1r),
        ]
        for h, (a, b) in enumerate(outs):
            cs = twid_v[0, rows, h * LANES : (h + 1) * LANES]
            sn = twid_v[1, rows, h * LANES : (h + 1) * LANES]
            for g in range(2):
                ga = a[:, g * LANES : (g + 1) * LANES]
                gb = b[:, g * LANES : (g + 1) * LANES]
                pair = jnp.concatenate([ga * cs + gb * sn, gb * cs - ga * sn], axis=1)
                high, low = split(pair)
                chi[g, h, rows, :] = high
                clo[g, h, rows, :] = low
        return carry

    lax.fori_loop(0, D // 16, ahead, 0)

    for h in range(RADIX):
        spectra = []
        for g in range(2):
            high, low = chi[g, h], clo[g, h]
            spectra.append(mm(high, fwd_v[0]) + mm(low, fwd_v[0]) + mm(high, fwd_v[1]))
        (gr, gi), (kr, ki) = [(z[:, :LANES], z[:, LANES:]) for z in spectra]
        product = jnp.concatenate([gr * kr - gi * ki, gr * ki + gi * kr], axis=1)
        high, low = split(product)
        z = mm(high, inv_v[0]) + mm(low, inv_v[0]) + mm(high, inv_v[1])
        zr, zi = z[:, :LANES], z[:, LANES:]
        cs = twid_v[0, :, h * LANES : (h + 1) * LANES]
        sn = twid_v[1, :, h * LANES : (h + 1) * LANES]
        back[h, 0] = zr * cs - zi * sn
        back[h, 1] = zi * cs + zr * sn

    def behind(step, carry):
        lo = pl.multiple_of(step * 16, 16)
        rows = pl.ds(lo, 16)
        rows_im = pl.ds(pl.multiple_of(D + lo, 16), 16)
        spins = spin_v[rows, :]
        re = [back[h, 0, rows, :] for h in range(RADIX)]
        im = [back[h, 1, rows, :] for h in range(RADIX)]
        e0r, e0i, e1r, e1i = re[0] + re[2], im[0] + im[2], re[0] - re[2], im[0] - im[2]
        o0r, o0i, o1r, o1i = re[1] + re[3], im[1] + im[3], re[1] - re[3], im[1] - im[3]
        outs = [
            (e0r + o0r, e0i + o0i),
            (e1r - o1i, e1i + o1r),
            (e0r - o0r, e0i - o0i),
            (e1r + o1i, e1i - o1r),
        ]
        for r, (a, b) in enumerate(outs):
            if r:
                cs, sn = spins[:, r : r + 1], spins[:, RADIX + r : RADIX + r + 1]
                a, b = a * cs - b * sn, b * cs + a * sn
            lanes = slice(r * LANES, (r + 1) * LANES)
            high, low = split(a)
            dhi[rows, lanes] = high
            dlo[rows, lanes] = low
            high, low = split(b)
            dhi[rows_im, lanes] = high
            dlo[rows_im, lanes] = low
        return carry

    lax.fori_loop(0, D // 16, behind, 0)
    last_hi, last_lo = last_v[0:D, :], last_v[D : 2 * D, :]
    settled = mm(last_hi, dhi[...]) + mm(last_lo, dhi[...]) + mm(last_hi, dlo[...])
    for r in range(RADIX):
        ystage[:, r, :] = settled[:, r * LANES : (r + 1) * LANES]
    ysnd[...] = ystage[...].astype(BF16)

    scatter(ysnd, yrcv, s5, r5)
    wait(yrcv, r5)

    ystage[...] = yrcv[...].astype(F32)
    convolved = jnp.concatenate([ystage[:, r, :] for r in range(RADIX)], axis=1)
    convolved = convolved + pbuf[:, DIRECT : DIRECT + 1] * keepg[...]
    mixed = (keep0[...] * convolved).astype(BF16)
    osnd[...] = (mm(wout_ref[...], mixed) + pbuf[:, OUTB : OUTB + 1]).astype(BF16)
    o_dst = out_ref.at[:, pl.ds(pl.multiple_of(c * CHUNK, CHUNK), CHUNK)]
    for i in range(1, CH):
        j = lax.rem(c + i, CH)
        put(osnd.at[pl.ds(pl.multiple_of(j * OWN, OWN), OWN), :], o_dst, s6, r6, (s, j))
    pltpu.make_async_copy(osnd.at[rows_own, :], o_dst, r6).start()

    wait(out_ref, r6)
    rest = pl.ds(0, D - OWN)
    wait(xc.at[rest, pl.ds(HALO, CHUNK)], s1.at[0])
    wait(wbuf.at[:, rest, :], s1.at[2])
    wait(pbuf.at[rest, :], s1.at[3])
    six = pl.ds(0, 6 * OWN)
    wait(xc.at[six, pl.ds(0, HALO)], s1.at[1])

    @pl.when(c == 0)
    def _():
        wait(xc.at[pl.ds(0, OWN), pl.ds(0, HALO)], s1.at[1])

    @pl.when(s < SEQ - 1)
    def _():
        wait(xc.at[pl.ds(0, OWN), pl.ds(0, HALO)], s1.at[1])

    wait(snd.at[pl.ds(0, DEV - 1)], s3)
    wait(ysnd.at[pl.ds(0, DEV - 1)], s5)
    wait(osnd.at[rest, :], s6)


def body(
    inputs,
    w_in,
    b_in,
    short_kernel,
    positional,
    filter_in,
    filter_bias,
    filter_freq,
    filter_hidden,
    filter_out,
    decay,
    conv_bias,
    w_out,
    b_out,
):
    prm = jnp.concatenate(
        [
            filter_out,
            b_in.T,
            short_kernel.transpose(1, 0, 2).reshape(OWN, 9),
            decay[:, None],
            conv_bias[:, None],
            b_out[:, None],
            jnp.zeros((OWN, LANES - 79), F32),
        ],
        axis=1,
    )
    net = jnp.concatenate(
        [filter_in, filter_bias.T, filter_freq.T, jnp.zeros((ORDER, LANES - 11), F32)], axis=1
    )
    hbm = pl.BlockSpec(memory_space=pl.ANY)
    vmem = pl.BlockSpec(memory_space=pltpu.VMEM)
    dma = pltpu.SemaphoreType.DMA
    return pl.pallas_call(
        kernel,
        out_shape=jax.ShapeDtypeStruct((OWN, SPAN), BF16),
        in_specs=[hbm, hbm, hbm, vmem, vmem, vmem, vmem] + [hbm] * 6,
        out_specs=vmem,
        scratch_shapes=[
            pltpu.VMEM((D, HALO + CHUNK), BF16),
            pltpu.VMEM((3, D, D), BF16),
            pltpu.VMEM((D, LANES), F32),
            pltpu.VMEM((3, D, HALO + CHUNK), F32),
            pltpu.VMEM((D * 8, LANES), F32),
            pltpu.VMEM((D, CHUNK), F32),
            pltpu.VMEM((D, CHUNK), F32),
            pltpu.VMEM((DEV, 8, LANES), BF16),
            pltpu.VMEM((DEV, 8, LANES), BF16),
            pltpu.VMEM((4 * D, D), BF16),
            pltpu.VMEM((2 * D, 2 * D), BF16),
            pltpu.VMEM((2, D, D), BF16),
            pltpu.VMEM((2, D, D), BF16),
            pltpu.VMEM((2, D, CHUNK), F32),
            pltpu.VMEM((D, LANES), F32),
            pltpu.VMEM((RADIX, 2, D, 2 * LANES), F32),
            pltpu.VMEM((2, RADIX, D, 2 * LANES), BF16),
            pltpu.VMEM((2, RADIX, D, 2 * LANES), BF16),
            pltpu.VMEM((RADIX, 2, D, LANES), F32),
            pltpu.VMEM((2 * D, CHUNK), BF16),
            pltpu.VMEM((2 * D, CHUNK), BF16),
            pltpu.VMEM((DEV, RADIX, LANES), F32),
            pltpu.VMEM((DEV, RADIX, LANES), BF16),
            pltpu.VMEM((DEV, RADIX, LANES), BF16),
            pltpu.VMEM((D, CHUNK), BF16),
            dma((6,)),
            dma((4,)),
            dma,
            dma,
            dma,
            dma,
            dma,
            dma,
            dma,
            dma,
            dma,
            dma,
        ],
        compiler_params=pltpu.CompilerParams(has_side_effects=True),
    )(inputs, w_in, prm, positional, net, filter_hidden, w_out, *tables())


def solution(mesh):
    in_specs = (
        P("ch", "seq"),
        P(None, "ch", None),
        P(None, "ch"),
        P(None, "ch", None),
        P(None, "seq"),
        P(),
        P(),
        P(),
        P(),
        P("ch", None),
        P("ch"),
        P("ch"),
        P(),
        P("ch"),
    )
    return jax.shard_map(
        body, mesh=mesh, in_specs=in_specs, out_specs=P("ch", "seq"), check_vma=False
    )
```

```python
import math

import jax
import jax.numpy as jnp
import numpy as np
from jax import lax
from jax.experimental import pallas as pl
from jax.experimental.pallas import tpu as pltpu
from jax.sharding import PartitionSpec as P

MESH = pl.DeviceIdType.MESH
F32 = jnp.float32
BF16 = jnp.bfloat16
HIGHEST = lax.Precision.HIGHEST

SEQ, CH = 32, 8
DEV = SEQ * CH
D = 256
OWN = D // CH
SPAN = 4096
CHUNK = SPAN // CH
LENGTH = SPAN * SEQ
HALO = 128
LANES = 128
RADIX = CHUNK // LANES
ORDER = 64
BLOCK = 16
BIAS, TAPS, DECAY, DIRECT, OUTB = 64, 67, 76, 77, 78


def halves(table):
    high = np.asarray(table, np.float64).astype(jnp.bfloat16)
    low = (np.asarray(table, np.float64) - high.astype(np.float64)).astype(jnp.bfloat16)
    return high, low


def tables():
    rows = np.arange(D)
    f1 = np.arange(D) + 0.25
    angle = 2.0 * np.pi * ((np.outer(4 * f1, rows) % (4 * D)) / (4 * D))
    first = np.concatenate([np.cos(angle), -np.sin(angle)], axis=0)
    first_stack = np.concatenate(halves(first), axis=0)
    last_stack = np.concatenate(halves(first.T / LENGTH), axis=0)
    lanes = np.arange(LANES)
    inner = 2.0 * np.pi * (np.outer(lanes, lanes) % LANES) / LANES
    c, s = np.cos(inner), np.sin(inner)
    forward = np.stack(halves(np.block([[c, -s], [s, c]])))
    inverse = np.stack(halves(np.block([[c, s], [-s, c]])))
    shift = f1[:, None] + D * np.arange(RADIX)[None, :]
    turn = 2.0 * np.pi / LENGTH * shift[:, :, None] * lanes[None, None, :]
    turn = turn.reshape(D, CHUNK)
    twiddle = np.stack([np.cos(turn), np.sin(turn)]).astype(np.float32)
    spin = 2.0 * np.pi / (RADIX * D) * f1[:, None] * np.arange(RADIX)[None, :]
    spins = np.zeros((D, LANES), np.float32)
    spins[:, 0:RADIX] = np.cos(spin)
    spins[:, RADIX : 2 * RADIX] = np.sin(spin)
    return first_stack, last_stack, forward, inverse, twiddle, spins


def split(x):
    high = x.astype(BF16)
    return high, (x - high.astype(F32)).astype(BF16)


def mm(a, b):
    return jnp.dot(a, b, preferred_element_type=F32)


def kernel(
    x_ref,
    w_ref,
    bin_ref,
    taps_ref,
    fout_ref,
    decay_ref,
    direct_ref,
    bout_ref,
    pos_ref,
    fin_ref,
    fbias_ref,
    ffreq_ref,
    fhid_ref,
    wout_ref,
    first_ref,
    last_ref,
    fwd_ref,
    inv_ref,
    twid_ref,
    spin_ref,
    out_ref,
    bin_v,
    taps_v,
    fout_v,
    decay_v,
    direct_v,
    bout_v,
    pos_v,
    fin_v,
    fbias_v,
    ffreq_v,
    fhid_v,
    wout_v,
    raw,
    rawnet,
    prm,
    xc,
    wbuf,
    pbuf,
    pflat,
    proj,
    stage,
    keep0,
    keepg,
    ksnd,
    krcv,
    gsnd,
    grcv,
    first_v,
    last_v,
    fwd_v,
    inv_v,
    twid_v,
    spin_v,
    sect,
    chi,
    clo,
    spec,
    back,
    dhi,
    dlo,
    ysnd,
    yrcv,
    osnd,
    small_sem,
    const_sem,
    gate,
    s1,
    r1,
    s3,
    r3,
    s6,
    r6,
):
    s = lax.axis_index("seq")
    c = lax.axis_index("ch")
    me = s * CH + c
    y = lax.rem(s // 2, 4)
    own = pl.multiple_of(c * OWN, OWN)
    rows_own = pl.ds(own, OWN)

    smalls = [
        pltpu.make_async_copy(src, dst, small_sem.at[i])
        for i, (src, dst) in enumerate(
            [
                (bin_ref, bin_v),
                (taps_ref, taps_v),
                (fout_ref, fout_v),
                (decay_ref, decay_v),
                (direct_ref, direct_v),
                (bout_ref, bout_v),
                (pos_ref, pos_v),
                (fin_ref, fin_v),
                (fbias_ref, fbias_v),
                (ffreq_ref, ffreq_v),
                (fhid_ref, fhid_v),
                (wout_ref, wout_v),
            ]
        )
    ]
    consts = [
        pltpu.make_async_copy(src, dst, const_sem.at[i])
        for i, (src, dst) in enumerate(
            [
                (first_ref, first_v),
                (spin_ref, spin_v),
                (twid_ref, twid_v),
                (fwd_ref, fwd_v),
                (inv_ref, inv_v),
                (last_ref, last_v),
            ]
        )
    ]
    for copy in smalls:
        copy.start()

    bar = pltpu.get_barrier_semaphore()

    def greet(sem, to):
        pl.semaphore_signal(sem, inc=1, device_id=to, device_id_type=MESH)

    for i in range(1, CH):
        greet(bar, (s, lax.rem(c + i, CH)))
    for i in range(1, SEQ):
        greet(bar, (lax.rem(s + i, SEQ), c))

    @pl.when(jnp.logical_and(c == 0, s > 0))
    def _():
        for j in range(CH):
            greet(bar, (s - 1, j))

    for copy in smalls[:6]:
        copy.wait()
    raw[...] = jnp.zeros_like(raw)
    raw[0:3, :] = bin_v[...]
    for j in range(3):
        raw[3 + 3 * j : 6 + 3 * j, :] = taps_v[j]
    raw[12:13, :] = decay_v[...]
    raw[13:14, :] = direct_v[...]
    raw[14:15, :] = bout_v[...]

    def columns(rows, n):
        eye = (
            lax.broadcasted_iota(jnp.int32, (n, n), 0) == lax.broadcasted_iota(jnp.int32, (n, n), 1)
        ).astype(F32)
        return lax.dot_general(
            eye, rows, (((1,), (1,)), ((), ())), precision=HIGHEST, preferred_element_type=F32
        )

    prm[...] = jnp.zeros_like(prm)
    prm[:, 0:ORDER] = fout_v[...]
    prm[:, ORDER : ORDER + 16] = columns(raw[...], OWN)
    pl.semaphore_wait(bar, jnp.where(s < SEQ - 1, SEQ + CH - 1, SEQ + CH - 2))

    def put(src, dst, send, recv, to):
        pltpu.make_async_remote_copy(
            src_ref=src, dst_ref=dst, send_sem=send, recv_sem=recv, device_id=to, device_id_type=MESH
        ).start()

    def wait(ref, sem):
        pltpu.make_async_copy(ref, ref, sem).wait()

    half = pl.ds(pl.multiple_of(lax.rem(y, 2) * LANES, LANES), LANES)
    quarter = pl.ds(pl.multiple_of(y * 8, 8), 8)
    w_src = w_ref.at[:, pl.ds(pl.multiple_of((y // 2) * 16, 16), 16), half]
    w_dst = wbuf.at[:, c, y // 2, :, half]
    p_src = prm.at[quarter, :]
    p_dst = pbuf.at[c, y]
    x_dst = xc.at[rows_own, pl.ds(HALO, CHUNK)]
    h_dst = xc.at[rows_own, pl.ds(0, HALO)]

    def chunk(j):
        return x_ref.at[:, pl.ds(pl.multiple_of(j * CHUNK, CHUNK), CHUNK)]

    def tail(j):
        return x_ref.at[:, pl.ds(pl.multiple_of(j * CHUNK + CHUNK - HALO, HALO), HALO)]

    for i in range(1, CH):
        to = (s, lax.rem(c + i, CH))
        put(p_src, p_dst, s1.at[0], r1.at[0], to)
        put(w_src, w_dst, s1.at[1], r1.at[1], to)
    for i in range(1, CH):
        j = lax.rem(c + i, CH)
        put(chunk(j), x_dst, s1.at[2], r1.at[2], (s, j))
    for i in range(1, CH):
        j = lax.rem(c + i, CH)

        @pl.when(j > 0)
        def _():
            put(tail(j - 1), h_dst, s1.at[3], r1.at[3], (s, j))

    @pl.when(s < SEQ - 1)
    def _():
        put(tail(CH - 1), h_dst, s1.at[3], r1.at[3], (s + 1, 0))

    pltpu.make_async_copy(p_src, p_dst, r1.at[0]).start()
    pltpu.make_async_copy(w_src, w_dst, r1.at[1]).start()
    pltpu.make_async_copy(chunk(c), x_dst, r1.at[2]).start()

    @pl.when(c > 0)
    def _():
        pltpu.make_async_copy(tail(c - 1), h_dst, r1.at[3]).start()

    @pl.when(me == 0)
    def _():
        xc[:, 0:HALO] = jnp.zeros((D, HALO), BF16)

    for i in range(1, SEQ):
        greet(gate, (lax.rem(s + i, SEQ), c))
    for copy in consts:
        copy.start()
    for copy in smalls[6:]:
        copy.wait()

    rawnet[...] = jnp.zeros_like(rawnet)
    rawnet[0:5, :] = fin_v[...]
    rawnet[5:8, :] = fbias_v[...]
    rawnet[8:11, :] = ffreq_v[...]
    net = columns(rawnet[...], ORDER)
    here = pl.ds(pl.multiple_of(c * CHUNK, CHUNK), CHUNK)
    inner = net[:, 0:1] * pos_v[0:1, here]
    for i in range(1, 5):
        inner = inner + net[:, i : i + 1] * pos_v[i : i + 1, here]
    activity = jnp.sin(net[:, 8:9] * (inner + net[:, 5:6]))
    for layer in range(2):
        inner = (
            jnp.dot(fhid_v[layer], activity, precision=HIGHEST, preferred_element_type=F32)
            + net[:, 6 + layer : 7 + layer]
        )
        activity = jnp.sin(net[:, 9 + layer : 10 + layer] * inner)
    places = me * CHUNK + lax.broadcasted_iota(jnp.int32, (1, CHUNK), 1)
    scaled = places.astype(F32) / (LENGTH - 1)

    p_mine = pbuf.at[:, y]
    w_mine = wbuf.at[:, :, y // 2, :, half]
    wait(p_mine, r1.at[0])
    around = [(s - 2 * y + 2 * lax.rem(y + i, 4), c) for i in (1, 3, 2)]
    for to in around:
        put(p_mine, p_mine, s1.at[4], r1.at[4], to)
    wait(w_mine, r1.at[1])
    for to in around:
        put(w_mine, w_mine, s1.at[5], r1.at[5], to)

    wait(pbuf.at[pl.ds(0, 6)], r1.at[4])
    pflat[...] = pbuf[...].reshape(D, LANES)

    for lo in range(0, D, 64):
        pm = pflat[lo : lo + 64, :]
        values = jnp.dot(pm[:, 0:ORDER], activity, precision=HIGHEST, preferred_element_type=F32)
        values = values * jnp.exp(-(scaled * pm[:, DECAY : DECAY + 1]))
        for r in range(RADIX):
            stage[lo : lo + 64, r, :] = values[:, r * LANES : (r + 1) * LANES]
    ksnd[...] = stage[...].astype(BF16)

    def scatter(src, dst, at):
        send, recv = s3.at[at], r3.at[at]

        def one(si, cj):
            to = si * CH + cj
            put(src.at[to], dst.at[me], send, recv, (si, cj))

        for i in range(1, CH):
            one(s, lax.rem(c + i, CH))

        def column(i, carry):
            si = lax.rem(s + i, SEQ)
            for j in range(CH):
                one(si, lax.rem(c + j, CH))
            return carry

        lax.fori_loop(1, SEQ, column, 0)
        pltpu.make_async_copy(src.at[me], dst.at[me], recv).start()

    pl.semaphore_wait(gate, SEQ - 1)
    scatter(ksnd, krcv, 0)

    wait(xc.at[:, pl.ds(HALO, CHUNK)], r1.at[2])

    @pl.when(me > 0)
    def _():
        wait(xc.at[:, pl.ds(0, HALO)], r1.at[3])

    wait(wbuf.at[:, pl.ds(0, 6)], r1.at[5])

    for j in range(3):
        proj[j] = mm(wbuf[j].reshape(D, D), xc[...])
    column = lax.broadcasted_iota(jnp.int32, (1, HALO + CHUNK), 1)
    inside = jnp.logical_or(column >= HALO, me > 0)

    def shorts(step, carry):
        lo = pl.multiple_of(step * BLOCK, BLOCK)
        pm = pflat[pl.ds(lo, BLOCK), :]
        streams = []
        for j in range(3):
            p = jnp.where(inside, proj[j, pl.ds(lo, BLOCK), :] + pm[:, BIAS + j : BIAS + j + 1], 0.0)
            taps = [pm[:, TAPS + 3 * j + i : TAPS + 3 * j + i + 1] for i in range(3)]
            streams.append(
                taps[0] * pltpu.roll(p, 2, 1)[:, HALO:]
                + taps[1] * pltpu.roll(p, 1, 1)[:, HALO:]
                + taps[2] * p[:, HALO:]
            )
        gated = streams[2] * streams[1]
        keep0[pl.ds(lo, BLOCK), :] = streams[0]
        keepg[pl.ds(lo, BLOCK), :] = gated
        for r in range(RADIX):
            stage[pl.ds(lo, BLOCK), r, :] = gated[:, r * LANES : (r + 1) * LANES]
        return carry

    lax.fori_loop(0, D // BLOCK, shorts, 0)
    gsnd[...] = stage[...].astype(BF16)

    scatter(gsnd, grcv, 1)

    def sections(rcv):
        stage[...] = rcv[...].astype(F32)
        x = jnp.concatenate([stage[:, r, :] for r in range(RADIX)], axis=1).astype(BF16)
        for part in range(2):
            sect[part] = mm(first_v[part * D : (part + 1) * D, :], x) + mm(
                first_v[(2 + part) * D : (3 + part) * D, :], x
            )

        def ahead(step, carry):
            rows = pl.ds(pl.multiple_of(step * 32, 32), 32)
            spins = spin_v[rows, :]
            re, im = [], []
            for r in range(RADIX):
                lanes = slice(r * LANES, (r + 1) * LANES)
                a, b = sect[0, rows, lanes], sect[1, rows, lanes]
                if r:
                    cs, sn = spins[:, r : r + 1], spins[:, RADIX + r : RADIX + r + 1]
                    a, b = a * cs + b * sn, b * cs - a * sn
                re.append(a)
                im.append(b)
            e0r, e0i, e1r, e1i = re[0] + re[2], im[0] + im[2], re[0] - re[2], im[0] - im[2]
            o0r, o0i, o1r, o1i = re[1] + re[3], im[1] + im[3], re[1] - re[3], im[1] - im[3]
            outs = [
                (e0r + o0r, e0i + o0i),
                (e1r + o1i, e1i - o1r),
                (e0r - o0r, e0i - o0i),
                (e1r - o1i, e1i + o1r),
            ]
            for h, (a, b) in enumerate(outs):
                cs = twid_v[0, rows, h * LANES : (h + 1) * LANES]
                sn = twid_v[1, rows, h * LANES : (h + 1) * LANES]
                high, low = split(jnp.concatenate([a * cs + b * sn, b * cs - a * sn], axis=1))
                chi[h, rows, :] = high
                clo[h, rows, :] = low
            return carry

        lax.fori_loop(0, D // 32, ahead, 0)

    def spectrum(h):
        high, low = chi[h], clo[h]
        return mm(high, fwd_v[0]) + mm(low, fwd_v[0]) + mm(high, fwd_v[1])

    for copy in consts:
        copy.wait()
    wait(krcv, r3.at[0])
    sections(krcv)
    for h in range(RADIX):
        spec[h] = spectrum(h)
    wait(grcv, r3.at[1])
    sections(grcv)
    for h in range(RADIX):
        g, k = spectrum(h), spec[h]
        gr, gi, kr, ki = g[:, :LANES], g[:, LANES:], k[:, :LANES], k[:, LANES:]
        high, low = split(jnp.concatenate([gr * kr - gi * ki, gr * ki + gi * kr], axis=1))
        z = mm(high, inv_v[0]) + mm(low, inv_v[0]) + mm(high, inv_v[1])
        zr, zi = z[:, :LANES], z[:, LANES:]
        cs = twid_v[0, :, h * LANES : (h + 1) * LANES]
        sn = twid_v[1, :, h * LANES : (h + 1) * LANES]
        back[h, 0] = zr * cs - zi * sn
        back[h, 1] = zi * cs + zr * sn

    def behind(step, carry):
        lo = pl.multiple_of(step * 32, 32)
        rows = pl.ds(lo, 32)
        rows_im = pl.ds(pl.multiple_of(D + lo, 32), 32)
        spins = spin_v[rows, :]
        re = [back[h, 0, rows, :] for h in range(RADIX)]
        im = [back[h, 1, rows, :] for h in range(RADIX)]
        e0r, e0i, e1r, e1i = re[0] + re[2], im[0] + im[2], re[0] - re[2], im[0] - im[2]
        o0r, o0i, o1r, o1i = re[1] + re[3], im[1] + im[3], re[1] - re[3], im[1] - im[3]
        outs = [
            (e0r + o0r, e0i + o0i),
            (e1r - o1i, e1i + o1r),
            (e0r - o0r, e0i - o0i),
            (e1r + o1i, e1i - o1r),
        ]
        for r, (a, b) in enumerate(outs):
            if r:
                cs, sn = spins[:, r : r + 1], spins[:, RADIX + r : RADIX + r + 1]
                a, b = a * cs - b * sn, b * cs + a * sn
            lanes = slice(r * LANES, (r + 1) * LANES)
            high, low = split(a)
            dhi[rows, lanes] = high
            dlo[rows, lanes] = low
            high, low = split(b)
            dhi[rows_im, lanes] = high
            dlo[rows_im, lanes] = low
        return carry

    lax.fori_loop(0, D // 32, behind, 0)
    last_hi, last_lo = last_v[0:D, :], last_v[D : 2 * D, :]
    settled = mm(last_hi, dhi[...]) + mm(last_lo, dhi[...]) + mm(last_hi, dlo[...])
    for r in range(RADIX):
        stage[:, r, :] = settled[:, r * LANES : (r + 1) * LANES]
    ysnd[...] = stage[...].astype(BF16)

    scatter(ysnd, yrcv, 2)
    wait(yrcv, r3.at[2])

    stage[...] = yrcv[...].astype(F32)
    convolved = jnp.concatenate([stage[:, r, :] for r in range(RADIX)], axis=1)
    convolved = convolved + pflat[:, DIRECT : DIRECT + 1] * keepg[...]
    mixed = (keep0[...] * convolved).astype(BF16)
    osnd[...] = (mm(wout_v[...], mixed) + pflat[:, OUTB : OUTB + 1]).astype(BF16)
    o_dst = out_ref.at[:, pl.ds(pl.multiple_of(c * CHUNK, CHUNK), CHUNK)]
    for i in range(1, CH):
        j = lax.rem(c + i, CH)
        put(osnd.at[pl.ds(pl.multiple_of(j * OWN, OWN), OWN), :], o_dst, s6, r6, (s, j))
    pltpu.make_async_copy(osnd.at[rows_own, :], o_dst, r6).start()

    wait(out_ref, r6)
    most = pl.ds(0, CH - 1)
    wait(pbuf.at[most, 0], s1.at[0])
    wait(wbuf.at[:, most, 0, :, pl.ds(0, LANES)], s1.at[1])
    wait(xc.at[pl.ds(0, D - OWN), pl.ds(HALO, CHUNK)], s1.at[2])
    tails = pl.ds(0, OWN)
    wait(xc.at[pl.ds(0, 6 * OWN), pl.ds(0, HALO)], s1.at[3])

    @pl.when(c == 0)
    def _():
        wait(xc.at[tails, pl.ds(0, HALO)], s1.at[3])

    @pl.when(s < SEQ - 1)
    def _():
        wait(xc.at[tails, pl.ds(0, HALO)], s1.at[3])

    wait(pbuf.at[pl.ds(0, 6)], s1.at[4])
    wait(wbuf.at[:, pl.ds(0, 6)], s1.at[5])
    for i, buf in enumerate((ksnd, gsnd, ysnd)):
        wait(buf.at[pl.ds(0, DEV - 1)], s3.at[i])
    wait(osnd.at[pl.ds(0, D - OWN), :], s6)


def body(
    inputs,
    w_in,
    b_in,
    short_kernel,
    positional,
    filter_in,
    filter_bias,
    filter_freq,
    filter_hidden,
    filter_out,
    decay,
    conv_bias,
    w_out,
    b_out,
):
    dma = pltpu.SemaphoreType.DMA
    hbm = pl.BlockSpec(memory_space=pl.ANY)
    vmem = pltpu.VMEM
    return pl.pallas_call(
        kernel,
        out_shape=pltpu.VMEM((OWN, SPAN), BF16),
        in_specs=[hbm] * 20,
        out_specs=pl.BlockSpec(memory_space=pltpu.VMEM),
        scratch_shapes=[
            vmem((3, OWN), F32),
            vmem((3, 3, OWN), F32),
            vmem((OWN, ORDER), F32),
            vmem((1, OWN), F32),
            vmem((1, OWN), F32),
            vmem((1, OWN), F32),
            vmem((5, SPAN), F32),
            vmem((5, ORDER), F32),
            vmem((3, ORDER), F32),
            vmem((3, ORDER), F32),
            vmem((2, ORDER, ORDER), F32),
            vmem((D, D), BF16),
            vmem((16, OWN), F32),
            vmem((16, ORDER), F32),
            vmem((OWN, LANES), F32),
            vmem((D, HALO + CHUNK), BF16),
            vmem((3, CH, 2, 16, D), BF16),
            vmem((CH, 4, 8, LANES), F32),
            vmem((D, LANES), F32),
            vmem((3, D, HALO + CHUNK), F32),
            vmem((DEV, RADIX, LANES), F32),
            vmem((D, CHUNK), F32),
            vmem((D, CHUNK), F32),
            vmem((DEV, RADIX, LANES), BF16),
            vmem((DEV, RADIX, LANES), BF16),
            vmem((DEV, RADIX, LANES), BF16),
            vmem((DEV, RADIX, LANES), BF16),
            vmem((4 * D, D), BF16),
            vmem((2 * D, 2 * D), BF16),
            vmem((2, D, D), BF16),
            vmem((2, D, D), BF16),
            vmem((2, D, CHUNK), F32),
            vmem((D, LANES), F32),
            vmem((2, D, CHUNK), F32),
            vmem((RADIX, D, 2 * LANES), BF16),
            vmem((RADIX, D, 2 * LANES), BF16),
            vmem((RADIX, D, 2 * LANES), F32),
            vmem((RADIX, 2, D, LANES), F32),
            vmem((2 * D, CHUNK), BF16),
            vmem((2 * D, CHUNK), BF16),
            vmem((DEV, RADIX, LANES), BF16),
            vmem((DEV, RADIX, LANES), BF16),
            vmem((D, CHUNK), BF16),
            dma((12,)),
            dma((6,)),
            pltpu.SemaphoreType.REGULAR,
            dma((6,)),
            dma((6,)),
            dma((3,)),
            dma((3,)),
            dma,
            dma,
        ],
        compiler_params=pltpu.CompilerParams(collective_id=0, has_side_effects=True),
    )(
        inputs,
        w_in,
        b_in,
        short_kernel.transpose(0, 2, 1),
        filter_out,
        decay.reshape(1, OWN),
        conv_bias.reshape(1, OWN),
        b_out.reshape(1, OWN),
        positional,
        filter_in.T,
        filter_bias,
        filter_freq,
        filter_hidden,
        w_out,
        *tables(),
    )


def solution(mesh):
    in_specs = (
        P("ch", "seq"),
        P(None, "ch", None),
        P(None, "ch"),
        P(None, "ch", None),
        P(None, "seq"),
        P(),
        P(),
        P(),
        P(),
        P("ch", None),
        P("ch"),
        P("ch"),
        P(),
        P("ch"),
    )
    return jax.shard_map(
        body, mesh=mesh, in_specs=in_specs, out_specs=P("ch", "seq"), check_vma=False
    )
```

```python
import math

import jax
import jax.numpy as jnp
import numpy as np
from jax import lax
from jax.experimental import pallas as pl
from jax.experimental.pallas import tpu as pltpu
from jax.sharding import PartitionSpec as P

MESH = pl.DeviceIdType.MESH
F32 = jnp.float32
BF16 = jnp.bfloat16
HIGHEST = lax.Precision.HIGHEST

SEQ, CH = 32, 8
DEV = SEQ * CH
D = 256
OWN = D // CH
SPAN = 4096
CHUNK = SPAN // CH
LENGTH = SPAN * SEQ
HALO = 128
LANES = 128
RADIX = CHUNK // LANES
ORDER = 64
FAR = (4, 3, 5, 2, 6, 1, 7)
FARX = (2, 1, 3, 0)
BIAS, TAPS, DECAY, DIRECT, OUTB = 64, 67, 76, 77, 78


def halves(table):
    high = np.asarray(table, np.float64).astype(jnp.bfloat16)
    low = (np.asarray(table, np.float64) - high.astype(np.float64)).astype(jnp.bfloat16)
    return high, low


def tables():
    rows = np.arange(D)
    f1 = np.arange(D) + 0.25
    angle = 2.0 * np.pi * ((np.outer(4 * f1, rows) % (4 * D)) / (4 * D))
    first = np.concatenate([np.cos(angle), -np.sin(angle)], axis=0)
    first_stack = np.concatenate(halves(first), axis=0)
    last_stack = np.concatenate(halves(first.T / LENGTH), axis=0)
    lanes = np.arange(LANES)
    inner = 2.0 * np.pi * (np.outer(lanes, lanes) % LANES) / LANES
    c, s = np.cos(inner), np.sin(inner)
    forward = np.stack(halves(np.block([[c, -s], [s, c]])))
    inverse = np.stack(halves(np.block([[c, s], [-s, c]])))
    shift = f1[:, None] + D * np.arange(RADIX)[None, :]
    turn = 2.0 * np.pi / LENGTH * shift[:, :, None] * lanes[None, None, :]
    turn = turn.reshape(D, CHUNK)
    twiddle = np.stack([np.cos(turn), np.sin(turn)]).astype(np.float32)
    spin = 2.0 * np.pi / (RADIX * D) * f1[:, None] * np.arange(RADIX)[None, :]
    spins = np.zeros((D, LANES), np.float32)
    spins[:, 0:RADIX] = np.cos(spin)
    spins[:, RADIX : 2 * RADIX] = np.sin(spin)
    return first_stack, last_stack, forward, inverse, twiddle, spins


def split(x):
    high = x.astype(BF16)
    return high, (x - high.astype(F32)).astype(BF16)


def mm(a, b):
    return jnp.dot(a, b, preferred_element_type=F32)


def kernel(
    x_ref,
    w_ref,
    bin_ref,
    taps_ref,
    fout_ref,
    decay_ref,
    direct_ref,
    bout_ref,
    pos_ref,
    fin_ref,
    fbias_ref,
    ffreq_ref,
    fhid_ref,
    wout_ref,
    first_ref,
    last_ref,
    fwd_ref,
    inv_ref,
    twid_ref,
    spin_ref,
    out_ref,
    bin_v,
    taps_v,
    fout_v,
    decay_v,
    direct_v,
    bout_v,
    pos_v,
    fin_v,
    fbias_v,
    ffreq_v,
    fhid_v,
    wout_v,
    raw,
    rawnet,
    prm,
    xc,
    wbuf,
    pbuf,
    pflat,
    xs,
    cols,
    spins,
    stage,
    keep0,
    keepg,
    ksnd,
    krcv,
    gsnd,
    grcv,
    first_v,
    last_v,
    fwd_v,
    inv_v,
    twid_v,
    spin_v,
    sect,
    chi,
    clo,
    spec,
    back,
    dhi,
    dlo,
    ysnd,
    yrcv,
    osnd,
    small_sem,
    const_sem,
    gate,
    s1,
    r1,
    s3,
    r3,
    s6,
    r6,
):
    s = lax.axis_index("seq")
    c = lax.axis_index("ch")
    me = s * CH + c
    px, py, pk = s // 8, lax.rem(s // 2, 4), lax.rem(s, 2)
    own = pl.multiple_of(c * OWN, OWN)
    rows_own = pl.ds(own, OWN)

    smalls = [
        pltpu.make_async_copy(src, dst, small_sem.at[i])
        for i, (src, dst) in enumerate(
            [
                (bin_ref, bin_v),
                (taps_ref, taps_v),
                (fout_ref, fout_v),
                (decay_ref, decay_v),
                (direct_ref, direct_v),
                (bout_ref, bout_v),
                (pos_ref, pos_v),
                (fin_ref, fin_v),
                (fbias_ref, fbias_v),
                (ffreq_ref, ffreq_v),
                (fhid_ref, fhid_v),
                (wout_ref, wout_v),
            ]
        )
    ]
    consts = [
        pltpu.make_async_copy(src, dst, const_sem.at[i])
        for i, (src, dst) in enumerate(
            [
                (spin_ref, spin_v),
                (first_ref, first_v),
                (twid_ref, twid_v),
                (fwd_ref, fwd_v),
                (inv_ref, inv_v),
                (last_ref, last_v),
            ]
        )
    ]
    for copy in smalls:
        copy.start()

    bar = pltpu.get_barrier_semaphore()

    def greet(sem, to):
        pl.semaphore_signal(sem, inc=1, device_id=to, device_id_type=MESH)

    for i in range(1, CH):
        greet(bar, (s, lax.rem(c + i, CH)))
    for i in range(1, SEQ):
        greet(bar, (lax.rem(s + i, SEQ), c))

    @pl.when(jnp.logical_and(c == 0, s > 0))
    def _():
        for j in range(CH):
            greet(bar, (s - 1, j))

    for copy in smalls[:6]:
        copy.wait()
    raw[...] = jnp.zeros_like(raw)
    raw[0:3, :] = bin_v[...]
    for j in range(3):
        raw[3 + 3 * j : 6 + 3 * j, :] = taps_v[j]
    raw[12:13, :] = decay_v[...]
    raw[13:14, :] = direct_v[...]
    raw[14:15, :] = bout_v[...]

    def columns(rows, n):
        eye = (
            lax.broadcasted_iota(jnp.int32, (n, n), 0) == lax.broadcasted_iota(jnp.int32, (n, n), 1)
        ).astype(F32)
        return lax.dot_general(
            eye, rows, (((1,), (1,)), ((), ())), precision=HIGHEST, preferred_element_type=F32
        )

    prm[...] = jnp.zeros_like(prm)
    prm[:, 0:ORDER] = fout_v[...]
    prm[:, ORDER : ORDER + 16] = columns(raw[...], OWN)
    pl.semaphore_wait(bar, jnp.where(s < SEQ - 1, SEQ + CH - 1, SEQ + CH - 2))

    def put(src, dst, send, recv, to):
        pltpu.make_async_remote_copy(
            src_ref=src, dst_ref=dst, send_sem=send, recv_sem=recv, device_id=to, device_id_type=MESH
        ).start()

    def wait(ref, sem):
        pltpu.make_async_copy(ref, ref, sem).wait()

    half = pl.ds(pl.multiple_of(lax.rem(py, 2) * LANES, LANES), LANES)
    quarter = pl.ds(pl.multiple_of(py * 8, 8), 8)
    w_src = w_ref.at[:, pl.ds(pl.multiple_of((py // 2) * 16, 16), 16), half]
    w_dst = wbuf.at[:, c, py // 2, :, half]
    p_src = prm.at[quarter, :]
    p_dst = pbuf.at[c, py]
    x_dst = xc.at[rows_own, pl.ds(HALO, CHUNK)]
    h_dst = xc.at[rows_own, pl.ds(0, HALO)]

    def chunk(j):
        return x_ref.at[:, pl.ds(pl.multiple_of(j * CHUNK, CHUNK), CHUNK)]

    def tail(j):
        return x_ref.at[:, pl.ds(pl.multiple_of(j * CHUNK + CHUNK - HALO, HALO), HALO)]

    for i in FAR:
        put(p_src, p_dst, s1.at[0], r1.at[0], (s, lax.rem(c + i, CH)))
    for i in FAR:
        put(w_src, w_dst, s1.at[1], r1.at[1], (s, lax.rem(c + i, CH)))
    for i in FAR:
        j = lax.rem(c + i, CH)
        put(chunk(j), x_dst, s1.at[2], r1.at[2], (s, j))

        @pl.when(j > 0)
        def _():
            put(tail(j - 1), h_dst, s1.at[3], r1.at[3], (s, j))

    @pl.when(s < SEQ - 1)
    def _():
        put(tail(CH - 1), h_dst, s1.at[3], r1.at[3], (s + 1, 0))

    pltpu.make_async_copy(p_src, p_dst, r1.at[0]).start()
    pltpu.make_async_copy(w_src, w_dst, r1.at[1]).start()
    pltpu.make_async_copy(chunk(c), x_dst, r1.at[2]).start()

    @pl.when(c > 0)
    def _():
        pltpu.make_async_copy(tail(c - 1), h_dst, r1.at[3]).start()

    @pl.when(me == 0)
    def _():
        xc[:, 0:HALO] = jnp.zeros((D, HALO), BF16)

    for i in range(1, SEQ):
        greet(gate, (lax.rem(s + i, SEQ), c))
    for copy in consts:
        copy.start()
    for copy in smalls[6:]:
        copy.wait()

    rawnet[...] = jnp.zeros_like(rawnet)
    rawnet[0:5, :] = fin_v[...]
    rawnet[5:8, :] = fbias_v[...]
    rawnet[8:11, :] = ffreq_v[...]
    net = columns(rawnet[...], ORDER)
    here = pl.ds(pl.multiple_of(c * CHUNK, CHUNK), CHUNK)
    inner = net[:, 0:1] * pos_v[0:1, here]
    for i in range(1, 5):
        inner = inner + net[:, i : i + 1] * pos_v[i : i + 1, here]
    activity = jnp.sin(net[:, 8:9] * (inner + net[:, 5:6]))
    for layer in range(2):
        inner = (
            jnp.dot(fhid_v[layer], activity, precision=HIGHEST, preferred_element_type=F32)
            + net[:, 6 + layer : 7 + layer]
        )
        activity = jnp.sin(net[:, 9 + layer : 10 + layer] * inner)
    places = me * CHUNK + lax.broadcasted_iota(jnp.int32, (1, CHUNK), 1)
    scaled = places.astype(F32) / (LENGTH - 1)

    p_mine = pbuf.at[:, py]
    w_mine = wbuf.at[:, :, py // 2, :, half]
    consts[0].wait()
    for i in range(6):
        at = 1 + i if i < 3 else 2 + i
        spins[i] = jnp.broadcast_to(spin_v[:, at : at + 1], (D, LANES))
    wait(p_mine, r1.at[0])
    around = [(s - 2 * py + 2 * lax.rem(py + i, 4), c) for i in (2, 1, 3)]
    for to in around:
        put(p_mine, p_mine, s1.at[4], r1.at[4], to)
    wait(w_mine, r1.at[1])
    for to in around:
        put(w_mine, w_mine, s1.at[5], r1.at[5], to)

    wait(pbuf.at[pl.ds(0, 6)], r1.at[4])
    pflat[...] = pbuf[...].reshape(D, LANES)

    for lo in range(0, D, 64):
        pm = pflat[lo : lo + 64, :]
        values = jnp.dot(pm[:, 0:ORDER], activity, precision=HIGHEST, preferred_element_type=F32)
        values = values * jnp.exp(-(scaled * pm[:, DECAY : DECAY + 1]))
        for r in range(RADIX):
            stage[lo : lo + 64, r, :] = values[:, r * LANES : (r + 1) * LANES]
    ksnd[...] = stage[...].astype(BF16)

    def scatter(src, dst, at, dx):
        send, recv = s3.at[at], r3.at[at]
        sx = lax.rem(px + dx, 4) * 8

        def ring(cj, near):
            for dy in (2, 1, 3, 0):
                for dk in (1, 0):
                    if not (near and dy == 0 and dk == 0):
                        si = sx + lax.rem(py + dy, 4) * 2 + lax.rem(pk + dk, 2)
                        put(src.at[si * CH + cj], dst.at[me], send, recv, (si, cj))

        def layer(t, carry):
            ring(lax.rem(c + 4 + (t + 1) // 2 * (1 - 2 * lax.rem(t, 2)), CH), False)
            return carry

        if dx:
            lax.fori_loop(0, CH, layer, 0)
        else:
            lax.fori_loop(0, CH - 1, layer, 0)
            ring(c, True)
            pltpu.make_async_copy(src.at[me], dst.at[me], recv).start()

    def scatter_all(src, dst, at):
        for dx in FARX:
            scatter(src, dst, at, dx)

    pl.semaphore_wait(gate, SEQ - 1)
    scatter_all(ksnd, krcv, 0)

    for j in range(3):
        bias = jnp.broadcast_to(pflat[:, BIAS + j : BIAS + j + 1], (D, LANES))
        for i in range(3):
            at = TAPS + 3 * j + i
            tap = jnp.broadcast_to(pflat[:, at : at + 1], (D, LANES))
            cols[3 * j + i, 0] = tap
            cols[3 * j + i, 1] = tap * bias

    wait(xc.at[:, pl.ds(HALO, CHUNK)], r1.at[2])

    @pl.when(me > 0)
    def _():
        wait(xc.at[:, pl.ds(0, HALO)], r1.at[3])

    wait(wbuf.at[:, pl.ds(0, 6)], r1.at[5])

    wide = xc[...].astype(F32)
    for i in (0, 1):
        xs[i] = pltpu.roll(wide, 2 - i, 1)[:, HALO:].astype(BF16)
    place = lax.broadcasted_iota(jnp.int32, (1, LANES), 1)
    started = [jnp.logical_or(place >= 2 - i, me > 0).astype(F32) for i in (0, 1)]

    for dx in FARX:
        block = lax.rem(px + dx, 4)
        lo = pl.multiple_of(block * 64, 64)
        rows = pl.ds(lo, 64)
        w = wbuf[:, pl.ds(block * 2, 2)].reshape(3 * 64, D)
        taken = [mm(w, xs[0]), mm(w, xs[1]), mm(w, xc[:, HALO:])]
        for r in range(RADIX):
            lanes = slice(r * LANES, (r + 1) * LANES)
            streams = []
            for j in range(3):
                total = None
                for i in range(3):
                    shifted_bias = cols[3 * j + i, 1, rows, :]
                    if r == 0 and i < 2:
                        shifted_bias = shifted_bias * started[i]
                    term = cols[3 * j + i, 0, rows, :] * taken[i][64 * j : 64 * j + 64, lanes]
                    term = term + shifted_bias
                    total = term if total is None else total + term
                streams.append(total)
            gated = streams[2] * streams[1]
            keep0[rows, lanes] = streams[0]
            keepg[rows, lanes] = gated
            stage[rows, r, :] = gated
        gsnd[rows] = stage[rows].astype(BF16)
        scatter(gsnd, grcv, 1, dx)

    def sections(rcv):
        stage[...] = rcv[...].astype(F32)
        x = jnp.concatenate([stage[:, r, :] for r in range(RADIX)], axis=1).astype(BF16)
        for part in range(2):
            sect[part] = mm(first_v[part * D : (part + 1) * D, :], x) + mm(
                first_v[(2 + part) * D : (3 + part) * D, :], x
            )

        def ahead(step, carry):
            rows = pl.ds(pl.multiple_of(step * 32, 32), 32)
            re, im = [], []
            for r in range(RADIX):
                lanes = slice(r * LANES, (r + 1) * LANES)
                a, b = sect[0, rows, lanes], sect[1, rows, lanes]
                if r:
                    cs, sn = spins[r - 1, rows, :], spins[r + 2, rows, :]
                    a, b = a * cs + b * sn, b * cs - a * sn
                re.append(a)
                im.append(b)
            e0r, e0i, e1r, e1i = re[0] + re[2], im[0] + im[2], re[0] - re[2], im[0] - im[2]
            o0r, o0i, o1r, o1i = re[1] + re[3], im[1] + im[3], re[1] - re[3], im[1] - im[3]
            outs = [
                (e0r + o0r, e0i + o0i),
                (e1r + o1i, e1i - o1r),
                (e0r - o0r, e0i - o0i),
                (e1r - o1i, e1i + o1r),
            ]
            for h, (a, b) in enumerate(outs):
                cs = twid_v[0, rows, h * LANES : (h + 1) * LANES]
                sn = twid_v[1, rows, h * LANES : (h + 1) * LANES]
                high, low = split(jnp.concatenate([a * cs + b * sn, b * cs - a * sn], axis=1))
                chi[h, rows, :] = high
                clo[h, rows, :] = low
            return carry

        lax.fori_loop(0, D // 32, ahead, 0)

    def spectrum(h):
        high, low = chi[h], clo[h]
        return mm(high, fwd_v[0]) + mm(low, fwd_v[0]) + mm(high, fwd_v[1])

    for copy in consts[1:]:
        copy.wait()
    wait(krcv, r3.at[0])
    sections(krcv)
    for h in range(RADIX):
        spec[h] = spectrum(h)
    wait(grcv, r3.at[1])
    sections(grcv)
    for h in range(RADIX):
        g, k = spectrum(h), spec[h]
        gr, gi, kr, ki = g[:, :LANES], g[:, LANES:], k[:, :LANES], k[:, LANES:]
        high, low = split(jnp.concatenate([gr * kr - gi * ki, gr * ki + gi * kr], axis=1))
        z = mm(high, inv_v[0]) + mm(low, inv_v[0]) + mm(high, inv_v[1])
        zr, zi = z[:, :LANES], z[:, LANES:]
        cs = twid_v[0, :, h * LANES : (h + 1) * LANES]
        sn = twid_v[1, :, h * LANES : (h + 1) * LANES]
        back[h, 0] = zr * cs - zi * sn
        back[h, 1] = zi * cs + zr * sn

    def behind(step, carry):
        lo = pl.multiple_of(step * 32, 32)
        rows = pl.ds(lo, 32)
        rows_im = pl.ds(pl.multiple_of(D + lo, 32), 32)
        re = [back[h, 0, rows, :] for h in range(RADIX)]
        im = [back[h, 1, rows, :] for h in range(RADIX)]
        e0r, e0i, e1r, e1i = re[0] + re[2], im[0] + im[2], re[0] - re[2], im[0] - im[2]
        o0r, o0i, o1r, o1i = re[1] + re[3], im[1] + im[3], re[1] - re[3], im[1] - im[3]
        outs = [
            (e0r + o0r, e0i + o0i),
            (e1r - o1i, e1i + o1r),
            (e0r - o0r, e0i - o0i),
            (e1r + o1i, e1i - o1r),
        ]
        for r, (a, b) in enumerate(outs):
            if r:
                cs, sn = spins[r - 1, rows, :], spins[r + 2, rows, :]
                a, b = a * cs - b * sn, b * cs + a * sn
            lanes = slice(r * LANES, (r + 1) * LANES)
            high, low = split(a)
            dhi[rows, lanes] = high
            dlo[rows, lanes] = low
            high, low = split(b)
            dhi[rows_im, lanes] = high
            dlo[rows_im, lanes] = low
        return carry

    lax.fori_loop(0, D // 32, behind, 0)
    last_hi, last_lo = last_v[0:D, :], last_v[D : 2 * D, :]
    settled = mm(last_hi, dhi[...]) + mm(last_lo, dhi[...]) + mm(last_hi, dlo[...])
    for r in range(RADIX):
        stage[:, r, :] = settled[:, r * LANES : (r + 1) * LANES]
    ysnd[...] = stage[...].astype(BF16)

    scatter_all(ysnd, yrcv, 2)
    wait(yrcv, r3.at[2])

    stage[...] = yrcv[...].astype(F32)
    convolved = jnp.concatenate([stage[:, r, :] for r in range(RADIX)], axis=1)
    convolved = convolved + pflat[:, DIRECT : DIRECT + 1] * keepg[...]
    mixed = (keep0[...] * convolved).astype(BF16)
    osnd[...] = (mm(wout_v[...], mixed) + pflat[:, OUTB : OUTB + 1]).astype(BF16)
    o_dst = out_ref.at[:, pl.ds(pl.multiple_of(c * CHUNK, CHUNK), CHUNK)]
    for i in FAR:
        j = lax.rem(c + i, CH)
        put(osnd.at[pl.ds(pl.multiple_of(j * OWN, OWN), OWN), :], o_dst, s6, r6, (s, j))
    pltpu.make_async_copy(osnd.at[rows_own, :], o_dst, r6).start()

    wait(out_ref, r6)
    most = pl.ds(0, CH - 1)
    wait(pbuf.at[most, 0], s1.at[0])
    wait(wbuf.at[:, most, 0, :, pl.ds(0, LANES)], s1.at[1])
    wait(xc.at[pl.ds(0, D - OWN), pl.ds(HALO, CHUNK)], s1.at[2])
    tails = pl.ds(0, OWN)
    wait(xc.at[pl.ds(0, 6 * OWN), pl.ds(0, HALO)], s1.at[3])

    @pl.when(c == 0)
    def _():
        wait(xc.at[tails, pl.ds(0, HALO)], s1.at[3])

    @pl.when(s < SEQ - 1)
    def _():
        wait(xc.at[tails, pl.ds(0, HALO)], s1.at[3])

    wait(pbuf.at[pl.ds(0, 6)], s1.at[4])
    wait(wbuf.at[:, pl.ds(0, 6)], s1.at[5])
    for i, buf in enumerate((ksnd, gsnd, ysnd)):
        wait(buf.at[pl.ds(0, DEV - 1)], s3.at[i])
    wait(osnd.at[pl.ds(0, D - OWN), :], s6)


def body(
    inputs,
    w_in,
    b_in,
    short_kernel,
    positional,
    filter_in,
    filter_bias,
    filter_freq,
    filter_hidden,
    filter_out,
    decay,
    conv_bias,
    w_out,
    b_out,
):
    dma = pltpu.SemaphoreType.DMA
    hbm = pl.BlockSpec(memory_space=pl.ANY)
    vmem = pltpu.VMEM
    return pl.pallas_call(
        kernel,
        out_shape=pltpu.VMEM((OWN, SPAN), BF16),
        in_specs=[hbm] * 20,
        out_specs=pl.BlockSpec(memory_space=pltpu.VMEM),
        scratch_shapes=[
            vmem((3, OWN), F32),
            vmem((3, 3, OWN), F32),
            vmem((OWN, ORDER), F32),
            vmem((1, OWN), F32),
            vmem((1, OWN), F32),
            vmem((1, OWN), F32),
            vmem((5, SPAN), F32),
            vmem((5, ORDER), F32),
            vmem((3, ORDER), F32),
            vmem((3, ORDER), F32),
            vmem((2, ORDER, ORDER), F32),
            vmem((D, D), BF16),
            vmem((16, OWN), F32),
            vmem((16, ORDER), F32),
            vmem((OWN, LANES), F32),
            vmem((D, HALO + CHUNK), BF16),
            vmem((3, CH, 2, 16, D), BF16),
            vmem((CH, 4, 8, LANES), F32),
            vmem((D, LANES), F32),
            vmem((2, D, CHUNK), BF16),
            vmem((9, 2, D, LANES), F32),
            vmem((6, D, LANES), F32),
            vmem((DEV, RADIX, LANES), F32),
            vmem((D, CHUNK), F32),
            vmem((D, CHUNK), F32),
            vmem((DEV, RADIX, LANES), BF16),
            vmem((DEV, RADIX, LANES), BF16),
            vmem((DEV, RADIX, LANES), BF16),
            vmem((DEV, RADIX, LANES), BF16),
            vmem((4 * D, D), BF16),
            vmem((2 * D, 2 * D), BF16),
            vmem((2, D, D), BF16),
            vmem((2, D, D), BF16),
            vmem((2, D, CHUNK), F32),
            vmem((D, LANES), F32),
            vmem((2, D, CHUNK), F32),
            vmem((RADIX, D, 2 * LANES), BF16),
            vmem((RADIX, D, 2 * LANES), BF16),
            vmem((RADIX, D, 2 * LANES), F32),
            vmem((RADIX, 2, D, LANES), F32),
            vmem((2 * D, CHUNK), BF16),
            vmem((2 * D, CHUNK), BF16),
            vmem((DEV, RADIX, LANES), BF16),
            vmem((DEV, RADIX, LANES), BF16),
            vmem((D, CHUNK), BF16),
            dma((12,)),
            dma((6,)),
            pltpu.SemaphoreType.REGULAR,
            dma((6,)),
            dma((6,)),
            dma((3,)),
            dma((3,)),
            dma,
            dma,
        ],
        compiler_params=pltpu.CompilerParams(collective_id=0, has_side_effects=True),
    )(
        inputs,
        w_in,
        b_in,
        short_kernel.transpose(0, 2, 1),
        filter_out,
        decay.reshape(1, OWN),
        conv_bias.reshape(1, OWN),
        b_out.reshape(1, OWN),
        positional,
        filter_in.T,
        filter_bias,
        filter_freq,
        filter_hidden,
        w_out,
        *tables(),
    )


def solution(mesh):
    in_specs = (
        P("ch", "seq"),
        P(None, "ch", None),
        P(None, "ch"),
        P(None, "ch", None),
        P(None, "seq"),
        P(),
        P(),
        P(),
        P(),
        P("ch", None),
        P("ch"),
        P("ch"),
        P(),
        P("ch"),
    )
    return jax.shard_map(
        body, mesh=mesh, in_specs=in_specs, out_specs=P("ch", "seq"), check_vma=False
    )
```

```python
import math

import jax
import jax.numpy as jnp
import numpy as np
from jax import lax
from jax.experimental import pallas as pl
from jax.experimental.pallas import tpu as pltpu
from jax.sharding import PartitionSpec as P

MESH = pl.DeviceIdType.MESH
F32 = jnp.float32
BF16 = jnp.bfloat16
HIGHEST = lax.Precision.HIGHEST

SEQ, CH = 32, 8
DEV = SEQ * CH
D = 256
OWN = D // CH
SPAN = 4096
CHUNK = SPAN // CH
LENGTH = SPAN * SEQ
HALO = 128
LANES = 128
RADIX = CHUNK // LANES
ORDER = 64
FAR = (4, 3, 5, 2, 6, 1, 7)
FARX = (2, 1, 3, 0)
BIAS, TAPS, DECAY, DIRECT, OUTB = 0, 3, 12, 13, 14
BLOCKS, WIDE = 4, 1024
PI_HIGH, PI_LOW = 3.1414794921875, 0.00011315941810607910156


def halves(table):
    high = np.asarray(table, np.float64).astype(jnp.bfloat16)
    low = (np.asarray(table, np.float64) - high.astype(np.float64)).astype(jnp.bfloat16)
    return high, low


def tables():
    rows = np.arange(D)
    f1 = np.arange(D) + 0.25
    angle = 2.0 * np.pi * ((np.outer(4 * f1, rows) % (4 * D)) / (4 * D))
    first = np.concatenate([np.cos(angle), -np.sin(angle)], axis=0)
    first_stack = np.concatenate(halves(first), axis=0)
    last_stack = np.concatenate(halves(first.T / LENGTH), axis=0)
    lanes = np.arange(LANES)
    inner = 2.0 * np.pi * (np.outer(lanes, lanes) % LANES) / LANES
    c, s = np.cos(inner), np.sin(inner)
    forward = np.stack(halves(np.block([[c, -s], [s, c]])))
    inverse = np.stack(halves(np.block([[c, s], [-s, c]])))
    turn = 2.0 * np.pi / LENGTH * f1[:, None] * lanes[None, :]
    step = 2.0 * np.pi / CHUNK * np.arange(RADIX)[:, None] * lanes[None, :]
    twiddle = np.stack([np.cos(turn), np.sin(turn)]).astype(np.float32)
    steps = np.concatenate([np.cos(step), np.sin(step)]).astype(np.float32)
    spin = 2.0 * np.pi / (RADIX * D) * f1[:, None] * np.arange(RADIX)[None, :]
    spins = np.zeros((D, LANES), np.float32)
    spins[:, 0:RADIX] = np.cos(spin)
    spins[:, RADIX : 2 * RADIX] = np.sin(spin)
    return first_stack, last_stack, forward, inverse, twiddle, steps, spins


def split(x):
    high = x.astype(BF16)
    return high, (x - high.astype(F32)).astype(BF16)


def sine(v):
    turns = jnp.floor(v * (1.0 / math.pi) + 0.5)
    rest = (v - turns * PI_HIGH) - turns * PI_LOW
    half = turns * 0.5
    rest = rest * (1.0 - 4.0 * (half - jnp.floor(half)))
    square = rest * rest
    poly = 2.6083159809786593541503e-06 * square - 0.0001981069071916863322258
    poly = poly * square + 0.00833307858556509017944336
    poly = poly * square - 0.166666597127914428710938
    return rest + rest * (square * poly)


def mm(a, b):
    return jnp.dot(a, b, preferred_element_type=F32)


def kernel(
    x_ref,
    w_ref,
    bin_ref,
    taps_ref,
    fout_ref,
    decay_ref,
    direct_ref,
    bout_ref,
    pos_ref,
    fin_ref,
    fbias_ref,
    ffreq_ref,
    fhid_ref,
    wout_ref,
    first_ref,
    last_ref,
    fwd_ref,
    inv_ref,
    twid_ref,
    step_ref,
    spin_ref,
    out_ref,
    bin_v,
    taps_v,
    fout_v,
    decay_v,
    direct_v,
    bout_v,
    pos_v,
    fin_v,
    fbias_v,
    ffreq_v,
    fhid_v,
    wout_v,
    raw,
    rawnet,
    prm,
    xc,
    wbuf,
    pbuf,
    pflat,
    xs,
    cols,
    spins,
    stage,
    keep0,
    keepg,
    diag,
    weight,
    act,
    value_v,
    kstage,
    ksnd,
    krcv,
    gsnd,
    grcv,
    first_v,
    last_v,
    fwd_v,
    inv_v,
    base_v,
    step_v,
    spin_v,
    twid_v,
    sect,
    chi,
    clo,
    spec,
    back,
    dhi,
    dlo,
    ysnd,
    yrcv,
    osnd,
    small_sem,
    const_sem,
    gate,
    s1,
    r1,
    s3,
    r3,
    s6,
    r6,
):
    s = lax.axis_index("seq")
    c = lax.axis_index("ch")
    me = s * CH + c
    px, py, pk = s // 8, lax.rem(s // 2, 4), lax.rem(s, 2)
    own = pl.multiple_of(c * OWN, OWN)
    rows_own = pl.ds(own, OWN)

    smalls = [
        pltpu.make_async_copy(src, dst, small_sem.at[i])
        for i, (src, dst) in enumerate(
            [
                (bin_ref, bin_v),
                (taps_ref, taps_v),
                (fout_ref, fout_v),
                (decay_ref, decay_v),
                (direct_ref, direct_v),
                (bout_ref, bout_v),
                (pos_ref, pos_v),
                (fin_ref, fin_v),
                (fbias_ref, fbias_v),
                (ffreq_ref, ffreq_v),
                (fhid_ref, fhid_v),
                (wout_ref, wout_v),
            ]
        )
    ]
    consts = [
        pltpu.make_async_copy(src, dst, const_sem.at[i])
        for i, (src, dst) in enumerate(
            [
                (spin_ref, spin_v),
                (first_ref, first_v),
                (twid_ref, base_v),
                (step_ref, step_v),
                (fwd_ref, fwd_v),
                (inv_ref, inv_v),
                (last_ref, last_v),
            ]
        )
    ]
    for copy in smalls:
        copy.start()

    bar = pltpu.get_barrier_semaphore()

    def greet(sem, to):
        pl.semaphore_signal(sem, inc=1, device_id=to, device_id_type=MESH)

    for i in range(1, CH):
        greet(bar, (s, lax.rem(c + i, CH)))
    for i in range(1, SEQ):
        greet(bar, (lax.rem(s + i, SEQ), c))

    @pl.when(jnp.logical_and(c == 0, s > 0))
    def _():
        for j in range(CH):
            greet(bar, (s - 1, j))

    for i in (0, 1, 3, 4, 5):
        smalls[i].wait()
    raw[...] = jnp.zeros_like(raw)
    raw[0:3, :] = bin_v[...]
    for j in range(3):
        raw[3 + 3 * j : 6 + 3 * j, :] = taps_v[j]
    raw[12:13, :] = decay_v[...]
    raw[13:14, :] = direct_v[...]
    raw[14:15, :] = bout_v[...]

    def columns(rows, n):
        eye = (
            lax.broadcasted_iota(jnp.int32, (n, n), 0) == lax.broadcasted_iota(jnp.int32, (n, n), 1)
        ).astype(F32)
        return lax.dot_general(
            eye, rows, (((1,), (1,)), ((), ())), precision=HIGHEST, preferred_element_type=F32
        )

    prm[...] = jnp.zeros_like(prm)
    mine = columns(raw[...], OWN)
    prm[:, 0:16] = mine
    pl.semaphore_wait(bar, jnp.where(s < SEQ - 1, SEQ + CH - 1, SEQ + CH - 2))

    def put(src, dst, send, recv, to):
        pltpu.make_async_remote_copy(
            src_ref=src, dst_ref=dst, send_sem=send, recv_sem=recv, device_id=to, device_id_type=MESH
        ).start()

    def wait(ref, sem):
        pltpu.make_async_copy(ref, ref, sem).wait()

    half = pl.ds(pl.multiple_of(lax.rem(py, 2) * LANES, LANES), LANES)
    quarter = pl.ds(pl.multiple_of(py * 8, 8), 8)
    parts = ((0, pl.ds(0, 2), 2), (1, pl.ds(2, 1), 1))
    slab = pl.ds(pl.multiple_of((py // 2) * 16, 16), 16)
    p_src = prm.at[quarter, :]
    p_dst = pbuf.at[c, py]
    x_dst = xc.at[rows_own, pl.ds(HALO, CHUNK)]
    h_dst = xc.at[rows_own, pl.ds(0, HALO)]

    def chunk(j):
        return x_ref.at[:, pl.ds(pl.multiple_of(j * CHUNK, CHUNK), CHUNK)]

    def tail(j):
        return x_ref.at[:, pl.ds(pl.multiple_of(j * CHUNK + CHUNK - HALO, HALO), HALO)]

    for i in FAR:
        put(p_src, p_dst, s1.at[0], r1.at[0], (s, lax.rem(c + i, CH)))
    for i in FAR:
        for part, js, _ in parts:

            @pl.when(pk == part)
            def _():
                put(
                    w_ref.at[js, slab, half],
                    wbuf.at[js, c, py // 2, :, half],
                    s1.at[1],
                    r1.at[1],
                    (s, lax.rem(c + i, CH)),
                )

    for i in FAR:
        j = lax.rem(c + i, CH)
        put(chunk(j), x_dst, s1.at[2], r1.at[2], (s, j))

        @pl.when(j > 0)
        def _():
            put(tail(j - 1), h_dst, s1.at[3], r1.at[3], (s, j))

    @pl.when(s < SEQ - 1)
    def _():
        put(tail(CH - 1), h_dst, s1.at[3], r1.at[3], (s + 1, 0))

    pltpu.make_async_copy(p_src, p_dst, r1.at[0]).start()
    for part, js, _ in parts:

        @pl.when(pk == part)
        def _():
            pltpu.make_async_copy(
                w_ref.at[js, slab, half], wbuf.at[js, c, py // 2, :, half], r1.at[1]
            ).start()

    pltpu.make_async_copy(chunk(c), x_dst, r1.at[2]).start()

    @pl.when(c > 0)
    def _():
        pltpu.make_async_copy(tail(c - 1), h_dst, r1.at[3]).start()

    @pl.when(me == 0)
    def _():
        xc[:, 0:HALO] = jnp.zeros((D, HALO), BF16)

    for i in range(1, SEQ):
        greet(gate, (lax.rem(s + i, SEQ), c))
    for copy in consts:
        copy.start()
    for i in (2, 6, 7, 8, 9, 10, 11):
        smalls[i].wait()

    rawnet[...] = jnp.zeros_like(rawnet)
    rawnet[0:5, :] = fin_v[...]
    rawnet[5:8, :] = fbias_v[...]
    rawnet[8:11, :] = ffreq_v[...]
    net = columns(rawnet[...], ORDER)
    diag[...] = jnp.zeros_like(diag)
    for b in range(BLOCKS):
        at = slice(b * ORDER, (b + 1) * ORDER)
        diag[0, at, at] = fhid_v[0]
        diag[1, at, at] = fhid_v[1]
        diag[2, b * OWN : (b + 1) * OWN, at] = fout_v[...]
    for i in range(3):
        high, low = split(diag[i])
        weight[i, 0:D] = high
        weight[i, D : 2 * D] = low

    def tile(step):
        b, side = step // 2, lax.rem(step, 2)
        rows = pl.ds(pl.multiple_of(b * ORDER, ORDER), ORDER)
        return b, side, rows, pl.ds(pl.multiple_of(side * CHUNK, CHUNK), CHUNK)

    def keep(layer, value, rows, lanes):
        high, low = split(
            sine(net[:, 8 + layer : 9 + layer] * (value + net[:, 5 + layer : 6 + layer]))
        )
        act[0, rows, lanes] = high
        act[1, rows, lanes] = low

    def enter(step, carry):
        b, side, rows, lanes = tile(step)
        here = pl.ds(pl.multiple_of(step * CHUNK, CHUNK), CHUNK)
        value = net[:, 0:1] * pos_v[0:1, here]
        for i in range(1, 5):
            value = value + net[:, i : i + 1] * pos_v[i : i + 1, here]
        keep(0, value, rows, lanes)
        return carry

    lax.fori_loop(0, 2 * BLOCKS, enter, 0)

    def product(i, n):
        both, one = weight[i, 0 : D + n], weight[i, 0:n]
        wide = mm(both, act[0])
        return wide[0:n] + wide[D : D + n] + mm(one, act[1])

    def hidden(layer):
        value_v[...] = product(layer - 1, D)

        def leave(step, carry):
            b, side, rows, lanes = tile(step)
            keep(layer, value_v[rows, lanes], rows, lanes)
            return carry

        lax.fori_loop(0, 2 * BLOCKS, leave, 0)

    hidden(1)

    p_mine = pbuf.at[:, py]
    wait(p_mine, r1.at[0])
    around = [(s - 2 * py + 2 * lax.rem(py + i, 4), c) for i in (2, 1, 3)]
    for to in around:
        put(p_mine, p_mine, s1.at[4], r1.at[4], to)
    for part, js, _ in parts:

        @pl.when(pk == part)
        def _():
            w_mine = wbuf.at[js, :, py // 2, :, half]
            wait(w_mine, r1.at[1])
            for to in around:
                put(w_mine, w_mine, s1.at[5], r1.at[5], to)

    hidden(2)
    values = product(2, BLOCKS * OWN)
    lane = lax.broadcasted_iota(jnp.int32, (1, WIDE), 1)
    for b in range(BLOCKS):
        places = s * SPAN + b * WIDE + lane
        scaled = places.astype(F32) / (LENGTH - 1)
        window = jnp.exp(-(scaled * mine[:, DECAY : DECAY + 1]))
        block = values[b * OWN : (b + 1) * OWN] * window
        for q in range(2 * RADIX):
            kstage[:, 2 * b + q // RADIX, q % RADIX, :] = block[:, q * LANES : (q + 1) * LANES]
    ksnd[...] = kstage[...].astype(BF16)
    far = [(i, j, l) for i in (2, 1, 3, 0) for j in (2, 1, 3, 0) for l in (1, 0)]
    theirs = pl.ds(pl.multiple_of(s * CH, CH), CH)
    for i, j, l in far[:-1]:
        si = lax.rem(px + i, 4) * 8 + lax.rem(py + j, 4) * 2 + lax.rem(pk + l, 2)
        put(ksnd.at[si], krcv.at[theirs], s3.at[0], r3.at[0], (si, c))
    pltpu.make_async_copy(ksnd.at[s], krcv.at[theirs], r3.at[0]).start()

    wait(pbuf.at[pl.ds(0, 6)], r1.at[4])
    pflat[...] = pbuf[...].reshape(D, LANES)
    for part, js, n in parts:

        @pl.when(pk == part)
        def _():
            wait(wbuf.at[js, pl.ds(0, 6)], r1.at[5])
            put(wbuf.at[js], wbuf.at[js], s1.at[6], r1.at[6], (s + 1 - 2 * pk, c))

    for copy in consts:
        copy.wait()
    for i in range(6):
        at = 1 + i if i < 3 else 2 + i
        spins[i] = jnp.broadcast_to(spin_v[:, at : at + 1], (D, LANES))
    for h in range(RADIX):
        lanes = slice(h * LANES, (h + 1) * LANES)
        cs, sn = step_v[h : h + 1, :], step_v[RADIX + h : RADIX + h + 1, :]
        twid_v[0, :, lanes] = base_v[0] * cs - base_v[1] * sn
        twid_v[1, :, lanes] = base_v[1] * cs + base_v[0] * sn

    def scatter(src, dst, row, at, dz, by_channel):
        send, recv = s3.at[at], r3.at[at]
        pair = 2 * lax.rem(c // 2 + dz, 4)
        odd = lax.rem(c, 2)
        planes = (pair + 1 - odd, pair + odd)

        def ring(dx, near):
            sx = lax.rem(px + dx, 4) * 8
            for dy in (2, 1, 3, 0):
                for dk in (1, 0):
                    si = sx + lax.rem(py + dy, 4) * 2 + lax.rem(pk + dk, 2)
                    for cj in planes[: 1 if near and dy == 0 and dk == 0 else 2]:
                        at_src = cj * SEQ + si if by_channel else si * CH + cj
                        put(src.at[at_src], dst.at[row], send, recv, (si, cj))

        def layer(t, carry):
            ring(2 + (t + 1) // 2 * (1 - 2 * lax.rem(t, 2)), False)
            return carry

        if dz:
            lax.fori_loop(0, 4, layer, 0)
        else:
            lax.fori_loop(0, 3, layer, 0)
            ring(0, True)
            at_src = c * SEQ + s if by_channel else me
            pltpu.make_async_copy(src.at[at_src], dst.at[row], recv).start()

    for j in range(3):
        bias = jnp.broadcast_to(pflat[:, BIAS + j : BIAS + j + 1], (D, LANES))
        for i in range(3):
            at = TAPS + 3 * j + i
            tap = jnp.broadcast_to(pflat[:, at : at + 1], (D, LANES))
            cols[3 * j + i, 0] = tap
            cols[3 * j + i, 1] = tap * bias

    pl.semaphore_wait(gate, SEQ - 1)
    wait(xc.at[:, pl.ds(HALO, CHUNK)], r1.at[2])

    @pl.when(me > 0)
    def _():
        wait(xc.at[:, pl.ds(0, HALO)], r1.at[3])

    for part, js, _ in parts:

        @pl.when(pk != part)
        def _():
            wait(wbuf.at[js], r1.at[6])

    wide = xc[...].astype(F32)
    for i in (0, 1):
        xs[i] = pltpu.roll(wide, 2 - i, 1)[:, HALO:].astype(BF16)
    place = lax.broadcasted_iota(jnp.int32, (1, LANES), 1)
    started = [jnp.logical_or(place >= 2 - i, me > 0).astype(F32) for i in (0, 1)]

    for dz in FARX:
        block = lax.rem(c // 2 + dz, 4)
        lo = pl.multiple_of(block * 64, 64)
        rows = pl.ds(lo, 64)
        w = wbuf[:, pl.ds(block * 2, 2)].reshape(3 * 64, D)
        taken = [mm(w, xs[0]), mm(w, xs[1]), mm(w, xc[:, HALO:])]
        for r in range(RADIX):
            lanes = slice(r * LANES, (r + 1) * LANES)
            streams = []
            for j in range(3):
                total = None
                for i in range(3):
                    shifted_bias = cols[3 * j + i, 1, rows, :]
                    if r == 0 and i < 2:
                        shifted_bias = shifted_bias * started[i]
                    term = cols[3 * j + i, 0, rows, :] * taken[i][64 * j : 64 * j + 64, lanes]
                    term = term + shifted_bias
                    total = term if total is None else total + term
                streams.append(total)
            gated = streams[2] * streams[1]
            keep0[rows, lanes] = streams[0]
            keepg[rows, lanes] = gated
            stage[rows, r, :] = gated
        gsnd[rows] = stage[rows].astype(BF16)
        scatter(gsnd, grcv, me, 1, dz, True)

    def sections(rcv):
        stage[...] = rcv[...].astype(F32)
        x = jnp.concatenate([stage[:, r, :] for r in range(RADIX)], axis=1).astype(BF16)
        for part in range(2):
            sect[part] = mm(first_v[part * D : (part + 1) * D, :], x) + mm(
                first_v[(2 + part) * D : (3 + part) * D, :], x
            )

        def ahead(step, carry):
            rows = pl.ds(pl.multiple_of(step * 32, 32), 32)
            re, im = [], []
            for r in range(RADIX):
                lanes = slice(r * LANES, (r + 1) * LANES)
                a, b = sect[0, rows, lanes], sect[1, rows, lanes]
                if r:
                    cs, sn = spins[r - 1, rows, :], spins[r + 2, rows, :]
                    a, b = a * cs + b * sn, b * cs - a * sn
                re.append(a)
                im.append(b)
            e0r, e0i, e1r, e1i = re[0] + re[2], im[0] + im[2], re[0] - re[2], im[0] - im[2]
            o0r, o0i, o1r, o1i = re[1] + re[3], im[1] + im[3], re[1] - re[3], im[1] - im[3]
            outs = [
                (e0r + o0r, e0i + o0i),
                (e1r + o1i, e1i - o1r),
                (e0r - o0r, e0i - o0i),
                (e1r - o1i, e1i + o1r),
            ]
            for h, (a, b) in enumerate(outs):
                cs = twid_v[0, rows, h * LANES : (h + 1) * LANES]
                sn = twid_v[1, rows, h * LANES : (h + 1) * LANES]
                high, low = split(jnp.concatenate([a * cs + b * sn, b * cs - a * sn], axis=1))
                chi[h, rows, :] = high
                clo[h, rows, :] = low
            return carry

        lax.fori_loop(0, D // 32, ahead, 0)

    def spectrum(h):
        high, low = chi[h], clo[h]
        return mm(high, fwd_v[0]) + mm(low, fwd_v[0]) + mm(high, fwd_v[1])

    wait(krcv, r3.at[0])
    sections(krcv)
    for h in range(RADIX):
        spec[h] = spectrum(h)
    wait(grcv, r3.at[1])
    sections(grcv)
    for h in range(RADIX):
        g, k = spectrum(h), spec[h]
        gr, gi, kr, ki = g[:, :LANES], g[:, LANES:], k[:, :LANES], k[:, LANES:]
        high, low = split(jnp.concatenate([gr * kr - gi * ki, gr * ki + gi * kr], axis=1))
        z = mm(high, inv_v[0]) + mm(low, inv_v[0]) + mm(high, inv_v[1])
        zr, zi = z[:, :LANES], z[:, LANES:]
        cs = twid_v[0, :, h * LANES : (h + 1) * LANES]
        sn = twid_v[1, :, h * LANES : (h + 1) * LANES]
        back[h, 0] = zr * cs - zi * sn
        back[h, 1] = zi * cs + zr * sn

    def behind(step, carry):
        lo = pl.multiple_of(step * 32, 32)
        rows = pl.ds(lo, 32)
        rows_im = pl.ds(pl.multiple_of(D + lo, 32), 32)
        re = [back[h, 0, rows, :] for h in range(RADIX)]
        im = [back[h, 1, rows, :] for h in range(RADIX)]
        e0r, e0i, e1r, e1i = re[0] + re[2], im[0] + im[2], re[0] - re[2], im[0] - im[2]
        o0r, o0i, o1r, o1i = re[1] + re[3], im[1] + im[3], re[1] - re[3], im[1] - im[3]
        outs = [
            (e0r + o0r, e0i + o0i),
            (e1r - o1i, e1i + o1r),
            (e0r - o0r, e0i - o0i),
            (e1r + o1i, e1i - o1r),
        ]
        for r, (a, b) in enumerate(outs):
            if r:
                cs, sn = spins[r - 1, rows, :], spins[r + 2, rows, :]
                a, b = a * cs - b * sn, b * cs + a * sn
            lanes = slice(r * LANES, (r + 1) * LANES)
            high, low = split(a)
            dhi[rows, lanes] = high
            dlo[rows, lanes] = low
            high, low = split(b)
            dhi[rows_im, lanes] = high
            dlo[rows_im, lanes] = low
        return carry

    lax.fori_loop(0, D // 32, behind, 0)
    last_hi, last_lo = last_v[0:D, :], last_v[D : 2 * D, :]
    settled = mm(last_hi, dhi[...]) + mm(last_lo, dhi[...]) + mm(last_hi, dlo[...])
    for r in range(RADIX):
        stage[:, r, :] = settled[:, r * LANES : (r + 1) * LANES]
    ysnd[...] = stage[...].astype(BF16)

    for dz in FARX:
        scatter(ysnd, yrcv, c * SEQ + s, 2, dz, False)
    wait(yrcv, r3.at[2])

    stage[...] = yrcv[...].astype(F32)
    convolved = jnp.concatenate([stage[:, r, :] for r in range(RADIX)], axis=1)
    convolved = convolved + pflat[:, DIRECT : DIRECT + 1] * keepg[...]
    mixed = (keep0[...] * convolved).astype(BF16)
    osnd[...] = (mm(wout_v[...], mixed) + pflat[:, OUTB : OUTB + 1]).astype(BF16)
    o_dst = out_ref.at[:, pl.ds(pl.multiple_of(c * CHUNK, CHUNK), CHUNK)]
    for i in FAR:
        j = lax.rem(c + i, CH)
        put(osnd.at[pl.ds(pl.multiple_of(j * OWN, OWN), OWN), :], o_dst, s6, r6, (s, j))
    pltpu.make_async_copy(osnd.at[rows_own, :], o_dst, r6).start()

    wait(out_ref, r6)
    most = pl.ds(0, CH - 1)
    wait(pbuf.at[most, 0], s1.at[0])
    for part, js, _ in parts:

        @pl.when(pk == part)
        def _():
            wait(wbuf.at[js, most, 0, :, pl.ds(0, LANES)], s1.at[1])
            wait(wbuf.at[js, pl.ds(0, 6)], s1.at[5])
            wait(wbuf.at[js], s1.at[6])

    wait(xc.at[pl.ds(0, D - OWN), pl.ds(HALO, CHUNK)], s1.at[2])
    tails = pl.ds(0, OWN)
    wait(xc.at[pl.ds(0, 6 * OWN), pl.ds(0, HALO)], s1.at[3])

    @pl.when(c == 0)
    def _():
        wait(xc.at[tails, pl.ds(0, HALO)], s1.at[3])

    @pl.when(s < SEQ - 1)
    def _():
        wait(xc.at[tails, pl.ds(0, HALO)], s1.at[3])

    wait(pbuf.at[pl.ds(0, 6)], s1.at[4])
    wait(ksnd.at[pl.ds(0, SEQ - 1)], s3.at[0])
    for i, buf in ((1, gsnd), (2, ysnd)):
        wait(buf.at[pl.ds(0, DEV - 1)], s3.at[i])
    wait(osnd.at[pl.ds(0, D - OWN), :], s6)


def body(
    inputs,
    w_in,
    b_in,
    short_kernel,
    positional,
    filter_in,
    filter_bias,
    filter_freq,
    filter_hidden,
    filter_out,
    decay,
    conv_bias,
    w_out,
    b_out,
):
    dma = pltpu.SemaphoreType.DMA
    hbm = pl.BlockSpec(memory_space=pl.ANY)
    vmem = pltpu.VMEM
    return pl.pallas_call(
        kernel,
        out_shape=pltpu.VMEM((OWN, SPAN), BF16),
        in_specs=[hbm] * 21,
        out_specs=pl.BlockSpec(memory_space=pltpu.VMEM),
        scratch_shapes=[
            vmem((3, OWN), F32),
            vmem((3, 3, OWN), F32),
            vmem((OWN, ORDER), F32),
            vmem((1, OWN), F32),
            vmem((1, OWN), F32),
            vmem((1, OWN), F32),
            vmem((5, SPAN), F32),
            vmem((5, ORDER), F32),
            vmem((3, ORDER), F32),
            vmem((3, ORDER), F32),
            vmem((2, ORDER, ORDER), F32),
            vmem((D, D), BF16),
            vmem((16, OWN), F32),
            vmem((16, ORDER), F32),
            vmem((OWN, LANES), F32),
            vmem((D, HALO + CHUNK), BF16),
            vmem((3, CH, 2, 16, D), BF16),
            vmem((CH, 4, 8, LANES), F32),
            vmem((D, LANES), F32),
            vmem((2, D, CHUNK), BF16),
            vmem((9, 2, D, LANES), F32),
            vmem((6, D, LANES), F32),
            vmem((DEV, RADIX, LANES), F32),
            vmem((D, CHUNK), F32),
            vmem((D, CHUNK), F32),
            vmem((3, D, D), F32),
            vmem((3, 2 * D, D), BF16),
            vmem((2, D, WIDE), BF16),
            vmem((D, WIDE), F32),
            vmem((OWN, CH, RADIX, LANES), F32),
            vmem((OWN, CH, RADIX, LANES), BF16),
            vmem((DEV, RADIX, LANES), BF16),
            vmem((DEV, RADIX, LANES), BF16),
            vmem((DEV, RADIX, LANES), BF16),
            vmem((4 * D, D), BF16),
            vmem((2 * D, 2 * D), BF16),
            vmem((2, D, D), BF16),
            vmem((2, D, D), BF16),
            vmem((2, D, LANES), F32),
            vmem((2 * RADIX, LANES), F32),
            vmem((D, LANES), F32),
            vmem((2, D, CHUNK), F32),
            vmem((2, D, CHUNK), F32),
            vmem((RADIX, D, 2 * LANES), BF16),
            vmem((RADIX, D, 2 * LANES), BF16),
            vmem((RADIX, D, 2 * LANES), F32),
            vmem((RADIX, 2, D, LANES), F32),
            vmem((2 * D, CHUNK), BF16),
            vmem((2 * D, CHUNK), BF16),
            vmem((DEV, RADIX, LANES), BF16),
            vmem((DEV, RADIX, LANES), BF16),
            vmem((D, CHUNK), BF16),
            dma((12,)),
            dma((7,)),
            pltpu.SemaphoreType.REGULAR,
            dma((7,)),
            dma((7,)),
            dma((3,)),
            dma((3,)),
            dma,
            dma,
        ],
        compiler_params=pltpu.CompilerParams(collective_id=0, has_side_effects=True),
    )(
        inputs,
        w_in,
        b_in,
        short_kernel.transpose(0, 2, 1),
        filter_out,
        decay.reshape(1, OWN),
        conv_bias.reshape(1, OWN),
        b_out.reshape(1, OWN),
        positional,
        filter_in.T,
        filter_bias,
        filter_freq,
        filter_hidden,
        w_out,
        *tables(),
    )


def solution(mesh):
    in_specs = (
        P("ch", "seq"),
        P(None, "ch", None),
        P(None, "ch"),
        P(None, "ch", None),
        P(None, "seq"),
        P(),
        P(),
        P(),
        P(),
        P("ch", None),
        P("ch"),
        P("ch"),
        P(),
        P("ch"),
    )
    return jax.shard_map(
        body, mesh=mesh, in_specs=in_specs, out_specs=P("ch", "seq"), check_vma=False
    )
```

```python
import math

import jax
import jax.numpy as jnp
import numpy as np
from jax import lax
from jax.experimental import pallas as pl
from jax.experimental.pallas import tpu as pltpu
from jax.sharding import PartitionSpec as P

MESH = pl.DeviceIdType.MESH
F32 = jnp.float32
BF16 = jnp.bfloat16
HIGHEST = lax.Precision.HIGHEST

SEQ, CH = 32, 8
DEV = SEQ * CH
D = 256
OWN = D // CH
SPAN = 4096
CHUNK = SPAN // CH
LENGTH = SPAN * SEQ
HALO = 128
LANES = 128
RADIX = CHUNK // LANES
ORDER = 64
HALF = CHUNK // 2
PAIR = RADIX // 2
FAR = (4, 3, 5, 2, 6, 1, 7)
BIAS, TAPS, DECAY, DIRECT, OUTB = 0, 3, 12, 13, 14
BLOCKS, WIDE = 4, 1024
PI_HIGH, PI_LOW = 3.1414794921875, 0.00011315941810607910156


def halves(table):
    high = np.asarray(table, np.float64).astype(jnp.bfloat16)
    low = (np.asarray(table, np.float64) - high.astype(np.float64)).astype(jnp.bfloat16)
    return high, low


def tables():
    rows = np.arange(D)
    f1 = np.arange(D) + 0.25
    angle = 2.0 * np.pi * ((np.outer(4 * f1, rows) % (4 * D)) / (4 * D))
    first = np.concatenate([np.cos(angle), -np.sin(angle)], axis=0)
    first_stack = np.concatenate(halves(first), axis=0)
    last_stack = np.concatenate(halves(first.T / LENGTH), axis=0)
    lanes = np.arange(LANES)
    inner = 2.0 * np.pi * (np.outer(lanes, lanes) % LANES) / LANES
    c, s = np.cos(inner), np.sin(inner)
    forward = np.stack(halves(np.block([[c, -s], [s, c]])))
    inverse = np.stack(halves(np.block([[c, s], [-s, c]])))
    turn = 2.0 * np.pi / LENGTH * f1[:, None] * lanes[None, :]
    step = 2.0 * np.pi / CHUNK * np.arange(RADIX)[:, None] * lanes[None, :]
    twiddle = np.stack([np.cos(turn), np.sin(turn)]).astype(np.float32)
    steps = np.concatenate([np.cos(step), np.sin(step)]).astype(np.float32)
    spin = 2.0 * np.pi / (RADIX * D) * f1[:, None] * np.arange(RADIX)[None, :]
    spins = np.zeros((D, LANES), np.float32)
    spins[:, 0:RADIX] = np.cos(spin)
    spins[:, RADIX : 2 * RADIX] = np.sin(spin)
    return first_stack, last_stack, forward, inverse, twiddle, steps, spins


def split(x):
    high = x.astype(BF16)
    return high, (x - high.astype(F32)).astype(BF16)


def sine(v):
    turns = jnp.floor(v * (1.0 / math.pi) + 0.5)
    rest = (v - turns * PI_HIGH) - turns * PI_LOW
    half = turns * 0.5
    rest = rest * (1.0 - 4.0 * (half - jnp.floor(half)))
    square = rest * rest
    poly = 2.6083159809786593541503e-06 * square - 0.0001981069071916863322258
    poly = poly * square + 0.00833307858556509017944336
    poly = poly * square - 0.166666597127914428710938
    return rest + rest * (square * poly)


def mm(a, b):
    return jnp.dot(a, b, preferred_element_type=F32)


def kernel(
    x_ref,
    w_ref,
    bin_ref,
    taps_ref,
    fout_ref,
    decay_ref,
    direct_ref,
    bout_ref,
    pos_ref,
    fin_ref,
    fbias_ref,
    ffreq_ref,
    fhid_ref,
    wout_ref,
    first_ref,
    last_ref,
    fwd_ref,
    inv_ref,
    twid_ref,
    step_ref,
    spin_ref,
    out_ref,
    bin_v,
    taps_v,
    fout_v,
    decay_v,
    direct_v,
    bout_v,
    pos_v,
    fin_v,
    fbias_v,
    ffreq_v,
    fhid_v,
    wout_v,
    raw,
    rawnet,
    prm,
    xc,
    wbuf,
    pbuf,
    pflat,
    xs,
    cols,
    spins,
    stage,
    stage2,
    keep0,
    keepg,
    diag,
    weight,
    act,
    value_v,
    kstage,
    ksnd,
    krcv,
    gsnd,
    grcv,
    first_v,
    last_v,
    fwd_v,
    inv_v,
    base_v,
    step_v,
    spin_v,
    twid_v,
    sect,
    chi,
    clo,
    spec,
    back,
    dhi,
    dlo,
    ysnd,
    yrcv,
    osnd,
    small_sem,
    const_sem,
    ring_sem,
    gate,
    s1,
    r1,
    s3,
    r3,
    s6,
    r6,
):
    s = lax.axis_index("seq")
    c = lax.axis_index("ch")
    me = s * CH + c
    px, py, pk = s // 8, lax.rem(s // 2, 4), lax.rem(s, 2)
    quad = py + pk * (px - py)
    own = pl.multiple_of(c * OWN, OWN)
    rows_own = pl.ds(own, OWN)

    smalls = [
        pltpu.make_async_copy(src, dst, small_sem.at[i])
        for i, (src, dst) in enumerate(
            [
                (bin_ref, bin_v),
                (taps_ref, taps_v),
                (fout_ref, fout_v),
                (decay_ref, decay_v),
                (direct_ref, direct_v),
                (bout_ref, bout_v),
                (pos_ref, pos_v),
                (fin_ref, fin_v),
                (fbias_ref, fbias_v),
                (ffreq_ref, ffreq_v),
                (fhid_ref, fhid_v),
                (wout_ref, wout_v),
            ]
        )
    ]
    consts = [
        pltpu.make_async_copy(src, dst, const_sem.at[i])
        for i, (src, dst) in enumerate(
            [
                (spin_ref, spin_v),
                (first_ref, first_v),
                (twid_ref, base_v),
                (step_ref, step_v),
                (fwd_ref, fwd_v),
                (inv_ref, inv_v),
                (last_ref, last_v),
            ]
        )
    ]
    for copy in smalls:
        copy.start()

    bar = pltpu.get_barrier_semaphore()

    def greet(sem, to):
        pl.semaphore_signal(sem, inc=1, device_id=to, device_id_type=MESH)

    for i in range(1, CH):
        greet(bar, (s, lax.rem(c + i, CH)))
    for i in range(1, SEQ):
        greet(bar, (lax.rem(s + i, SEQ), c))

    @pl.when(jnp.logical_and(c == 0, s > 0))
    def _():
        for j in range(CH):
            greet(bar, (s - 1, j))

    for i in (0, 1, 3, 4, 5):
        smalls[i].wait()
    raw[...] = jnp.zeros_like(raw)
    raw[0:3, :] = bin_v[...]
    for j in range(3):
        raw[3 + 3 * j : 6 + 3 * j, :] = taps_v[j]
    raw[12:13, :] = decay_v[...]
    raw[13:14, :] = direct_v[...]
    raw[14:15, :] = bout_v[...]

    def columns(rows, n):
        eye = (
            lax.broadcasted_iota(jnp.int32, (n, n), 0) == lax.broadcasted_iota(jnp.int32, (n, n), 1)
        ).astype(F32)
        return lax.dot_general(
            eye, rows, (((1,), (1,)), ((), ())), precision=HIGHEST, preferred_element_type=F32
        )

    prm[...] = jnp.zeros_like(prm)
    mine = columns(raw[...], OWN)
    prm[:, 0:16] = mine
    pl.semaphore_wait(bar, jnp.where(s < SEQ - 1, SEQ + CH - 1, SEQ + CH - 2))

    def put(src, dst, send, recv, to):
        pltpu.make_async_remote_copy(
            src_ref=src, dst_ref=dst, send_sem=send, recv_sem=recv, device_id=to, device_id_type=MESH
        ).start()

    def wait(ref, sem):
        pltpu.make_async_copy(ref, ref, sem).wait()

    half = pl.ds(pl.multiple_of(lax.rem(quad, 2) * LANES, LANES), LANES)
    quarter = pl.ds(pl.multiple_of(quad * 8, 8), 8)
    octet = 2 * pk + quad // 2
    w_src = w_ref.at[:, pl.ds(pl.multiple_of(octet * 8, 8), 8), half]
    w_dst = wbuf.at[:, c, octet, :, half]
    p_src = prm.at[quarter, :]
    p_dst = pbuf.at[c, quad]
    x_dst = xc.at[rows_own, pl.ds(HALO, CHUNK)]
    h_dst = xc.at[rows_own, pl.ds(0, HALO)]

    def chunk(j):
        return x_ref.at[:, pl.ds(pl.multiple_of(j * CHUNK, CHUNK), CHUNK)]

    def tail(j):
        return x_ref.at[:, pl.ds(pl.multiple_of(j * CHUNK + CHUNK - HALO, HALO), HALO)]

    for i in FAR:
        put(p_src, p_dst, s1.at[0], r1.at[0], (s, lax.rem(c + i, CH)))
    for i in FAR:
        put(w_src, w_dst, s1.at[1], r1.at[1], (s, lax.rem(c + i, CH)))

    @pl.when(s < SEQ - 1)
    def _():
        put(tail(CH - 1), h_dst, s1.at[3], r1.at[3], (s + 1, 0))

    for i in FAR:
        j = lax.rem(c + i, CH)
        put(chunk(j), x_dst, s1.at[2], r1.at[2], (s, j))

        @pl.when(j > 0)
        def _():
            put(tail(j - 1), h_dst, s1.at[3], r1.at[3], (s, j))


    pltpu.make_async_copy(p_src, p_dst, r1.at[0]).start()
    pltpu.make_async_copy(w_src, w_dst, r1.at[1]).start()
    pltpu.make_async_copy(chunk(c), x_dst, r1.at[2]).start()

    @pl.when(c > 0)
    def _():
        pltpu.make_async_copy(tail(c - 1), h_dst, r1.at[3]).start()

    @pl.when(me == 0)
    def _():
        xc[:, 0:HALO] = jnp.zeros((D, HALO), BF16)

    for i in range(1, SEQ):
        greet(gate, (lax.rem(s + i, SEQ), c))
    for copy in consts:
        copy.start()
    for i in (2, 6, 7, 8, 9, 10, 11):
        smalls[i].wait()

    rawnet[...] = jnp.zeros_like(rawnet)
    rawnet[0:5, :] = fin_v[...]
    rawnet[5:8, :] = fbias_v[...]
    rawnet[8:11, :] = ffreq_v[...]
    net = columns(rawnet[...], ORDER)
    diag[...] = jnp.zeros_like(diag)
    for b in range(BLOCKS):
        at = slice(b * ORDER, (b + 1) * ORDER)
        diag[0, at, at] = fhid_v[0]
        diag[1, at, at] = fhid_v[1]
        diag[2, b * OWN : (b + 1) * OWN, at] = fout_v[...]
    for i in range(3):
        high, low = split(diag[i])
        weight[i, 0:D] = high
        weight[i, D : 2 * D] = low

    def tile(step):
        b, side = step // 2, lax.rem(step, 2)
        rows = pl.ds(pl.multiple_of(b * ORDER, ORDER), ORDER)
        return b, side, rows, pl.ds(pl.multiple_of(side * CHUNK, CHUNK), CHUNK)

    def keep(layer, value, rows, lanes):
        high, low = split(
            sine(net[:, 8 + layer : 9 + layer] * (value + net[:, 5 + layer : 6 + layer]))
        )
        act[0, rows, lanes] = high
        act[1, rows, lanes] = low

    def enter(step, carry):
        b, side, rows, lanes = tile(step)
        here = pl.ds(pl.multiple_of(step * CHUNK, CHUNK), CHUNK)
        value = net[:, 0:1] * pos_v[0:1, here]
        for i in range(1, 5):
            value = value + net[:, i : i + 1] * pos_v[i : i + 1, here]
        keep(0, value, rows, lanes)
        return carry

    lax.fori_loop(0, 2 * BLOCKS, enter, 0)

    def product(i, n):
        both, one = weight[i, 0 : D + n], weight[i, 0:n]
        wide = mm(both, act[0])
        return wide[0:n] + wide[D : D + n] + mm(one, act[1])

    def hidden(layer):
        value_v[...] = product(layer - 1, D)

        def leave(step, carry):
            b, side, rows, lanes = tile(step)
            keep(layer, value_v[rows, lanes], rows, lanes)
            return carry

        lax.fori_loop(0, 2 * BLOCKS, leave, 0)

    hidden(1)

    ring = 2 + 6 * pk
    around = [(i, (s + ring * (lax.rem(quad + i, 4) - quad), c)) for i in (2, 1, 3)]
    partner = (s + 1 - 2 * pk, c)

    def piece(q):
        lanes = pl.ds(pl.multiple_of(lax.rem(q, 2) * LANES, LANES), LANES)
        return wbuf.at[:, :, 2 * pk + q // 2, :, lanes]

    p_mine = pbuf.at[:, quad]
    wait(p_mine, r1.at[0])
    for _, to in around:
        put(p_mine, p_mine, s1.at[4], r1.at[4], to)
    w_mine = piece(quad)
    wait(w_mine, r1.at[1])
    for i, to in around:
        put(w_mine, w_mine, s1.at[5], ring_sem.at[i - 1], to)
    put(w_mine, w_mine, s1.at[6], r1.at[6], partner)

    hidden(2)
    values = product(2, BLOCKS * OWN)
    lane = lax.broadcasted_iota(jnp.int32, (1, WIDE), 1)
    for b in range(BLOCKS):
        places = s * SPAN + b * WIDE + lane
        scaled = places.astype(F32) / (LENGTH - 1)
        window = jnp.exp(-(scaled * mine[:, DECAY : DECAY + 1]))
        block = values[b * OWN : (b + 1) * OWN] * window
        for q in range(2 * RADIX):
            kstage[:, 2 * b + q // RADIX, q % RADIX, :] = block[:, q * LANES : (q + 1) * LANES]
    ksnd[...] = kstage[...].astype(BF16)
    far = [(i, j, l) for i in (2, 1, 3, 0) for j in (2, 1, 3, 0) for l in (1, 0)]
    theirs = pl.ds(pl.multiple_of(s * CH, CH), CH)
    for i, j, l in far[:-1]:
        si = lax.rem(px + i, 4) * 8 + lax.rem(py + j, 4) * 2 + lax.rem(pk + l, 2)
        put(ksnd.at[si], krcv.at[theirs], s3.at[0], r3.at[0], (si, c))
    pltpu.make_async_copy(ksnd.at[s], krcv.at[theirs], r3.at[0]).start()

    def hand_over(i):
        got = piece(lax.rem(quad + 4 - i, 4))
        wait(got, ring_sem.at[i - 1])
        put(got, got, s1.at[6], r1.at[6], partner)

    hand_over(1)
    hand_over(3)
    for copy in consts:
        copy.wait()
    for i in range(6):
        at = 1 + i if i < 3 else 2 + i
        spins[i] = jnp.broadcast_to(spin_v[:, at : at + 1], (D, LANES))
    for h in range(RADIX):
        lanes = slice(h * LANES, (h + 1) * LANES)
        cs, sn = step_v[h : h + 1, :], step_v[RADIX + h : RADIX + h + 1, :]
        twid_v[0, :, lanes] = base_v[0] * cs - base_v[1] * sn
        twid_v[1, :, lanes] = base_v[1] * cs + base_v[0] * sn

    spots = [(i, j, l) for i in range(4) for j in range(4) for l in range(2)]
    spots.sort(key=lambda o: -(min(o[0], 4 - o[0]) + min(o[1], 4 - o[1])))
    spots = [o for o in spots if o != (0, 0, 0)] + [(0, 0, 0)]
    at_x = [lax.rem(px + i, 4) * 8 for i in range(4)]
    at_y = [lax.rem(py + i, 4) * 2 for i in range(4)]
    at_k = [lax.rem(pk + i, 2) for i in range(2)]

    hand_over(2)
    wait(pbuf.at[pl.ds(0, 6)], r1.at[4])
    pflat[...] = pbuf[...].reshape(D, LANES)
    for j in range(3):
        bias = jnp.broadcast_to(pflat[:, BIAS + j : BIAS + j + 1], (D, LANES))
        for i in range(3):
            at = TAPS + 3 * j + i
            tap = jnp.broadcast_to(pflat[:, at : at + 1], (D, LANES))
            cols[3 * j + i, 0] = tap
            cols[3 * j + i, 1] = tap * bias

    pl.semaphore_wait(gate, SEQ - 1)
    wait(xc.at[:, pl.ds(HALO, CHUNK)], r1.at[2])

    @pl.when(me > 0)
    def _():
        wait(xc.at[:, pl.ds(0, HALO)], r1.at[3])

    wait(wbuf.at[:, :, pl.ds(0, 2)], r1.at[6])

    wide = xc[...].astype(F32)
    for i in (0, 1):
        xs[i] = pltpu.roll(wide, 2 - i, 1)[:, HALO:].astype(BF16)
    place = lax.broadcasted_iota(jnp.int32, (1, LANES), 1)
    started = [jnp.logical_or(place >= 2 - i, me > 0).astype(F32) for i in (0, 1)]

    def gates(t, carry):
        pair = lax.rem(c // 2 + 2 + (t + 1) // 2 * (1 - 2 * lax.rem(t, 2)), 4)
        rows = pl.ds(pl.multiple_of(pair * 64, 64), 64)
        w = wbuf[:, pl.ds(pair * 2, 2)].astype(F32).reshape(3 * 64, D).astype(BF16)
        taken = [mm(w, xs[0]), mm(w, xs[1]), mm(w, xc[:, HALO:])]
        for r in range(RADIX):
            lanes = slice(r * LANES, (r + 1) * LANES)
            streams = []
            for j in range(3):
                total = None
                for i in range(3):
                    shifted_bias = cols[3 * j + i, 1, rows, :]
                    if r == 0 and i < 2:
                        shifted_bias = shifted_bias * started[i]
                    term = cols[3 * j + i, 0, rows, :] * taken[i][64 * j : 64 * j + 64, lanes]
                    term = term + shifted_bias
                    total = term if total is None else total + term
                streams.append(total)
            gated = streams[2] * streams[1]
            keep0[rows, lanes] = streams[0]
            keepg[rows, lanes] = gated
            stage[rows, r, :] = gated
        gsnd[rows] = stage[rows].astype(BF16)
        for i, j, l in spots:
            si = at_x[i] + at_y[j] + at_k[l]
            for e in range(2):
                cj = 2 * pair + e
                src, dst = gsnd.at[cj * SEQ + si], grcv.at[me]
                if (i, j, l) == (0, 0, 0):

                    @pl.when(cj != c)
                    def _():
                        put(src, dst, s3.at[1], r3.at[1], (si, cj))

                    @pl.when(cj == c)
                    def _():
                        pltpu.make_async_copy(src, dst, r3.at[1]).start()

                else:
                    put(src, dst, s3.at[1], r3.at[1], (si, cj))
        return carry

    lax.fori_loop(0, 4, gates, 0)

    def whole(rcv):
        stage[...] = rcv[...].astype(F32)
        x = jnp.concatenate([stage[:, r, :] for r in range(RADIX)], axis=1).astype(BF16)
        for part in range(2):
            sect[part] = mm(first_v[part * D : (part + 1) * D, :], x) + mm(
                first_v[(2 + part) * D : (3 + part) * D, :], x
            )

    def turned():
        def ahead(step, carry):
            rows = pl.ds(pl.multiple_of(step * 32, 32), 32)
            re, im = [], []
            for r in range(RADIX):
                lanes = slice(r * LANES, (r + 1) * LANES)
                a, b = sect[0, rows, lanes], sect[1, rows, lanes]
                if r:
                    cs, sn = spins[r - 1, rows, :], spins[r + 2, rows, :]
                    a, b = a * cs + b * sn, b * cs - a * sn
                re.append(a)
                im.append(b)
            e0r, e0i, e1r, e1i = re[0] + re[2], im[0] + im[2], re[0] - re[2], im[0] - im[2]
            o0r, o0i, o1r, o1i = re[1] + re[3], im[1] + im[3], re[1] - re[3], im[1] - im[3]
            outs = [
                (e0r + o0r, e0i + o0i),
                (e1r + o1i, e1i - o1r),
                (e0r - o0r, e0i - o0i),
                (e1r - o1i, e1i + o1r),
            ]
            for h, (a, b) in enumerate(outs):
                cs = twid_v[0, rows, h * LANES : (h + 1) * LANES]
                sn = twid_v[1, rows, h * LANES : (h + 1) * LANES]
                high, low = split(jnp.concatenate([a * cs + b * sn, b * cs - a * sn], axis=1))
                chi[h, rows, :] = high
                clo[h, rows, :] = low
            return carry

        lax.fori_loop(0, D // 32, ahead, 0)

    def spectrum(h):
        high, low = chi[h], clo[h]
        return mm(high, fwd_v[0]) + mm(low, fwd_v[0]) + mm(high, fwd_v[1])

    wait(krcv, r3.at[0])
    whole(krcv)
    turned()
    for h in range(RADIX):
        spec[h] = spectrum(h)
    wait(grcv, r3.at[1])
    whole(grcv)
    turned()
    for h in range(RADIX):
        g, k = spectrum(h), spec[h]
        gr, gi, kr, ki = g[:, :LANES], g[:, LANES:], k[:, :LANES], k[:, LANES:]
        high, low = split(jnp.concatenate([gr * kr - gi * ki, gr * ki + gi * kr], axis=1))
        z = mm(high, inv_v[0]) + mm(low, inv_v[0]) + mm(high, inv_v[1])
        zr, zi = z[:, :LANES], z[:, LANES:]
        cs = twid_v[0, :, h * LANES : (h + 1) * LANES]
        sn = twid_v[1, :, h * LANES : (h + 1) * LANES]
        back[h, 0] = zr * cs - zi * sn
        back[h, 1] = zi * cs + zr * sn

    def behind(step, carry):
        lo = pl.multiple_of(step * 32, 32)
        rows = pl.ds(lo, 32)
        rows_im = pl.ds(pl.multiple_of(D + lo, 32), 32)
        re = [back[h, 0, rows, :] for h in range(RADIX)]
        im = [back[h, 1, rows, :] for h in range(RADIX)]
        e0r, e0i, e1r, e1i = re[0] + re[2], im[0] + im[2], re[0] - re[2], im[0] - im[2]
        o0r, o0i, o1r, o1i = re[1] + re[3], im[1] + im[3], re[1] - re[3], im[1] - im[3]
        outs = [
            (e0r + o0r, e0i + o0i),
            (e1r - o1i, e1i + o1r),
            (e0r - o0r, e0i - o0i),
            (e1r + o1i, e1i - o1r),
        ]
        for r, (a, b) in enumerate(outs):
            if r:
                cs, sn = spins[r - 1, rows, :], spins[r + 2, rows, :]
                a, b = a * cs - b * sn, b * cs + a * sn
            lanes = slice(r * LANES, (r + 1) * LANES)
            high, low = split(a)
            dhi[rows, lanes] = high
            dlo[rows, lanes] = low
            high, low = split(b)
            dhi[rows_im, lanes] = high
            dlo[rows_im, lanes] = low
        return carry

    lax.fori_loop(0, D // 32, behind, 0)
    last_hi, last_lo = last_v[0:D, :], last_v[D : 2 * D, :]
    def settle(h, carry):
        lanes_h = pl.ds(pl.multiple_of(h * HALF, HALF), HALF)
        high, low = dhi[:, lanes_h], dlo[:, lanes_h]
        settled = mm(last_hi, high) + mm(last_lo, high) + mm(last_hi, low)
        for r in range(PAIR):
            stage2[:, r, :] = settled[:, r * LANES : (r + 1) * LANES]
        ysnd[h] = stage2[...].astype(BF16)
        to_row = c * SEQ + s
        for i, j, l in spots:
            si = at_x[i] + at_y[j] + at_k[l]
            for far in FAR + (0,):
                if (i, j, l, far) != (0, 0, 0, 0):
                    cj = lax.rem(c + far, CH)
                    put(
                        ysnd.at[h, si * CH + cj],
                        yrcv.at[h, to_row],
                        s3.at[3 + h],
                        r3.at[3 + h],
                        (si, cj),
                    )
        pltpu.make_async_copy(ysnd.at[h, me], yrcv.at[h, to_row], r3.at[3 + h]).start()
        return carry

    lax.fori_loop(0, 2, settle, 0)

    def mix(h):
        wait(yrcv.at[h], r3.at[3 + h])
        cols_h = slice(h * HALF, (h + 1) * HALF)
        stage2[...] = yrcv[h].astype(F32)
        convolved = jnp.concatenate([stage2[:, r, :] for r in range(PAIR)], axis=1)
        convolved = convolved + pflat[:, DIRECT : DIRECT + 1] * keepg[:, cols_h]
        mixed = (keep0[:, cols_h] * convolved).astype(BF16)
        osnd[h] = (mm(wout_v[...], mixed) + pflat[:, OUTB : OUTB + 1]).astype(BF16)
        o_dst = out_ref.at[:, pl.ds(pl.multiple_of(c * CHUNK + h * HALF, HALF), HALF)]
        for i in FAR:
            j = lax.rem(c + i, CH)
            put(
                osnd.at[h, pl.ds(pl.multiple_of(j * OWN, OWN), OWN), :],
                o_dst,
                s6.at[h],
                r6.at[h],
                (s, j),
            )
        pltpu.make_async_copy(osnd.at[h, rows_own, :], o_dst, r6.at[h]).start()

    mix(0)
    mix(1)

    for h in range(2):
        wait(out_ref.at[:, pl.ds(0, SPAN // 2)], r6.at[h])
    most = pl.ds(0, CH - 1)
    wait(pbuf.at[most, 0], s1.at[0])
    wait(wbuf.at[:, most, 0, :, pl.ds(0, LANES)], s1.at[1])
    wait(wbuf.at[:, pl.ds(0, 6), pl.ds(0, 2)], s1.at[5])
    wait(wbuf.at[:, :, pl.ds(0, 2)], s1.at[6])
    wait(xc.at[pl.ds(0, D - OWN), pl.ds(HALO, CHUNK)], s1.at[2])
    tails = pl.ds(0, OWN)
    wait(xc.at[pl.ds(0, 6 * OWN), pl.ds(0, HALO)], s1.at[3])

    @pl.when(c == 0)
    def _():
        wait(xc.at[tails, pl.ds(0, HALO)], s1.at[3])

    @pl.when(s < SEQ - 1)
    def _():
        wait(xc.at[tails, pl.ds(0, HALO)], s1.at[3])

    wait(pbuf.at[pl.ds(0, 6)], s1.at[4])
    wait(ksnd.at[pl.ds(0, SEQ - 1)], s3.at[0])
    wait(gsnd.at[pl.ds(0, DEV - 1)], s3.at[1])
    for h in range(2):
        wait(ysnd.at[h, pl.ds(0, DEV - 1)], s3.at[3 + h])
        wait(osnd.at[h, pl.ds(0, D - OWN), :], s6.at[h])


def body(
    inputs,
    w_in,
    b_in,
    short_kernel,
    positional,
    filter_in,
    filter_bias,
    filter_freq,
    filter_hidden,
    filter_out,
    decay,
    conv_bias,
    w_out,
    b_out,
):
    dma = pltpu.SemaphoreType.DMA
    hbm = pl.BlockSpec(memory_space=pl.ANY)
    vmem = pltpu.VMEM
    return pl.pallas_call(
        kernel,
        out_shape=pltpu.VMEM((OWN, SPAN), BF16),
        in_specs=[hbm] * 21,
        out_specs=pl.BlockSpec(memory_space=pltpu.VMEM),
        scratch_shapes=[
            vmem((3, OWN), F32),
            vmem((3, 3, OWN), F32),
            vmem((OWN, ORDER), F32),
            vmem((1, OWN), F32),
            vmem((1, OWN), F32),
            vmem((1, OWN), F32),
            vmem((5, SPAN), F32),
            vmem((5, ORDER), F32),
            vmem((3, ORDER), F32),
            vmem((3, ORDER), F32),
            vmem((2, ORDER, ORDER), F32),
            vmem((D, D), BF16),
            vmem((16, OWN), F32),
            vmem((16, ORDER), F32),
            vmem((OWN, LANES), F32),
            vmem((D, HALO + CHUNK), BF16),
            vmem((3, CH, 4, 8, D), BF16),
            vmem((CH, 4, 8, LANES), F32),
            vmem((D, LANES), F32),
            vmem((2, D, CHUNK), BF16),
            vmem((9, 2, D, LANES), F32),
            vmem((6, D, LANES), F32),
            vmem((DEV, RADIX, LANES), F32),
            vmem((DEV, PAIR, LANES), F32),
            vmem((D, CHUNK), F32),
            vmem((D, CHUNK), F32),
            vmem((3, D, D), F32),
            vmem((3, 2 * D, D), BF16),
            vmem((2, D, WIDE), BF16),
            vmem((D, WIDE), F32),
            vmem((OWN, CH, RADIX, LANES), F32),
            vmem((OWN, CH, RADIX, LANES), BF16),
            vmem((DEV, RADIX, LANES), BF16),
            vmem((DEV, RADIX, LANES), BF16),
            vmem((DEV, RADIX, LANES), BF16),
            vmem((4 * D, D), BF16),
            vmem((2 * D, 2 * D), BF16),
            vmem((2, D, D), BF16),
            vmem((2, D, D), BF16),
            vmem((2, D, LANES), F32),
            vmem((2 * RADIX, LANES), F32),
            vmem((D, LANES), F32),
            vmem((2, D, CHUNK), F32),
            vmem((2, D, CHUNK), F32),
            vmem((RADIX, D, 2 * LANES), BF16),
            vmem((RADIX, D, 2 * LANES), BF16),
            vmem((RADIX, D, 2 * LANES), F32),
            vmem((RADIX, 2, D, LANES), F32),
            vmem((2 * D, CHUNK), BF16),
            vmem((2 * D, CHUNK), BF16),
            vmem((2, DEV, PAIR, LANES), BF16),
            vmem((2, DEV, PAIR, LANES), BF16),
            vmem((2, D, HALF), BF16),
            dma((12,)),
            dma((7,)),
            dma((3,)),
            pltpu.SemaphoreType.REGULAR,
            dma((8,)),
            dma((8,)),
            dma((5,)),
            dma((5,)),
            dma((2,)),
            dma((2,)),
        ],
        compiler_params=pltpu.CompilerParams(collective_id=0, has_side_effects=True),
    )(
        inputs,
        w_in,
        b_in,
        short_kernel.transpose(0, 2, 1),
        filter_out,
        decay.reshape(1, OWN),
        conv_bias.reshape(1, OWN),
        b_out.reshape(1, OWN),
        positional,
        filter_in.T,
        filter_bias,
        filter_freq,
        filter_hidden,
        w_out,
        *tables(),
    )


def solution(mesh):
    in_specs = (
        P("ch", "seq"),
        P(None, "ch", None),
        P(None, "ch"),
        P(None, "ch", None),
        P(None, "seq"),
        P(),
        P(),
        P(),
        P(),
        P("ch", None),
        P("ch"),
        P("ch"),
        P(),
        P("ch"),
    )
    return jax.shard_map(
        body, mesh=mesh, in_specs=in_specs, out_specs=P("ch", "seq"), check_vma=False
    )
```

```python
import math

import jax
import jax.numpy as jnp
import numpy as np
from jax import lax
from jax.experimental import pallas as pl
from jax.experimental.pallas import tpu as pltpu
from jax.sharding import PartitionSpec as P

MESH = pl.DeviceIdType.MESH
F32 = jnp.float32
BF16 = jnp.bfloat16
HIGHEST = lax.Precision.HIGHEST

SEQ, CH = 32, 8
DEV = SEQ * CH
D = 256
OWN = D // CH
SPAN = 4096
CHUNK = SPAN // CH
LENGTH = SPAN * SEQ
HALO = 128
LANES = 128
RADIX = CHUNK // LANES
ORDER = 64
HALF = CHUNK // 2
PAIR = RADIX // 2
FAR = (4, 3, 5, 2, 6, 1, 7)
BIAS, TAPS, DECAY, DIRECT, OUTB = 0, 3, 12, 13, 14
BLOCKS, WIDE = 4, 1024
PI_HIGH, PI_LOW = 3.1414794921875, 0.00011315941810607910156


def halves(table):
    high = np.asarray(table, np.float64).astype(jnp.bfloat16)
    low = (np.asarray(table, np.float64) - high.astype(np.float64)).astype(jnp.bfloat16)
    return high, low


def tables():
    rows = np.arange(D)
    f1 = np.arange(D) + 0.25
    angle = 2.0 * np.pi * ((np.outer(4 * f1, rows) % (4 * D)) / (4 * D))
    first = np.concatenate([np.cos(angle), -np.sin(angle)], axis=0)
    first_stack = np.concatenate(halves(first), axis=0)
    last_stack = np.concatenate(halves(first.T / LENGTH), axis=0)
    lanes = np.arange(LANES)
    inner = 2.0 * np.pi * (np.outer(lanes, lanes) % LANES) / LANES
    c, s = np.cos(inner), np.sin(inner)
    forward = np.stack(halves(np.block([[c, -s], [s, c]])))
    inverse = np.stack(halves(np.block([[c, s], [-s, c]])))
    turn = 2.0 * np.pi / LENGTH * f1[:, None] * lanes[None, :]
    step = 2.0 * np.pi / CHUNK * np.arange(RADIX)[:, None] * lanes[None, :]
    twiddle = np.stack([np.cos(turn), np.sin(turn)]).astype(np.float32)
    steps = np.concatenate([np.cos(step), np.sin(step)]).astype(np.float32)
    spin = 2.0 * np.pi / (RADIX * D) * f1[:, None] * np.arange(RADIX)[None, :]
    spins = np.zeros((D, LANES), np.float32)
    spins[:, 0:RADIX] = np.cos(spin)
    spins[:, RADIX : 2 * RADIX] = np.sin(spin)
    return first_stack, last_stack, forward, inverse, twiddle, steps, spins


def split(x):
    high = x.astype(BF16)
    return high, (x - high.astype(F32)).astype(BF16)


def sine(v):
    turns = jnp.floor(v * (1.0 / math.pi) + 0.5)
    rest = (v - turns * PI_HIGH) - turns * PI_LOW
    half = turns * 0.5
    rest = rest * (1.0 - 4.0 * (half - jnp.floor(half)))
    square = rest * rest
    poly = 2.6083159809786593541503e-06 * square - 0.0001981069071916863322258
    poly = poly * square + 0.00833307858556509017944336
    poly = poly * square - 0.166666597127914428710938
    return rest + rest * (square * poly)


def mm(a, b):
    return jnp.dot(a, b, preferred_element_type=F32)


def kernel(
    x_ref,
    w_ref,
    bin_ref,
    taps_ref,
    fout_ref,
    decay_ref,
    direct_ref,
    bout_ref,
    pos_ref,
    fin_ref,
    fbias_ref,
    ffreq_ref,
    fhid_ref,
    wout_ref,
    first_ref,
    last_ref,
    fwd_ref,
    inv_ref,
    twid_ref,
    step_ref,
    spin_ref,
    out_ref,
    bin_v,
    taps_v,
    fout_v,
    decay_v,
    direct_v,
    bout_v,
    pos_v,
    fin_v,
    fbias_v,
    ffreq_v,
    fhid_v,
    wout_v,
    raw,
    rawnet,
    prm,
    psend,
    xc,
    wbuf,
    pbuf,
    pflat,
    xs,
    cols,
    spins,
    stage,
    stage2,
    keep0,
    keepg,
    diag,
    weight,
    act,
    value_v,
    kstage,
    ksnd,
    krcv,
    gsnd,
    grcv,
    first_v,
    last_v,
    fwd_v,
    inv_v,
    base_v,
    step_v,
    spin_v,
    twid_v,
    sect,
    chi,
    clo,
    spec,
    back,
    dhi,
    dlo,
    ysnd,
    yrcv,
    osnd,
    small_sem,
    const_sem,
    ring_sem,
    gate,
    s1,
    r1,
    s3,
    r3,
    s6,
    r6,
):
    s = lax.axis_index("seq")
    c = lax.axis_index("ch")
    me = s * CH + c
    px, py, pk = s // 8, lax.rem(s // 2, 4), lax.rem(s, 2)
    quad = py + pk * (px - py)
    own = pl.multiple_of(c * OWN, OWN)
    rows_own = pl.ds(own, OWN)

    smalls = [
        pltpu.make_async_copy(src, dst, small_sem.at[i])
        for i, (src, dst) in enumerate(
            [
                (bin_ref, bin_v),
                (taps_ref, taps_v),
                (fout_ref, fout_v),
                (decay_ref, decay_v),
                (direct_ref, direct_v),
                (bout_ref, bout_v),
                (pos_ref, pos_v),
                (fin_ref, fin_v),
                (fbias_ref, fbias_v),
                (ffreq_ref, ffreq_v),
                (fhid_ref, fhid_v),
                (wout_ref, wout_v),
            ]
        )
    ]
    consts = [
        pltpu.make_async_copy(src, dst, const_sem.at[i])
        for i, (src, dst) in enumerate(
            [
                (spin_ref, spin_v),
                (first_ref, first_v),
                (twid_ref, base_v),
                (step_ref, step_v),
                (fwd_ref, fwd_v),
                (inv_ref, inv_v),
                (last_ref, last_v),
            ]
        )
    ]
    for copy in smalls:
        copy.start()

    bar = pltpu.get_barrier_semaphore()

    def greet(sem, to):
        pl.semaphore_signal(sem, inc=1, device_id=to, device_id_type=MESH)

    for i in range(1, CH):
        greet(bar, (s, lax.rem(c + i, CH)))
    for i in range(1, SEQ):
        greet(bar, (lax.rem(s + i, SEQ), c))

    @pl.when(jnp.logical_and(c == 0, s > 0))
    def _():
        for j in range(CH):
            greet(bar, (s - 1, j))

    for i in (0, 1, 3, 4, 5):
        smalls[i].wait()
    raw[...] = jnp.zeros_like(raw)
    raw[0:3, :] = bin_v[...]
    for j in range(3):
        raw[3 + 3 * j : 6 + 3 * j, :] = taps_v[j]
    raw[12:13, :] = decay_v[...]
    raw[13:14, :] = direct_v[...]
    raw[14:15, :] = bout_v[...]

    def columns(rows, n):
        eye = (
            lax.broadcasted_iota(jnp.int32, (n, n), 0) == lax.broadcasted_iota(jnp.int32, (n, n), 1)
        ).astype(F32)
        return lax.dot_general(
            eye, rows, (((1,), (1,)), ((), ())), precision=HIGHEST, preferred_element_type=F32
        )

    prm[...] = jnp.zeros_like(prm)
    mine = columns(raw[...], OWN)
    left = mine
    for i in range(3):
        part = left.astype(BF16)
        prm[:, 16 * i : 16 * i + 16] = part.astype(F32)
        left = left - part.astype(F32)
    psend[...] = prm[...].reshape(4, 8, LANES).astype(BF16)
    pl.semaphore_wait(bar, jnp.where(s < SEQ - 1, SEQ + CH - 1, SEQ + CH - 2))

    def put(src, dst, send, recv, to):
        pltpu.make_async_remote_copy(
            src_ref=src, dst_ref=dst, send_sem=send, recv_sem=recv, device_id=to, device_id_type=MESH
        ).start()

    def wait(ref, sem):
        pltpu.make_async_copy(ref, ref, sem).wait()

    half = pl.ds(pl.multiple_of(lax.rem(quad, 2) * LANES, LANES), LANES)
    octet = 2 * pk + quad // 2
    w_src = w_ref.at[:, pl.ds(pl.multiple_of(octet * 8, 8), 8), half]
    w_dst = wbuf.at[:, c, octet, :, half]
    p_src = psend.at[quad]
    p_dst = pbuf.at[c, quad]
    x_dst = xc.at[rows_own, pl.ds(HALO, CHUNK)]
    h_dst = xc.at[rows_own, pl.ds(0, HALO)]

    def chunk(j):
        return x_ref.at[:, pl.ds(pl.multiple_of(j * CHUNK, CHUNK), CHUNK)]

    def tail(j):
        return x_ref.at[:, pl.ds(pl.multiple_of(j * CHUNK + CHUNK - HALO, HALO), HALO)]

    for i in FAR:
        put(p_src, p_dst, s1.at[0], r1.at[0], (s, lax.rem(c + i, CH)))
    for i in FAR:
        put(w_src, w_dst, s1.at[1], r1.at[1], (s, lax.rem(c + i, CH)))

    @pl.when(s < SEQ - 1)
    def _():
        put(tail(CH - 1), h_dst, s1.at[3], r1.at[3], (s + 1, 0))

    for i in FAR:
        j = lax.rem(c + i, CH)
        put(chunk(j), x_dst, s1.at[2], r1.at[2], (s, j))

        @pl.when(j > 0)
        def _():
            put(tail(j - 1), h_dst, s1.at[3], r1.at[3], (s, j))


    pltpu.make_async_copy(p_src, p_dst, r1.at[0]).start()
    pltpu.make_async_copy(w_src, w_dst, r1.at[1]).start()
    pltpu.make_async_copy(chunk(c), x_dst, r1.at[2]).start()

    @pl.when(c > 0)
    def _():
        pltpu.make_async_copy(tail(c - 1), h_dst, r1.at[3]).start()

    @pl.when(me == 0)
    def _():
        xc[:, 0:HALO] = jnp.zeros((D, HALO), BF16)

    for i in range(1, SEQ):
        greet(gate, (lax.rem(s + i, SEQ), c))
    for copy in consts:
        copy.start()
    for i in (2, 6, 7, 8, 9, 10, 11):
        smalls[i].wait()

    rawnet[...] = jnp.zeros_like(rawnet)
    rawnet[0:5, :] = fin_v[...]
    rawnet[5:8, :] = fbias_v[...]
    rawnet[8:11, :] = ffreq_v[...]
    net = columns(rawnet[...], ORDER)
    diag[...] = jnp.zeros_like(diag)
    for b in range(BLOCKS):
        at = slice(b * ORDER, (b + 1) * ORDER)
        diag[0, at, at] = fhid_v[0]
        diag[1, at, at] = fhid_v[1]
        diag[2, b * OWN : (b + 1) * OWN, at] = fout_v[...]
    for i in range(3):
        high, low = split(diag[i])
        weight[i, 0:D] = high
        weight[i, D : 2 * D] = low

    def tile(step):
        b, side = step // 2, lax.rem(step, 2)
        rows = pl.ds(pl.multiple_of(b * ORDER, ORDER), ORDER)
        return b, side, rows, pl.ds(pl.multiple_of(side * CHUNK, CHUNK), CHUNK)

    def keep(layer, value, rows, lanes):
        high, low = split(
            sine(net[:, 8 + layer : 9 + layer] * (value + net[:, 5 + layer : 6 + layer]))
        )
        act[0, rows, lanes] = high
        act[1, rows, lanes] = low

    def enter(step, carry):
        b, side, rows, lanes = tile(step)
        here = pl.ds(pl.multiple_of(step * CHUNK, CHUNK), CHUNK)
        value = net[:, 0:1] * pos_v[0:1, here]
        for i in range(1, 5):
            value = value + net[:, i : i + 1] * pos_v[i : i + 1, here]
        keep(0, value, rows, lanes)
        return carry

    lax.fori_loop(0, 2 * BLOCKS, enter, 0)

    def product(i, n):
        both, one = weight[i, 0 : D + n], weight[i, 0:n]
        wide = mm(both, act[0])
        return wide[0:n] + wide[D : D + n] + mm(one, act[1])

    def hidden(layer):
        value_v[...] = product(layer - 1, D)

        def leave(step, carry):
            b, side, rows, lanes = tile(step)
            keep(layer, value_v[rows, lanes], rows, lanes)
            return carry

        lax.fori_loop(0, 2 * BLOCKS, leave, 0)

    hidden(1)

    ring = 2 + 6 * pk
    around = [(i, (s + ring * (lax.rem(quad + i, 4) - quad), c)) for i in (2, 1, 3)]
    partner = (s + 1 - 2 * pk, c)

    def piece(q):
        lanes = pl.ds(pl.multiple_of(lax.rem(q, 2) * LANES, LANES), LANES)
        return wbuf.at[:, :, 2 * pk + q // 2, :, lanes]

    p_mine = pbuf.at[:, quad]
    wait(p_mine, r1.at[0])
    for _, to in around:
        put(p_mine, p_mine, s1.at[4], r1.at[4], to)
    w_mine = piece(quad)
    wait(w_mine, r1.at[1])
    for i, to in around:
        put(w_mine, w_mine, s1.at[5], ring_sem.at[i - 1], to)
    put(w_mine, w_mine, s1.at[6], r1.at[6], partner)

    hidden(2)
    values = product(2, BLOCKS * OWN)
    lane = lax.broadcasted_iota(jnp.int32, (1, WIDE), 1)
    for b in range(BLOCKS):
        places = s * SPAN + b * WIDE + lane
        scaled = places.astype(F32) / (LENGTH - 1)
        window = jnp.exp(-(scaled * mine[:, DECAY : DECAY + 1]))
        block = values[b * OWN : (b + 1) * OWN] * window
        for q in range(2 * RADIX):
            kstage[:, 2 * b + q // RADIX, q % RADIX, :] = block[:, q * LANES : (q + 1) * LANES]
    ksnd[...] = kstage[...].astype(BF16)
    far = [(i, j, l) for i in (2, 1, 3, 0) for j in (2, 1, 3, 0) for l in (1, 0)]
    theirs = pl.ds(pl.multiple_of(s * CH, CH), CH)
    for i, j, l in far[:-1]:
        si = lax.rem(px + i, 4) * 8 + lax.rem(py + j, 4) * 2 + lax.rem(pk + l, 2)
        put(ksnd.at[si], krcv.at[theirs], s3.at[0], r3.at[0], (si, c))
    pltpu.make_async_copy(ksnd.at[s], krcv.at[theirs], r3.at[0]).start()

    def hand_over(i):
        got = piece(lax.rem(quad + 4 - i, 4))
        wait(got, ring_sem.at[i - 1])
        put(got, got, s1.at[6], r1.at[6], partner)

    hand_over(1)
    hand_over(3)
    spots = [(i, j, l) for i in range(4) for j in range(4) for l in range(2)]
    spots.sort(key=lambda o: -(min(o[0], 4 - o[0]) + min(o[1], 4 - o[1])))
    spots = [o for o in spots if o != (0, 0, 0)] + [(0, 0, 0)]
    at_x = [lax.rem(px + i, 4) * 8 for i in range(4)]
    at_y = [lax.rem(py + i, 4) * 2 for i in range(4)]
    at_k = [lax.rem(pk + i, 2) for i in range(2)]

    hand_over(2)
    wait(pbuf.at[pl.ds(0, 6)], r1.at[4])
    arrived = pbuf[...].astype(F32).reshape(D, LANES)
    pflat[...] = arrived + (
        pltpu.roll(arrived, LANES - 16, 1) + pltpu.roll(arrived, LANES - 32, 1)
    )
    for j in range(3):
        bias = jnp.broadcast_to(pflat[:, BIAS + j : BIAS + j + 1], (D, LANES))
        total = None
        for i in range(3):
            at = TAPS + 3 * j + i
            tap = jnp.broadcast_to(pflat[:, at : at + 1], (D, LANES))
            cols[3 * j + i] = tap
            total = tap * bias if total is None else total + tap * bias
            if i < 2:
                cols[9 + 3 * j + i] = tap * bias
            else:
                cols[11 + 3 * j] = total
                cols[18 + j] = tap * bias

    pl.semaphore_wait(gate, SEQ - 1)
    wait(xc.at[:, pl.ds(HALO, CHUNK)], r1.at[2])

    @pl.when(me > 0)
    def _():
        wait(xc.at[:, pl.ds(0, HALO)], r1.at[3])

    wait(wbuf.at[:, :, pl.ds(0, 2)], r1.at[6])

    wide = xc[...].astype(F32)
    for i in (0, 1):
        xs[i] = pltpu.roll(wide, 2 - i, 1)[:, HALO:].astype(BF16)
    place = lax.broadcasted_iota(jnp.int32, (1, LANES), 1)
    started = [jnp.logical_or(place >= 2 - i, me > 0).astype(F32) for i in (0, 1)]

    def gates(t, carry):
        pair = lax.rem(c // 2 + 2 + (t + 1) // 2 * (1 - 2 * lax.rem(t, 2)), 4)
        rows = pl.ds(pl.multiple_of(pair * 64, 64), 64)
        w = wbuf[:, pl.ds(pair * 2, 2)].astype(F32).reshape(3 * 64, D).astype(BF16)
        taken = [mm(w, xs[0]), mm(w, xs[1]), mm(w, xc[:, HALO:])]
        for r in range(RADIX):
            lanes = slice(r * LANES, (r + 1) * LANES)
            streams = []
            for j in range(3):
                if r:
                    total = cols[11 + 3 * j, rows, :]
                else:
                    total = cols[18 + j, rows, :]
                    for i in range(2):
                        total = total + cols[9 + 3 * j + i, rows, :] * started[i]
                for i in range(3):
                    part = taken[i][64 * j : 64 * j + 64, lanes]
                    total = total + cols[3 * j + i, rows, :] * part
                streams.append(total)
            gated = streams[2] * streams[1]
            keep0[rows, lanes] = streams[0]
            keepg[rows, lanes] = gated
            stage[rows, r, :] = gated
        gsnd[rows] = stage[rows].astype(BF16)
        for i, j, l in spots:
            si = at_x[i] + at_y[j] + at_k[l]
            for e in range(2):
                cj = 2 * pair + e
                src, dst = gsnd.at[cj * SEQ + si], grcv.at[me]
                if (i, j, l) == (0, 0, 0):

                    @pl.when(cj != c)
                    def _():
                        put(src, dst, s3.at[1], r3.at[1], (si, cj))

                    @pl.when(cj == c)
                    def _():
                        pltpu.make_async_copy(src, dst, r3.at[1]).start()

                else:
                    put(src, dst, s3.at[1], r3.at[1], (si, cj))
        return carry

    lax.fori_loop(0, 4, gates, 0)

    for copy in consts:
        copy.wait()
    for i in range(6):
        at = 1 + i if i < 3 else 2 + i
        spins[i] = jnp.broadcast_to(spin_v[:, at : at + 1], (D, LANES))
    for h in range(RADIX):
        lanes = slice(h * LANES, (h + 1) * LANES)
        cs, sn = step_v[h : h + 1, :], step_v[RADIX + h : RADIX + h + 1, :]
        twid_v[0, :, lanes] = base_v[0] * cs - base_v[1] * sn
        twid_v[1, :, lanes] = base_v[1] * cs + base_v[0] * sn


    def whole(rcv):
        stage[...] = rcv[...].astype(F32)
        x = jnp.concatenate([stage[:, r, :] for r in range(RADIX)], axis=1).astype(BF16)
        for part in range(2):
            sect[part] = mm(first_v[part * D : (part + 1) * D, :], x) + mm(
                first_v[(2 + part) * D : (3 + part) * D, :], x
            )

    def turned():
        def ahead(step, carry):
            rows = pl.ds(pl.multiple_of(step * 32, 32), 32)
            re, im = [], []
            for r in range(RADIX):
                lanes = slice(r * LANES, (r + 1) * LANES)
                a, b = sect[0, rows, lanes], sect[1, rows, lanes]
                if r:
                    cs, sn = spins[r - 1, rows, :], spins[r + 2, rows, :]
                    a, b = a * cs + b * sn, b * cs - a * sn
                re.append(a)
                im.append(b)
            e0r, e0i, e1r, e1i = re[0] + re[2], im[0] + im[2], re[0] - re[2], im[0] - im[2]
            o0r, o0i, o1r, o1i = re[1] + re[3], im[1] + im[3], re[1] - re[3], im[1] - im[3]
            outs = [
                (e0r + o0r, e0i + o0i),
                (e1r + o1i, e1i - o1r),
                (e0r - o0r, e0i - o0i),
                (e1r - o1i, e1i + o1r),
            ]
            for h, (a, b) in enumerate(outs):
                cs = twid_v[0, rows, h * LANES : (h + 1) * LANES]
                sn = twid_v[1, rows, h * LANES : (h + 1) * LANES]
                high, low = split(jnp.concatenate([a * cs + b * sn, b * cs - a * sn], axis=1))
                chi[h, rows, :] = high
                clo[h, rows, :] = low
            return carry

        lax.fori_loop(0, D // 32, ahead, 0)

    def spectrum(h):
        high, low = chi[h], clo[h]
        return mm(high, fwd_v[0]) + mm(low, fwd_v[0]) + mm(high, fwd_v[1])

    wait(krcv, r3.at[0])
    whole(krcv)
    turned()
    for h in range(RADIX):
        spec[h] = spectrum(h)
    wait(grcv, r3.at[1])
    whole(grcv)
    turned()
    for h in range(RADIX):
        g, k = spectrum(h), spec[h]
        gr, gi, kr, ki = g[:, :LANES], g[:, LANES:], k[:, :LANES], k[:, LANES:]
        high, low = split(jnp.concatenate([gr * kr - gi * ki, gr * ki + gi * kr], axis=1))
        z = mm(high, inv_v[0]) + mm(low, inv_v[0]) + mm(high, inv_v[1])
        zr, zi = z[:, :LANES], z[:, LANES:]
        cs = twid_v[0, :, h * LANES : (h + 1) * LANES]
        sn = twid_v[1, :, h * LANES : (h + 1) * LANES]
        back[h, 0] = zr * cs - zi * sn
        back[h, 1] = zi * cs + zr * sn

    def behind(step, carry):
        lo = pl.multiple_of(step * 32, 32)
        rows = pl.ds(lo, 32)
        rows_im = pl.ds(pl.multiple_of(D + lo, 32), 32)
        re = [back[h, 0, rows, :] for h in range(RADIX)]
        im = [back[h, 1, rows, :] for h in range(RADIX)]
        e0r, e0i, e1r, e1i = re[0] + re[2], im[0] + im[2], re[0] - re[2], im[0] - im[2]
        o0r, o0i, o1r, o1i = re[1] + re[3], im[1] + im[3], re[1] - re[3], im[1] - im[3]
        outs = [
            (e0r + o0r, e0i + o0i),
            (e1r - o1i, e1i + o1r),
            (e0r - o0r, e0i - o0i),
            (e1r + o1i, e1i - o1r),
        ]
        for r, (a, b) in enumerate(outs):
            if r:
                cs, sn = spins[r - 1, rows, :], spins[r + 2, rows, :]
                a, b = a * cs - b * sn, b * cs + a * sn
            lanes = slice(r * LANES, (r + 1) * LANES)
            high, low = split(a)
            dhi[rows, lanes] = high
            dlo[rows, lanes] = low
            high, low = split(b)
            dhi[rows_im, lanes] = high
            dlo[rows_im, lanes] = low
        return carry

    lax.fori_loop(0, D // 32, behind, 0)
    last_hi, last_lo = last_v[0:D, :], last_v[D : 2 * D, :]
    def settle(h, carry):
        lanes_h = pl.ds(pl.multiple_of(h * HALF, HALF), HALF)
        high, low = dhi[:, lanes_h], dlo[:, lanes_h]
        settled = mm(last_hi, high) + mm(last_lo, high) + mm(last_hi, low)
        for r in range(PAIR):
            stage2[:, r, :] = settled[:, r * LANES : (r + 1) * LANES]
        ysnd[h] = stage2[...].astype(BF16)
        to_row = c * SEQ + s
        for i, j, l in spots:
            si = at_x[i] + at_y[j] + at_k[l]
            for far in FAR + (0,):
                if (i, j, l, far) != (0, 0, 0, 0):
                    cj = lax.rem(c + far, CH)
                    put(
                        ysnd.at[h, si * CH + cj],
                        yrcv.at[h, to_row],
                        s3.at[3 + h],
                        r3.at[3 + h],
                        (si, cj),
                    )
        pltpu.make_async_copy(ysnd.at[h, me], yrcv.at[h, to_row], r3.at[3 + h]).start()
        return carry

    lax.fori_loop(0, 2, settle, 0)

    def mix(h):
        wait(yrcv.at[h], r3.at[3 + h])
        cols_h = slice(h * HALF, (h + 1) * HALF)
        stage2[...] = yrcv[h].astype(F32)
        convolved = jnp.concatenate([stage2[:, r, :] for r in range(PAIR)], axis=1)
        convolved = convolved + pflat[:, DIRECT : DIRECT + 1] * keepg[:, cols_h]
        mixed = (keep0[:, cols_h] * convolved).astype(BF16)
        osnd[h] = (mm(wout_v[...], mixed) + pflat[:, OUTB : OUTB + 1]).astype(BF16)
        o_dst = out_ref.at[:, pl.ds(pl.multiple_of(c * CHUNK + h * HALF, HALF), HALF)]
        for i in FAR:
            j = lax.rem(c + i, CH)
            put(
                osnd.at[h, pl.ds(pl.multiple_of(j * OWN, OWN), OWN), :],
                o_dst,
                s6.at[h],
                r6.at[h],
                (s, j),
            )
        pltpu.make_async_copy(osnd.at[h, rows_own, :], o_dst, r6.at[h]).start()

    mix(0)
    mix(1)

    for h in range(2):
        wait(out_ref.at[:, pl.ds(0, SPAN // 2)], r6.at[h])
    most = pl.ds(0, CH - 1)
    wait(pbuf.at[most, 0], s1.at[0])
    wait(wbuf.at[:, most, 0, :, pl.ds(0, LANES)], s1.at[1])
    wait(wbuf.at[:, pl.ds(0, 6), pl.ds(0, 2)], s1.at[5])
    wait(wbuf.at[:, :, pl.ds(0, 2)], s1.at[6])
    wait(xc.at[pl.ds(0, D - OWN), pl.ds(HALO, CHUNK)], s1.at[2])
    tails = pl.ds(0, OWN)
    wait(xc.at[pl.ds(0, 6 * OWN), pl.ds(0, HALO)], s1.at[3])

    @pl.when(c == 0)
    def _():
        wait(xc.at[tails, pl.ds(0, HALO)], s1.at[3])

    @pl.when(s < SEQ - 1)
    def _():
        wait(xc.at[tails, pl.ds(0, HALO)], s1.at[3])

    wait(pbuf.at[pl.ds(0, 6)], s1.at[4])
    wait(ksnd.at[pl.ds(0, SEQ - 1)], s3.at[0])
    wait(gsnd.at[pl.ds(0, DEV - 1)], s3.at[1])
    for h in range(2):
        wait(ysnd.at[h, pl.ds(0, DEV - 1)], s3.at[3 + h])
        wait(osnd.at[h, pl.ds(0, D - OWN), :], s6.at[h])


def body(
    inputs,
    w_in,
    b_in,
    short_kernel,
    positional,
    filter_in,
    filter_bias,
    filter_freq,
    filter_hidden,
    filter_out,
    decay,
    conv_bias,
    w_out,
    b_out,
):
    dma = pltpu.SemaphoreType.DMA
    hbm = pl.BlockSpec(memory_space=pl.ANY)
    vmem = pltpu.VMEM
    return pl.pallas_call(
        kernel,
        out_shape=pltpu.VMEM((OWN, SPAN), BF16),
        in_specs=[hbm] * 21,
        out_specs=pl.BlockSpec(memory_space=pltpu.VMEM),
        scratch_shapes=[
            vmem((3, OWN), F32),
            vmem((3, 3, OWN), F32),
            vmem((OWN, ORDER), F32),
            vmem((1, OWN), F32),
            vmem((1, OWN), F32),
            vmem((1, OWN), F32),
            vmem((5, SPAN), F32),
            vmem((5, ORDER), F32),
            vmem((3, ORDER), F32),
            vmem((3, ORDER), F32),
            vmem((2, ORDER, ORDER), F32),
            vmem((D, D), BF16),
            vmem((16, OWN), F32),
            vmem((16, ORDER), F32),
            vmem((OWN, LANES), F32),
            vmem((4, 8, LANES), BF16),
            vmem((D, HALO + CHUNK), BF16),
            vmem((3, CH, 4, 8, D), BF16),
            vmem((CH, 4, 8, LANES), BF16),
            vmem((D, LANES), F32),
            vmem((2, D, CHUNK), BF16),
            vmem((21, D, LANES), F32),
            vmem((6, D, LANES), F32),
            vmem((DEV, RADIX, LANES), F32),
            vmem((DEV, PAIR, LANES), F32),
            vmem((D, CHUNK), F32),
            vmem((D, CHUNK), F32),
            vmem((3, D, D), F32),
            vmem((3, 2 * D, D), BF16),
            vmem((2, D, WIDE), BF16),
            vmem((D, WIDE), F32),
            vmem((OWN, CH, RADIX, LANES), F32),
            vmem((OWN, CH, RADIX, LANES), BF16),
            vmem((DEV, RADIX, LANES), BF16),
            vmem((DEV, RADIX, LANES), BF16),
            vmem((DEV, RADIX, LANES), BF16),
            vmem((4 * D, D), BF16),
            vmem((2 * D, 2 * D), BF16),
            vmem((2, D, D), BF16),
            vmem((2, D, D), BF16),
            vmem((2, D, LANES), F32),
            vmem((2 * RADIX, LANES), F32),
            vmem((D, LANES), F32),
            vmem((2, D, CHUNK), F32),
            vmem((2, D, CHUNK), F32),
            vmem((RADIX, D, 2 * LANES), BF16),
            vmem((RADIX, D, 2 * LANES), BF16),
            vmem((RADIX, D, 2 * LANES), F32),
            vmem((RADIX, 2, D, LANES), F32),
            vmem((2 * D, CHUNK), BF16),
            vmem((2 * D, CHUNK), BF16),
            vmem((2, DEV, PAIR, LANES), BF16),
            vmem((2, DEV, PAIR, LANES), BF16),
            vmem((2, D, HALF), BF16),
            dma((12,)),
            dma((7,)),
            dma((3,)),
            pltpu.SemaphoreType.REGULAR,
            dma((8,)),
            dma((8,)),
            dma((5,)),
            dma((5,)),
            dma((2,)),
            dma((2,)),
        ],
        compiler_params=pltpu.CompilerParams(collective_id=0, has_side_effects=True),
    )(
        inputs,
        w_in,
        b_in,
        short_kernel.transpose(0, 2, 1),
        filter_out,
        decay.reshape(1, OWN),
        conv_bias.reshape(1, OWN),
        b_out.reshape(1, OWN),
        positional,
        filter_in.T,
        filter_bias,
        filter_freq,
        filter_hidden,
        w_out,
        *tables(),
    )


def solution(mesh):
    in_specs = (
        P("ch", "seq"),
        P(None, "ch", None),
        P(None, "ch"),
        P(None, "ch", None),
        P(None, "seq"),
        P(),
        P(),
        P(),
        P(),
        P("ch", None),
        P("ch"),
        P("ch"),
        P(),
        P("ch"),
    )
    return jax.shard_map(
        body, mesh=mesh, in_specs=in_specs, out_specs=P("ch", "seq"), check_vma=False
    )
```

```python
import math

import jax
import jax.numpy as jnp
import numpy as np
from jax import lax
from jax.experimental import pallas as pl
from jax.experimental.pallas import tpu as pltpu
from jax.sharding import PartitionSpec as P

MESH = pl.DeviceIdType.MESH
F32 = jnp.float32
BF16 = jnp.bfloat16
HIGHEST = lax.Precision.HIGHEST

SEQ, CH = 32, 8
DEV = SEQ * CH
D = 256
OWN = D // CH
SPAN = 4096
CHUNK = SPAN // CH
LENGTH = SPAN * SEQ
HALO = 128
LANES = 128
RADIX = CHUNK // LANES
ORDER = 64
HALF = CHUNK // 2
PAIR = RADIX // 2
FAR = (4, 3, 5, 2, 6, 1, 7)
BIAS, TAPS, DECAY, DIRECT, OUTB = 0, 3, 12, 13, 14
BLOCKS, WIDE = 4, 1024
PI_HIGH, PI_LOW = 3.1414794921875, 0.00011315941810607910156


def halves(table):
    high = np.asarray(table, np.float64).astype(jnp.bfloat16)
    low = (np.asarray(table, np.float64) - high.astype(np.float64)).astype(jnp.bfloat16)
    return high, low


def tables():
    rows = np.arange(D)
    f1 = np.arange(D) + 0.25
    angle = 2.0 * np.pi * ((np.outer(4 * f1, rows) % (4 * D)) / (4 * D))
    first = np.concatenate([np.cos(angle), -np.sin(angle)], axis=0)
    first_stack = np.concatenate(halves(first), axis=0)
    last_stack = np.concatenate(halves(first.T / LENGTH), axis=0)
    lanes = np.arange(LANES)
    inner = 2.0 * np.pi * (np.outer(lanes, lanes) % LANES) / LANES
    c, s = np.cos(inner), np.sin(inner)
    forward = np.stack(halves(np.block([[c, -s], [s, c]])))
    inverse = np.stack(halves(np.block([[c, s], [-s, c]])))
    turn = 2.0 * np.pi / LENGTH * f1[:, None] * lanes[None, :]
    step = 2.0 * np.pi / CHUNK * np.arange(RADIX)[:, None] * lanes[None, :]
    twiddle = np.stack([np.cos(turn), np.sin(turn)]).astype(np.float32)
    steps = np.concatenate([np.cos(step), np.sin(step)]).astype(np.float32)
    spin = 2.0 * np.pi / (RADIX * D) * f1[:, None] * np.arange(RADIX)[None, :]
    spins = np.zeros((D, LANES), np.float32)
    spins[:, 0:RADIX] = np.cos(spin)
    spins[:, RADIX : 2 * RADIX] = np.sin(spin)
    return first_stack, last_stack, forward, inverse, twiddle, steps, spins


def split(x):
    high = x.astype(BF16)
    return high, (x - high.astype(F32)).astype(BF16)


def sine(v):
    turns = jnp.floor(v * (1.0 / math.pi) + 0.5)
    rest = (v - turns * PI_HIGH) - turns * PI_LOW
    half = turns * 0.5
    rest = rest * (1.0 - 4.0 * (half - jnp.floor(half)))
    square = rest * rest
    poly = 2.6083159809786593541503e-06 * square - 0.0001981069071916863322258
    poly = poly * square + 0.00833307858556509017944336
    poly = poly * square - 0.166666597127914428710938
    return rest + rest * (square * poly)


def mm(a, b):
    return jnp.dot(a, b, preferred_element_type=F32)


def kernel(
    x_ref,
    w_ref,
    bin_ref,
    taps_ref,
    fout_ref,
    decay_ref,
    direct_ref,
    bout_ref,
    pos_ref,
    fin_ref,
    fbias_ref,
    ffreq_ref,
    fhid_ref,
    wout_ref,
    first_ref,
    last_ref,
    fwd_ref,
    inv_ref,
    twid_ref,
    step_ref,
    spin_ref,
    out_ref,
    bin_v,
    taps_v,
    fout_v,
    decay_v,
    direct_v,
    bout_v,
    pos_v,
    fin_v,
    fbias_v,
    ffreq_v,
    fhid_v,
    wout_v,
    raw,
    rawnet,
    prm,
    psend,
    ends,
    tails,
    halo,
    before,
    xc,
    wbuf,
    pbuf,
    pflat,
    xs,
    cols,
    spins,
    stage,
    stage2,
    keep0,
    keepg,
    diag,
    weight,
    act,
    value_v,
    kstage,
    ksnd,
    krcv,
    gsnd,
    grcv,
    first_v,
    last_v,
    fwd_v,
    inv_v,
    base_v,
    step_v,
    spin_v,
    twid_v,
    sect,
    chi,
    clo,
    spec,
    back,
    dhi,
    dlo,
    ysnd,
    yrcv,
    osnd,
    small_sem,
    end_sem,
    const_sem,
    ring_sem,
    gate,
    s1,
    r1,
    s3,
    r3,
    s6,
    r6,
):
    s = lax.axis_index("seq")
    c = lax.axis_index("ch")
    me = s * CH + c
    px, py, pk = s // 8, lax.rem(s // 2, 4), lax.rem(s, 2)
    quad = py + pk * (px - py)
    own = pl.multiple_of(c * OWN, OWN)
    rows_own = pl.ds(own, OWN)

    smalls = [
        pltpu.make_async_copy(src, dst, small_sem.at[i])
        for i, (src, dst) in enumerate(
            [
                (bin_ref, bin_v),
                (taps_ref, taps_v),
                (fout_ref, fout_v),
                (decay_ref, decay_v),
                (direct_ref, direct_v),
                (bout_ref, bout_v),
                (pos_ref, pos_v),
                (fin_ref, fin_v),
                (fbias_ref, fbias_v),
                (ffreq_ref, ffreq_v),
                (fhid_ref, fhid_v),
                (wout_ref, wout_v),
            ]
        )
    ]
    consts = [
        pltpu.make_async_copy(src, dst, const_sem.at[i])
        for i, (src, dst) in enumerate(
            [
                (spin_ref, spin_v),
                (first_ref, first_v),
                (twid_ref, base_v),
                (step_ref, step_v),
                (fwd_ref, fwd_v),
                (inv_ref, inv_v),
                (last_ref, last_v),
            ]
        )
    ]
    for copy in smalls:
        copy.start()
    for j in range(CH):
        pltpu.make_async_copy(
            x_ref.at[:, pl.ds((j + 1) * CHUNK - HALO, HALO)], ends.at[j], end_sem
        ).start()

    bar = pltpu.get_barrier_semaphore()

    def greet(sem, to):
        pl.semaphore_signal(sem, inc=1, device_id=to, device_id_type=MESH)

    for i in range(1, CH):
        greet(bar, (s, lax.rem(c + i, CH)))
    for i in range(1, SEQ):
        greet(bar, (lax.rem(s + i, SEQ), c))

    @pl.when(jnp.logical_and(c == 0, s > 0))
    def _():
        for j in range(CH):
            greet(bar, (s - 1, j))

    for i in (0, 1, 3, 4, 5):
        smalls[i].wait()
    raw[...] = jnp.zeros_like(raw)
    raw[0:3, :] = bin_v[...]
    for j in range(3):
        raw[3 + 3 * j : 6 + 3 * j, :] = taps_v[j]
    raw[12:13, :] = decay_v[...]
    raw[13:14, :] = direct_v[...]
    raw[14:15, :] = bout_v[...]

    def columns(rows, n):
        eye = (
            lax.broadcasted_iota(jnp.int32, (n, n), 0) == lax.broadcasted_iota(jnp.int32, (n, n), 1)
        ).astype(F32)
        return lax.dot_general(
            eye, rows, (((1,), (1,)), ((), ())), precision=HIGHEST, preferred_element_type=F32
        )

    prm[...] = jnp.zeros_like(prm)
    mine = columns(raw[...], OWN)
    left = mine
    for i in range(3):
        part = left.astype(BF16)
        prm[:, 16 * i : 16 * i + 16] = part.astype(F32)
        left = left - part.astype(F32)
    psend[...] = prm[...].reshape(4, 8, LANES).astype(BF16)
    pick = (
        lax.broadcasted_iota(jnp.int32, (8, HALO), 1)
        == lax.broadcasted_iota(jnp.int32, (8, HALO), 0) + HALO - 2
    ).astype(BF16)
    tails[...] = jnp.zeros_like(tails)
    pltpu.make_async_copy(ends, ends, end_sem).wait()
    for j in range(CH):
        turned_end = lax.dot_general(
            pick, ends[j], (((1,), (1,)), ((), ())), preferred_element_type=F32
        )
        tails[j, :, 0:OWN] = turned_end.astype(BF16)
    for i in (2, 7, 8, 9, 10):
        smalls[i].wait()
    rawnet[...] = jnp.zeros_like(rawnet)
    rawnet[0:5, :] = fin_v[...]
    rawnet[5:8, :] = fbias_v[...]
    rawnet[8:11, :] = ffreq_v[...]
    net = columns(rawnet[...], ORDER)
    diag[...] = jnp.zeros_like(diag)
    for b in range(BLOCKS):
        at = slice(b * ORDER, (b + 1) * ORDER)
        diag[0, at, at] = fhid_v[0]
        diag[1, at, at] = fhid_v[1]
        diag[2, b * OWN : (b + 1) * OWN, at] = fout_v[...]
    for i in range(3):
        high, low = split(diag[i])
        weight[i, 0:D] = high
        weight[i, D : 2 * D] = low

    pl.semaphore_wait(bar, jnp.where(s < SEQ - 1, SEQ + CH - 1, SEQ + CH - 2))

    def put(src, dst, send, recv, to):
        pltpu.make_async_remote_copy(
            src_ref=src, dst_ref=dst, send_sem=send, recv_sem=recv, device_id=to, device_id_type=MESH
        ).start()

    def wait(ref, sem):
        pltpu.make_async_copy(ref, ref, sem).wait()

    half = pl.ds(pl.multiple_of(lax.rem(quad, 2) * LANES, LANES), LANES)
    octet = 2 * pk + quad // 2
    w_src = w_ref.at[:, pl.ds(pl.multiple_of(octet * 8, 8), 8), half]
    w_dst = wbuf.at[:, c, octet, :, half]
    p_src = psend.at[quad]
    p_dst = pbuf.at[c, quad]
    x_dst = xc.at[rows_own, :]
    h_dst = halo.at[c]

    def chunk(j):
        return x_ref.at[:, pl.ds(pl.multiple_of(j * CHUNK, CHUNK), CHUNK)]

    for i in FAR:
        put(p_src, p_dst, s1.at[0], r1.at[0], (s, lax.rem(c + i, CH)))
    for i in FAR:
        put(w_src, w_dst, s1.at[1], r1.at[1], (s, lax.rem(c + i, CH)))

    @pl.when(s < SEQ - 1)
    def _():
        put(tails.at[CH - 1], h_dst, s1.at[3], r1.at[3], (s + 1, 0))

    for i in FAR:
        j = lax.rem(c + i, CH)
        put(chunk(j), x_dst, s1.at[2], r1.at[2], (s, j))

        @pl.when(j > 0)
        def _():
            put(tails.at[j - 1], h_dst, s1.at[3], r1.at[3], (s, j))


    pltpu.make_async_copy(p_src, p_dst, r1.at[0]).start()
    pltpu.make_async_copy(w_src, w_dst, r1.at[1]).start()
    pltpu.make_async_copy(chunk(c), x_dst, r1.at[2]).start()

    @pl.when(c > 0)
    def _():
        pltpu.make_async_copy(tails.at[c - 1], h_dst, r1.at[3]).start()

    for i in range(1, SEQ):
        greet(gate, (lax.rem(s + i, SEQ), c))
    for copy in consts:
        copy.start()
    for i in (6, 11):
        smalls[i].wait()

    def tile(step):
        b, side = step // 2, lax.rem(step, 2)
        rows = pl.ds(pl.multiple_of(b * ORDER, ORDER), ORDER)
        return b, side, rows, pl.ds(pl.multiple_of(side * CHUNK, CHUNK), CHUNK)

    def keep(layer, value, rows, lanes):
        high, low = split(
            sine(net[:, 8 + layer : 9 + layer] * (value + net[:, 5 + layer : 6 + layer]))
        )
        act[0, rows, lanes] = high
        act[1, rows, lanes] = low

    def enter(step, carry):
        b, side, rows, lanes = tile(step)
        here = pl.ds(pl.multiple_of(step * CHUNK, CHUNK), CHUNK)
        value = net[:, 0:1] * pos_v[0:1, here]
        for i in range(1, 5):
            value = value + net[:, i : i + 1] * pos_v[i : i + 1, here]
        keep(0, value, rows, lanes)
        return carry

    lax.fori_loop(0, 2 * BLOCKS, enter, 0)

    def product(i, n):
        both, one = weight[i, 0 : D + n], weight[i, 0:n]
        wide = mm(both, act[0])
        return wide[0:n] + wide[D : D + n] + mm(one, act[1])

    def hidden(layer):
        value_v[...] = product(layer - 1, D)

        def leave(step, carry):
            b, side, rows, lanes = tile(step)
            keep(layer, value_v[rows, lanes], rows, lanes)
            return carry

        lax.fori_loop(0, 2 * BLOCKS, leave, 0)

    hidden(1)

    ring = 2 + 6 * pk
    around = [(i, (s + ring * (lax.rem(quad + i, 4) - quad), c)) for i in (2, 1, 3)]
    partner = (s + 1 - 2 * pk, c)

    def piece(q):
        lanes = pl.ds(pl.multiple_of(lax.rem(q, 2) * LANES, LANES), LANES)
        return wbuf.at[:, :, 2 * pk + q // 2, :, lanes]

    p_mine = pbuf.at[:, quad]
    wait(p_mine, r1.at[0])
    for _, to in around:
        put(p_mine, p_mine, s1.at[4], r1.at[4], to)
    w_mine = piece(quad)
    wait(w_mine, r1.at[1])
    for i, to in around:
        put(w_mine, w_mine, s1.at[5], ring_sem.at[i - 1], to)
    put(w_mine, w_mine, s1.at[6], r1.at[6], partner)

    hidden(2)
    values = product(2, BLOCKS * OWN)
    lane = lax.broadcasted_iota(jnp.int32, (1, WIDE), 1)
    for b in range(BLOCKS):
        places = s * SPAN + b * WIDE + lane
        scaled = places.astype(F32) / (LENGTH - 1)
        window = jnp.exp(-(scaled * mine[:, DECAY : DECAY + 1]))
        block = values[b * OWN : (b + 1) * OWN] * window
        for q in range(2 * RADIX):
            kstage[:, 2 * b + q // RADIX, q % RADIX, :] = block[:, q * LANES : (q + 1) * LANES]
    ksnd[...] = kstage[...].astype(BF16)
    far = [(i, j, l) for i in (2, 1, 3, 0) for j in (2, 1, 3, 0) for l in (1, 0)]
    theirs = pl.ds(pl.multiple_of(s * CH, CH), CH)
    for i, j, l in far[:-1]:
        si = lax.rem(px + i, 4) * 8 + lax.rem(py + j, 4) * 2 + lax.rem(pk + l, 2)
        put(ksnd.at[si], krcv.at[theirs], s3.at[0], r3.at[0], (si, c))
    pltpu.make_async_copy(ksnd.at[s], krcv.at[theirs], r3.at[0]).start()

    def hand_over(i):
        got = piece(lax.rem(quad + 4 - i, 4))
        wait(got, ring_sem.at[i - 1])
        put(got, got, s1.at[6], r1.at[6], partner)

    hand_over(1)
    hand_over(3)
    spots = [(i, j, l) for i in range(4) for j in range(4) for l in range(2)]
    spots.sort(key=lambda o: -(min(o[0], 4 - o[0]) + min(o[1], 4 - o[1])))
    spots = [o for o in spots if o != (0, 0, 0)] + [(0, 0, 0)]
    at_x = [lax.rem(px + i, 4) * 8 for i in range(4)]
    at_y = [lax.rem(py + i, 4) * 2 for i in range(4)]
    at_k = [lax.rem(pk + i, 2) for i in range(2)]

    hand_over(2)
    wait(pbuf.at[pl.ds(0, 6)], r1.at[4])
    arrived = pbuf[...].astype(F32).reshape(D, LANES)
    pflat[...] = arrived + (
        pltpu.roll(arrived, LANES - 16, 1) + pltpu.roll(arrived, LANES - 32, 1)
    )
    for j in range(3):
        bias = jnp.broadcast_to(pflat[:, BIAS + j : BIAS + j + 1], (D, LANES))
        total = None
        for i in range(3):
            at = TAPS + 3 * j + i
            tap = jnp.broadcast_to(pflat[:, at : at + 1], (D, LANES))
            cols[3 * j + i] = tap
            total = tap * bias if total is None else total + tap * bias
            if i < 2:
                cols[9 + 3 * j + i] = tap * bias
            else:
                cols[11 + 3 * j] = total
                cols[18 + j] = tap * bias

    before[...] = jnp.zeros_like(before)

    @pl.when(me > 0)
    def _():
        wait(halo, r1.at[3])
        eye = (
            lax.broadcasted_iota(jnp.int32, (OWN, OWN), 0)
            == lax.broadcasted_iota(jnp.int32, (OWN, OWN), 1)
        ).astype(BF16)
        for j in range(CH):
            pair_columns = lax.dot_general(
                eye, halo[j, :, 0:OWN], (((1,), (1,)), ((), ())), preferred_element_type=F32
            )
            before[j * OWN : (j + 1) * OWN, HALO - 2 : HALO] = pair_columns[:, 0:2]

    pl.semaphore_wait(gate, SEQ - 1)
    wait(xc, r1.at[2])

    wait(wbuf.at[:, :, pl.ds(0, 2)], r1.at[6])

    wide = jnp.concatenate([before[...], xc[...].astype(F32)], axis=1)
    for i in (0, 1):
        xs[i] = pltpu.roll(wide, 2 - i, 1)[:, HALO:].astype(BF16)
    place = lax.broadcasted_iota(jnp.int32, (1, LANES), 1)
    started = [jnp.logical_or(place >= 2 - i, me > 0).astype(F32) for i in (0, 1)]

    def gates(t, carry):
        pair = lax.rem(c // 2 + 2 + (t + 1) // 2 * (1 - 2 * lax.rem(t, 2)), 4)
        rows = pl.ds(pl.multiple_of(pair * 64, 64), 64)
        w = wbuf[:, pl.ds(pair * 2, 2)].astype(F32).reshape(3 * 64, D).astype(BF16)
        taken = [mm(w, xs[0]), mm(w, xs[1]), mm(w, xc[...])]
        for r in range(RADIX):
            lanes = slice(r * LANES, (r + 1) * LANES)
            streams = []
            for j in range(3):
                if r:
                    total = cols[11 + 3 * j, rows, :]
                else:
                    total = cols[18 + j, rows, :]
                    for i in range(2):
                        total = total + cols[9 + 3 * j + i, rows, :] * started[i]
                for i in range(3):
                    part = taken[i][64 * j : 64 * j + 64, lanes]
                    total = total + cols[3 * j + i, rows, :] * part
                streams.append(total)
            gated = streams[2] * streams[1]
            keep0[rows, lanes] = streams[0]
            keepg[rows, lanes] = gated
            stage[rows, r, :] = gated
        gsnd[rows] = stage[rows].astype(BF16)
        for i, j, l in spots:
            si = at_x[i] + at_y[j] + at_k[l]
            for e in range(2):
                cj = 2 * pair + e
                src, dst = gsnd.at[cj * SEQ + si], grcv.at[me]
                if (i, j, l) == (0, 0, 0):

                    @pl.when(cj != c)
                    def _():
                        put(src, dst, s3.at[1], r3.at[1], (si, cj))

                    @pl.when(cj == c)
                    def _():
                        pltpu.make_async_copy(src, dst, r3.at[1]).start()

                else:
                    put(src, dst, s3.at[1], r3.at[1], (si, cj))
        return carry

    lax.fori_loop(0, 4, gates, 0)

    for copy in consts:
        copy.wait()
    for i in range(6):
        at = 1 + i if i < 3 else 2 + i
        spins[i] = jnp.broadcast_to(spin_v[:, at : at + 1], (D, LANES))
    for h in range(RADIX):
        lanes = slice(h * LANES, (h + 1) * LANES)
        cs, sn = step_v[h : h + 1, :], step_v[RADIX + h : RADIX + h + 1, :]
        twid_v[0, :, lanes] = base_v[0] * cs - base_v[1] * sn
        twid_v[1, :, lanes] = base_v[1] * cs + base_v[0] * sn


    def whole(rcv):
        stage[...] = rcv[...].astype(F32)
        x = jnp.concatenate([stage[:, r, :] for r in range(RADIX)], axis=1).astype(BF16)
        for part in range(2):
            sect[part] = mm(first_v[part * D : (part + 1) * D, :], x) + mm(
                first_v[(2 + part) * D : (3 + part) * D, :], x
            )

    def turned():
        def ahead(step, carry):
            rows = pl.ds(pl.multiple_of(step * 32, 32), 32)
            re, im = [], []
            for r in range(RADIX):
                lanes = slice(r * LANES, (r + 1) * LANES)
                a, b = sect[0, rows, lanes], sect[1, rows, lanes]
                if r:
                    cs, sn = spins[r - 1, rows, :], spins[r + 2, rows, :]
                    a, b = a * cs + b * sn, b * cs - a * sn
                re.append(a)
                im.append(b)
            e0r, e0i, e1r, e1i = re[0] + re[2], im[0] + im[2], re[0] - re[2], im[0] - im[2]
            o0r, o0i, o1r, o1i = re[1] + re[3], im[1] + im[3], re[1] - re[3], im[1] - im[3]
            outs = [
                (e0r + o0r, e0i + o0i),
                (e1r + o1i, e1i - o1r),
                (e0r - o0r, e0i - o0i),
                (e1r - o1i, e1i + o1r),
            ]
            for h, (a, b) in enumerate(outs):
                cs = twid_v[0, rows, h * LANES : (h + 1) * LANES]
                sn = twid_v[1, rows, h * LANES : (h + 1) * LANES]
                high, low = split(jnp.concatenate([a * cs + b * sn, b * cs - a * sn], axis=1))
                chi[h, rows, :] = high
                clo[h, rows, :] = low
            return carry

        lax.fori_loop(0, D // 32, ahead, 0)

    def spectrum(h):
        high, low = chi[h], clo[h]
        return mm(high, fwd_v[0]) + mm(low, fwd_v[0]) + mm(high, fwd_v[1])

    wait(krcv, r3.at[0])
    whole(krcv)
    turned()
    for h in range(RADIX):
        spec[h] = spectrum(h)
    wait(grcv, r3.at[1])
    whole(grcv)
    turned()
    for h in range(RADIX):
        g, k = spectrum(h), spec[h]
        gr, gi, kr, ki = g[:, :LANES], g[:, LANES:], k[:, :LANES], k[:, LANES:]
        high, low = split(jnp.concatenate([gr * kr - gi * ki, gr * ki + gi * kr], axis=1))
        z = mm(high, inv_v[0]) + mm(low, inv_v[0]) + mm(high, inv_v[1])
        zr, zi = z[:, :LANES], z[:, LANES:]
        cs = twid_v[0, :, h * LANES : (h + 1) * LANES]
        sn = twid_v[1, :, h * LANES : (h + 1) * LANES]
        back[h, 0] = zr * cs - zi * sn
        back[h, 1] = zi * cs + zr * sn

    def behind(step, carry):
        lo = pl.multiple_of(step * 32, 32)
        rows = pl.ds(lo, 32)
        rows_im = pl.ds(pl.multiple_of(D + lo, 32), 32)
        re = [back[h, 0, rows, :] for h in range(RADIX)]
        im = [back[h, 1, rows, :] for h in range(RADIX)]
        e0r, e0i, e1r, e1i = re[0] + re[2], im[0] + im[2], re[0] - re[2], im[0] - im[2]
        o0r, o0i, o1r, o1i = re[1] + re[3], im[1] + im[3], re[1] - re[3], im[1] - im[3]
        outs = [
            (e0r + o0r, e0i + o0i),
            (e1r - o1i, e1i + o1r),
            (e0r - o0r, e0i - o0i),
            (e1r + o1i, e1i - o1r),
        ]
        for r, (a, b) in enumerate(outs):
            if r:
                cs, sn = spins[r - 1, rows, :], spins[r + 2, rows, :]
                a, b = a * cs - b * sn, b * cs + a * sn
            lanes = slice(r * LANES, (r + 1) * LANES)
            high, low = split(a)
            dhi[rows, lanes] = high
            dlo[rows, lanes] = low
            high, low = split(b)
            dhi[rows_im, lanes] = high
            dlo[rows_im, lanes] = low
        return carry

    lax.fori_loop(0, D // 32, behind, 0)
    last_hi, last_lo = last_v[0:D, :], last_v[D : 2 * D, :]
    def settle(h, carry):
        lanes_h = pl.ds(pl.multiple_of(h * HALF, HALF), HALF)
        high, low = dhi[:, lanes_h], dlo[:, lanes_h]
        settled = mm(last_hi, high) + mm(last_lo, high) + mm(last_hi, low)
        for r in range(PAIR):
            stage2[:, r, :] = settled[:, r * LANES : (r + 1) * LANES]
        ysnd[h] = stage2[...].astype(BF16)
        to_row = c * SEQ + s
        for i, j, l in spots:
            si = at_x[i] + at_y[j] + at_k[l]
            for far in FAR + (0,):
                if (i, j, l, far) != (0, 0, 0, 0):
                    cj = lax.rem(c + far, CH)
                    put(
                        ysnd.at[h, si * CH + cj],
                        yrcv.at[h, to_row],
                        s3.at[3 + h],
                        r3.at[3 + h],
                        (si, cj),
                    )
        pltpu.make_async_copy(ysnd.at[h, me], yrcv.at[h, to_row], r3.at[3 + h]).start()
        return carry

    lax.fori_loop(0, 2, settle, 0)

    def mix(h):
        wait(yrcv.at[h], r3.at[3 + h])
        cols_h = slice(h * HALF, (h + 1) * HALF)
        stage2[...] = yrcv[h].astype(F32)
        convolved = jnp.concatenate([stage2[:, r, :] for r in range(PAIR)], axis=1)
        convolved = convolved + pflat[:, DIRECT : DIRECT + 1] * keepg[:, cols_h]
        mixed = (keep0[:, cols_h] * convolved).astype(BF16)
        osnd[h] = (mm(wout_v[...], mixed) + pflat[:, OUTB : OUTB + 1]).astype(BF16)
        o_dst = out_ref.at[:, pl.ds(pl.multiple_of(c * CHUNK + h * HALF, HALF), HALF)]
        for i in FAR:
            j = lax.rem(c + i, CH)
            put(
                osnd.at[h, pl.ds(pl.multiple_of(j * OWN, OWN), OWN), :],
                o_dst,
                s6.at[h],
                r6.at[h],
                (s, j),
            )
        pltpu.make_async_copy(osnd.at[h, rows_own, :], o_dst, r6.at[h]).start()

    mix(0)
    mix(1)

    for h in range(2):
        wait(out_ref.at[:, pl.ds(0, SPAN // 2)], r6.at[h])
    most = pl.ds(0, CH - 1)
    wait(pbuf.at[most, 0], s1.at[0])
    wait(wbuf.at[:, most, 0, :, pl.ds(0, LANES)], s1.at[1])
    wait(wbuf.at[:, pl.ds(0, 6), pl.ds(0, 2)], s1.at[5])
    wait(wbuf.at[:, :, pl.ds(0, 2)], s1.at[6])
    wait(xc.at[pl.ds(0, D - OWN), :], s1.at[2])
    wait(halo.at[pl.ds(0, 6)], s1.at[3])

    @pl.when(c == 0)
    def _():
        wait(halo.at[0], s1.at[3])

    @pl.when(s < SEQ - 1)
    def _():
        wait(halo.at[0], s1.at[3])

    wait(pbuf.at[pl.ds(0, 6)], s1.at[4])
    wait(ksnd.at[pl.ds(0, SEQ - 1)], s3.at[0])
    wait(gsnd.at[pl.ds(0, DEV - 1)], s3.at[1])
    for h in range(2):
        wait(ysnd.at[h, pl.ds(0, DEV - 1)], s3.at[3 + h])
        wait(osnd.at[h, pl.ds(0, D - OWN), :], s6.at[h])


def body(
    inputs,
    w_in,
    b_in,
    short_kernel,
    positional,
    filter_in,
    filter_bias,
    filter_freq,
    filter_hidden,
    filter_out,
    decay,
    conv_bias,
    w_out,
    b_out,
):
    dma = pltpu.SemaphoreType.DMA
    hbm = pl.BlockSpec(memory_space=pl.ANY)
    vmem = pltpu.VMEM
    return pl.pallas_call(
        kernel,
        out_shape=pltpu.VMEM((OWN, SPAN), BF16),
        in_specs=[hbm] * 21,
        out_specs=pl.BlockSpec(memory_space=pltpu.VMEM),
        scratch_shapes=[
            vmem((3, OWN), F32),
            vmem((3, 3, OWN), F32),
            vmem((OWN, ORDER), F32),
            vmem((1, OWN), F32),
            vmem((1, OWN), F32),
            vmem((1, OWN), F32),
            vmem((5, SPAN), F32),
            vmem((5, ORDER), F32),
            vmem((3, ORDER), F32),
            vmem((3, ORDER), F32),
            vmem((2, ORDER, ORDER), F32),
            vmem((D, D), BF16),
            vmem((16, OWN), F32),
            vmem((16, ORDER), F32),
            vmem((OWN, LANES), F32),
            vmem((4, 8, LANES), BF16),
            vmem((CH, OWN, HALO), BF16),
            vmem((CH, 8, LANES), BF16),
            vmem((CH, 8, LANES), BF16),
            vmem((D, HALO), F32),
            vmem((D, CHUNK), BF16),
            vmem((3, CH, 4, 8, D), BF16),
            vmem((CH, 4, 8, LANES), BF16),
            vmem((D, LANES), F32),
            vmem((2, D, CHUNK), BF16),
            vmem((21, D, LANES), F32),
            vmem((6, D, LANES), F32),
            vmem((DEV, RADIX, LANES), F32),
            vmem((DEV, PAIR, LANES), F32),
            vmem((D, CHUNK), F32),
            vmem((D, CHUNK), F32),
            vmem((3, D, D), F32),
            vmem((3, 2 * D, D), BF16),
            vmem((2, D, WIDE), BF16),
            vmem((D, WIDE), F32),
            vmem((OWN, CH, RADIX, LANES), F32),
            vmem((OWN, CH, RADIX, LANES), BF16),
            vmem((DEV, RADIX, LANES), BF16),
            vmem((DEV, RADIX, LANES), BF16),
            vmem((DEV, RADIX, LANES), BF16),
            vmem((4 * D, D), BF16),
            vmem((2 * D, 2 * D), BF16),
            vmem((2, D, D), BF16),
            vmem((2, D, D), BF16),
            vmem((2, D, LANES), F32),
            vmem((2 * RADIX, LANES), F32),
            vmem((D, LANES), F32),
            vmem((2, D, CHUNK), F32),
            vmem((2, D, CHUNK), F32),
            vmem((RADIX, D, 2 * LANES), BF16),
            vmem((RADIX, D, 2 * LANES), BF16),
            vmem((RADIX, D, 2 * LANES), F32),
            vmem((RADIX, 2, D, LANES), F32),
            vmem((2 * D, CHUNK), BF16),
            vmem((2 * D, CHUNK), BF16),
            vmem((2, DEV, PAIR, LANES), BF16),
            vmem((2, DEV, PAIR, LANES), BF16),
            vmem((2, D, HALF), BF16),
            dma((12,)),
            dma,
            dma((7,)),
            dma((3,)),
            pltpu.SemaphoreType.REGULAR,
            dma((8,)),
            dma((8,)),
            dma((5,)),
            dma((5,)),
            dma((2,)),
            dma((2,)),
        ],
        compiler_params=pltpu.CompilerParams(collective_id=0, has_side_effects=True),
    )(
        inputs,
        w_in,
        b_in,
        short_kernel.transpose(0, 2, 1),
        filter_out,
        decay.reshape(1, OWN),
        conv_bias.reshape(1, OWN),
        b_out.reshape(1, OWN),
        positional,
        filter_in.T,
        filter_bias,
        filter_freq,
        filter_hidden,
        w_out,
        *tables(),
    )


def solution(mesh):
    in_specs = (
        P("ch", "seq"),
        P(None, "ch", None),
        P(None, "ch"),
        P(None, "ch", None),
        P(None, "seq"),
        P(),
        P(),
        P(),
        P(),
        P("ch", None),
        P("ch"),
        P("ch"),
        P(),
        P("ch"),
    )
    return jax.shard_map(
        body, mesh=mesh, in_specs=in_specs, out_specs=P("ch", "seq"), check_vma=False
    )
```

```python
import math

import jax
import jax.numpy as jnp
import numpy as np
from jax import lax
from jax.experimental import pallas as pl
from jax.experimental.pallas import tpu as pltpu
from jax.sharding import PartitionSpec as P

MESH = pl.DeviceIdType.MESH
F32 = jnp.float32
BF16 = jnp.bfloat16
HIGHEST = lax.Precision.HIGHEST

SEQ, CH = 32, 8
DEV = SEQ * CH
D = 256
OWN = D // CH
SPAN = 4096
CHUNK = SPAN // CH
LENGTH = SPAN * SEQ
HALO = 128
LANES = 128
RADIX = CHUNK // LANES
ORDER = 64
HALF = CHUNK // 2
PAIR = RADIX // 2
FAR = (4, 3, 5, 2, 6, 1, 7)
BIAS, TAPS, DECAY, DIRECT, OUTB = 0, 3, 12, 13, 14
BLOCKS, WIDE = 4, 1024
PI_HIGH, PI_LOW = 3.1414794921875, 0.00011315941810607910156


def halves(table):
    high = np.asarray(table, np.float64).astype(jnp.bfloat16)
    low = (np.asarray(table, np.float64) - high.astype(np.float64)).astype(jnp.bfloat16)
    return high, low


def tables():
    rows = np.arange(D)
    f1 = np.arange(D) + 0.25
    angle = 2.0 * np.pi * ((np.outer(4 * f1, rows) % (4 * D)) / (4 * D))
    first = np.concatenate([np.cos(angle), -np.sin(angle)], axis=0)
    first_stack = np.concatenate(halves(first), axis=0)
    last_stack = np.concatenate(halves(first.T / LENGTH), axis=0)
    lanes = np.arange(LANES)
    inner = 2.0 * np.pi * (np.outer(lanes, lanes) % LANES) / LANES
    c, s = np.cos(inner), np.sin(inner)
    forward = np.stack(halves(np.block([[c, -s], [s, c]])))
    inverse = np.stack(halves(np.block([[c, s], [-s, c]])))
    turn = 2.0 * np.pi / LENGTH * f1[:, None] * lanes[None, :]
    step = 2.0 * np.pi / CHUNK * np.arange(RADIX)[:, None] * lanes[None, :]
    twiddle = np.stack([np.cos(turn), np.sin(turn)]).astype(np.float32)
    steps = np.concatenate([np.cos(step), np.sin(step)]).astype(np.float32)
    spin = 2.0 * np.pi / (RADIX * D) * f1[:, None] * np.arange(RADIX)[None, :]
    spins = np.zeros((D, LANES), np.float32)
    spins[:, 0:RADIX] = np.cos(spin)
    spins[:, RADIX : 2 * RADIX] = np.sin(spin)
    return first_stack, last_stack, forward, inverse, twiddle, steps, spins


def split(x):
    high = x.astype(BF16)
    return high, (x - high.astype(F32)).astype(BF16)


def sine(v):
    turns = jnp.floor(v * (1.0 / math.pi) + 0.5)
    rest = (v - turns * PI_HIGH) - turns * PI_LOW
    half = turns * 0.5
    rest = rest * (1.0 - 4.0 * (half - jnp.floor(half)))
    square = rest * rest
    poly = 2.6083159809786593541503e-06 * square - 0.0001981069071916863322258
    poly = poly * square + 0.00833307858556509017944336
    poly = poly * square - 0.166666597127914428710938
    return rest + rest * (square * poly)


def mm(a, b):
    return jnp.dot(a, b, preferred_element_type=F32)


def kernel(
    x_ref,
    w_ref,
    bin_ref,
    taps_ref,
    fout_ref,
    decay_ref,
    direct_ref,
    bout_ref,
    pos_ref,
    fin_ref,
    fbias_ref,
    ffreq_ref,
    fhid_ref,
    wout_ref,
    first_ref,
    last_ref,
    fwd_ref,
    inv_ref,
    twid_ref,
    step_ref,
    spin_ref,
    out_ref,
    bin_v,
    taps_v,
    fout_v,
    decay_v,
    direct_v,
    bout_v,
    pos_v,
    fin_v,
    fbias_v,
    ffreq_v,
    fhid_v,
    wout_v,
    raw,
    rawnet,
    prm,
    psend,
    xc,
    wbuf,
    pbuf,
    pflat,
    xs,
    cols,
    spins,
    stage,
    stage2,
    keep0,
    keepg,
    diag,
    weight,
    act,
    value_v,
    kstage,
    ksnd,
    krcv,
    gsnd,
    grcv,
    first_v,
    last_v,
    fwd_v,
    inv_v,
    base_v,
    step_v,
    spin_v,
    twid_v,
    sect,
    chi,
    clo,
    spec,
    back,
    dhi,
    dlo,
    ysnd,
    yrcv,
    osnd,
    small_sem,
    const_sem,
    ring_sem,
    gate,
    s1,
    r1,
    s3,
    r3,
    s6,
    r6,
):
    s = lax.axis_index("seq")
    c = lax.axis_index("ch")
    me = s * CH + c
    px, py, pk = s // 8, lax.rem(s // 2, 4), lax.rem(s, 2)
    quad = py + pk * (px - py)
    own = pl.multiple_of(c * OWN, OWN)
    rows_own = pl.ds(own, OWN)

    smalls = [
        pltpu.make_async_copy(src, dst, small_sem.at[i])
        for i, (src, dst) in enumerate(
            [
                (bin_ref, bin_v),
                (taps_ref, taps_v),
                (fout_ref, fout_v),
                (decay_ref, decay_v),
                (direct_ref, direct_v),
                (bout_ref, bout_v),
                (pos_ref, pos_v),
                (fin_ref, fin_v),
                (fbias_ref, fbias_v),
                (ffreq_ref, ffreq_v),
                (fhid_ref, fhid_v),
                (wout_ref, wout_v),
            ]
        )
    ]
    consts = [
        pltpu.make_async_copy(src, dst, const_sem.at[i])
        for i, (src, dst) in enumerate(
            [
                (spin_ref, spin_v),
                (first_ref, first_v),
                (twid_ref, base_v),
                (step_ref, step_v),
                (fwd_ref, fwd_v),
                (inv_ref, inv_v),
                (last_ref, last_v),
            ]
        )
    ]
    for copy in smalls:
        copy.start()

    bar = pltpu.get_barrier_semaphore()

    def greet(sem, to):
        pl.semaphore_signal(sem, inc=1, device_id=to, device_id_type=MESH)

    for i in range(1, CH):
        greet(bar, (s, lax.rem(c + i, CH)))
    for i in range(1, SEQ):
        greet(bar, (lax.rem(s + i, SEQ), c))

    @pl.when(jnp.logical_and(c == 0, s > 0))
    def _():
        for j in range(CH):
            greet(bar, (s - 1, j))

    for i in (0, 1, 3, 4, 5):
        smalls[i].wait()
    raw[...] = jnp.zeros_like(raw)
    raw[0:3, :] = bin_v[...]
    for j in range(3):
        raw[3 + 3 * j : 6 + 3 * j, :] = taps_v[j]
    raw[12:13, :] = decay_v[...]
    raw[13:14, :] = direct_v[...]
    raw[14:15, :] = bout_v[...]

    def columns(rows, n):
        eye = (
            lax.broadcasted_iota(jnp.int32, (n, n), 0) == lax.broadcasted_iota(jnp.int32, (n, n), 1)
        ).astype(F32)
        return lax.dot_general(
            eye, rows, (((1,), (1,)), ((), ())), precision=HIGHEST, preferred_element_type=F32
        )

    prm[...] = jnp.zeros_like(prm)
    mine = columns(raw[...], OWN)
    left = mine
    for i in range(3):
        part = left.astype(BF16)
        prm[:, 16 * i : 16 * i + 16] = part.astype(F32)
        left = left - part.astype(F32)
    psend[...] = prm[...].reshape(4, 8, LANES).astype(BF16)
    for i in (2, 7, 8, 9, 10):
        smalls[i].wait()
    rawnet[...] = jnp.zeros_like(rawnet)
    rawnet[0:5, :] = fin_v[...]
    rawnet[5:8, :] = fbias_v[...]
    rawnet[8:11, :] = ffreq_v[...]
    net = columns(rawnet[...], ORDER)
    diag[...] = jnp.zeros_like(diag)
    for b in range(BLOCKS):
        at = slice(b * ORDER, (b + 1) * ORDER)
        diag[0, at, at] = fhid_v[0]
        diag[1, at, at] = fhid_v[1]
        diag[2, b * OWN : (b + 1) * OWN, at] = fout_v[...]
    for i in range(3):
        high, low = split(diag[i])
        weight[i, 0:D] = high
        weight[i, D : 2 * D] = low

    pl.semaphore_wait(bar, jnp.where(s < SEQ - 1, SEQ + CH - 1, SEQ + CH - 2))

    def put(src, dst, send, recv, to):
        pltpu.make_async_remote_copy(
            src_ref=src, dst_ref=dst, send_sem=send, recv_sem=recv, device_id=to, device_id_type=MESH
        ).start()

    def wait(ref, sem):
        pltpu.make_async_copy(ref, ref, sem).wait()

    half = pl.ds(pl.multiple_of(lax.rem(quad, 2) * LANES, LANES), LANES)
    octet = 2 * pk + quad // 2
    w_src = w_ref.at[:, pl.ds(pl.multiple_of(octet * 8, 8), 8), half]
    w_dst = wbuf.at[:, c, octet, :, half]
    p_src = psend.at[quad]
    p_dst = pbuf.at[c, quad]
    x_dst = xc.at[rows_own, pl.ds(HALO, CHUNK)]
    h_dst = xc.at[rows_own, pl.ds(0, HALO)]

    def chunk(j):
        return x_ref.at[:, pl.ds(pl.multiple_of(j * CHUNK, CHUNK), CHUNK)]

    def tail(j):
        return x_ref.at[:, pl.ds(pl.multiple_of(j * CHUNK + CHUNK - HALO, HALO), HALO)]

    for i in FAR:
        put(p_src, p_dst, s1.at[0], r1.at[0], (s, lax.rem(c + i, CH)))
    for i in FAR:
        put(w_src, w_dst, s1.at[1], r1.at[1], (s, lax.rem(c + i, CH)))

    @pl.when(s < SEQ - 1)
    def _():
        put(tail(CH - 1), h_dst, s1.at[3], r1.at[3], (s + 1, 0))

    for i in FAR:
        j = lax.rem(c + i, CH)
        put(chunk(j), x_dst, s1.at[2], r1.at[2], (s, j))

        @pl.when(j > 0)
        def _():
            put(tail(j - 1), h_dst, s1.at[3], r1.at[3], (s, j))


    pltpu.make_async_copy(p_src, p_dst, r1.at[0]).start()
    pltpu.make_async_copy(w_src, w_dst, r1.at[1]).start()
    pltpu.make_async_copy(chunk(c), x_dst, r1.at[2]).start()

    @pl.when(c > 0)
    def _():
        pltpu.make_async_copy(tail(c - 1), h_dst, r1.at[3]).start()

    @pl.when(me == 0)
    def _():
        xc[:, 0:HALO] = jnp.zeros((D, HALO), BF16)

    for i in range(1, SEQ):
        greet(gate, (lax.rem(s + i, SEQ), c))
    for copy in consts:
        copy.start()
    for i in (6, 11):
        smalls[i].wait()

    def tile(step):
        b, side = step // 2, lax.rem(step, 2)
        rows = pl.ds(pl.multiple_of(b * ORDER, ORDER), ORDER)
        return b, side, rows, pl.ds(pl.multiple_of(side * CHUNK, CHUNK), CHUNK)

    def keep(layer, value, rows, lanes):
        high, low = split(
            sine(net[:, 8 + layer : 9 + layer] * (value + net[:, 5 + layer : 6 + layer]))
        )
        act[0, rows, lanes] = high
        act[1, rows, lanes] = low

    def enter(step, carry):
        b, side, rows, lanes = tile(step)
        here = pl.ds(pl.multiple_of(step * CHUNK, CHUNK), CHUNK)
        value = net[:, 0:1] * pos_v[0:1, here]
        for i in range(1, 5):
            value = value + net[:, i : i + 1] * pos_v[i : i + 1, here]
        keep(0, value, rows, lanes)
        return carry

    lax.fori_loop(0, 2 * BLOCKS, enter, 0)

    def product(i, n):
        both, one = weight[i, 0 : D + n], weight[i, 0:n]
        wide = mm(both, act[0])
        return wide[0:n] + wide[D : D + n] + mm(one, act[1])

    def hidden(layer):
        value_v[...] = product(layer - 1, D)

        def leave(step, carry):
            b, side, rows, lanes = tile(step)
            keep(layer, value_v[rows, lanes], rows, lanes)
            return carry

        lax.fori_loop(0, 2 * BLOCKS, leave, 0)

    hidden(1)

    ring = 2 + 6 * pk
    around = [(i, (s + ring * (lax.rem(quad + i, 4) - quad), c)) for i in (2, 1, 3)]
    partner = (s + 1 - 2 * pk, c)

    def piece(q):
        lanes = pl.ds(pl.multiple_of(lax.rem(q, 2) * LANES, LANES), LANES)
        return wbuf.at[:, :, 2 * pk + q // 2, :, lanes]

    p_mine = pbuf.at[:, quad]
    wait(p_mine, r1.at[0])
    for _, to in around:
        put(p_mine, p_mine, s1.at[4], r1.at[4], to)
    w_mine = piece(quad)
    wait(w_mine, r1.at[1])
    for i, to in around:
        put(w_mine, w_mine, s1.at[5], ring_sem.at[i - 1], to)
    put(w_mine, w_mine, s1.at[6], r1.at[6], partner)

    hidden(2)
    values = product(2, BLOCKS * OWN)
    lane = lax.broadcasted_iota(jnp.int32, (1, WIDE), 1)
    for b in range(BLOCKS):
        places = s * SPAN + b * WIDE + lane
        scaled = places.astype(F32) / (LENGTH - 1)
        window = jnp.exp(-(scaled * mine[:, DECAY : DECAY + 1]))
        block = values[b * OWN : (b + 1) * OWN] * window
        for q in range(2 * RADIX):
            kstage[:, 2 * b + q // RADIX, q % RADIX, :] = block[:, q * LANES : (q + 1) * LANES]
    ksnd[...] = kstage[...].astype(BF16)
    far = [(i, j, l) for i in (2, 1, 3, 0) for j in (2, 1, 3, 0) for l in (1, 0)]
    theirs = pl.ds(pl.multiple_of(s * CH, CH), CH)
    for i, j, l in far[:-1]:
        si = lax.rem(px + i, 4) * 8 + lax.rem(py + j, 4) * 2 + lax.rem(pk + l, 2)
        put(ksnd.at[si], krcv.at[theirs], s3.at[0], r3.at[0], (si, c))
    pltpu.make_async_copy(ksnd.at[s], krcv.at[theirs], r3.at[0]).start()

    def hand_over(i):
        got = piece(lax.rem(quad + 4 - i, 4))
        wait(got, ring_sem.at[i - 1])
        put(got, got, s1.at[6], r1.at[6], partner)

    hand_over(1)
    hand_over(3)
    spots = [(i, j, l) for i in range(4) for j in range(4) for l in range(2)]
    spots.sort(key=lambda o: -(min(o[0], 4 - o[0]) + min(o[1], 4 - o[1])))
    spots = [o for o in spots if o != (0, 0, 0)] + [(0, 0, 0)]
    at_x = [lax.rem(px + i, 4) * 8 for i in range(4)]
    at_y = [lax.rem(py + i, 4) * 2 for i in range(4)]
    at_k = [lax.rem(pk + i, 2) for i in range(2)]

    hand_over(2)
    wait(pbuf.at[pl.ds(0, 6)], r1.at[4])
    arrived = pbuf[...].astype(F32).reshape(D, LANES)
    pflat[...] = arrived + (
        pltpu.roll(arrived, LANES - 16, 1) + pltpu.roll(arrived, LANES - 32, 1)
    )
    for j in range(3):
        bias = jnp.broadcast_to(pflat[:, BIAS + j : BIAS + j + 1], (D, LANES))
        total = None
        for i in range(3):
            at = TAPS + 3 * j + i
            tap = jnp.broadcast_to(pflat[:, at : at + 1], (D, LANES))
            cols[3 * j + i] = tap
            total = tap * bias if total is None else total + tap * bias
            if i < 2:
                cols[9 + 3 * j + i] = tap * bias
            else:
                cols[11 + 3 * j] = total
                cols[18 + j] = tap * bias

    pl.semaphore_wait(gate, SEQ - 1)
    wait(xc.at[:, pl.ds(HALO, CHUNK)], r1.at[2])

    @pl.when(me > 0)
    def _():
        wait(xc.at[:, pl.ds(0, HALO)], r1.at[3])

    wait(wbuf.at[:, :, pl.ds(0, 2)], r1.at[6])

    wide = xc[...].astype(F32)
    for i in (0, 1):
        xs[i] = pltpu.roll(wide, 2 - i, 1)[:, HALO:].astype(BF16)
    place = lax.broadcasted_iota(jnp.int32, (1, LANES), 1)
    started = [jnp.logical_or(place >= 2 - i, me > 0).astype(F32) for i in (0, 1)]

    def gates(t, carry):
        pair = lax.rem(c // 2 + 2 + (t + 1) // 2 * (1 - 2 * lax.rem(t, 2)), 4)
        rows = pl.ds(pl.multiple_of(pair * 64, 64), 64)
        w = wbuf[:, pl.ds(pair * 2, 2)].astype(F32).reshape(3 * 64, D).astype(BF16)
        taken = [mm(w, xs[0]), mm(w, xs[1]), mm(w, xc[:, HALO:])]
        for r in range(RADIX):
            lanes = slice(r * LANES, (r + 1) * LANES)
            streams = []
            for j in range(3):
                if r:
                    total = cols[11 + 3 * j, rows, :]
                else:
                    total = cols[18 + j, rows, :]
                    for i in range(2):
                        total = total + cols[9 + 3 * j + i, rows, :] * started[i]
                for i in range(3):
                    part = taken[i][64 * j : 64 * j + 64, lanes]
                    total = total + cols[3 * j + i, rows, :] * part
                streams.append(total)
            gated = streams[2] * streams[1]
            keep0[rows, lanes] = streams[0]
            keepg[rows, lanes] = gated
            stage[rows, r, :] = gated
        gsnd[rows] = stage[rows].astype(BF16)
        for i, j, l in spots:
            si = at_x[i] + at_y[j] + at_k[l]
            for e in range(2):
                cj = 2 * pair + e
                src, dst = gsnd.at[cj * SEQ + si], grcv.at[me]
                if (i, j, l) == (0, 0, 0):

                    @pl.when(cj != c)
                    def _():
                        put(src, dst, s3.at[1], r3.at[1], (si, cj))

                    @pl.when(cj == c)
                    def _():
                        pltpu.make_async_copy(src, dst, r3.at[1]).start()

                else:
                    put(src, dst, s3.at[1], r3.at[1], (si, cj))
        return carry

    lax.fori_loop(0, 4, gates, 0)

    for copy in consts:
        copy.wait()
    for i in range(6):
        at = 1 + i if i < 3 else 2 + i
        spins[i] = jnp.broadcast_to(spin_v[:, at : at + 1], (D, LANES))
    for h in range(RADIX):
        lanes = slice(h * LANES, (h + 1) * LANES)
        cs, sn = step_v[h : h + 1, :], step_v[RADIX + h : RADIX + h + 1, :]
        twid_v[0, :, lanes] = base_v[0] * cs - base_v[1] * sn
        twid_v[1, :, lanes] = base_v[1] * cs + base_v[0] * sn


    def whole(rcv):
        stage[...] = rcv[...].astype(F32)
        x = jnp.concatenate([stage[:, r, :] for r in range(RADIX)], axis=1).astype(BF16)
        for part in range(2):
            sect[part] = mm(first_v[part * D : (part + 1) * D, :], x) + mm(
                first_v[(2 + part) * D : (3 + part) * D, :], x
            )

    def turned():
        def ahead(step, carry):
            rows = pl.ds(pl.multiple_of(step * 32, 32), 32)
            re, im = [], []
            for r in range(RADIX):
                lanes = slice(r * LANES, (r + 1) * LANES)
                a, b = sect[0, rows, lanes], sect[1, rows, lanes]
                if r:
                    cs, sn = spins[r - 1, rows, :], spins[r + 2, rows, :]
                    a, b = a * cs + b * sn, b * cs - a * sn
                re.append(a)
                im.append(b)
            e0r, e0i, e1r, e1i = re[0] + re[2], im[0] + im[2], re[0] - re[2], im[0] - im[2]
            o0r, o0i, o1r, o1i = re[1] + re[3], im[1] + im[3], re[1] - re[3], im[1] - im[3]
            outs = [
                (e0r + o0r, e0i + o0i),
                (e1r + o1i, e1i - o1r),
                (e0r - o0r, e0i - o0i),
                (e1r - o1i, e1i + o1r),
            ]
            for h, (a, b) in enumerate(outs):
                cs = twid_v[0, rows, h * LANES : (h + 1) * LANES]
                sn = twid_v[1, rows, h * LANES : (h + 1) * LANES]
                high, low = split(jnp.concatenate([a * cs + b * sn, b * cs - a * sn], axis=1))
                chi[h, rows, :] = high
                clo[h, rows, :] = low
            return carry

        lax.fori_loop(0, D // 32, ahead, 0)

    def spectrum(h):
        high, low = chi[h], clo[h]
        return mm(high, fwd_v[0]) + mm(low, fwd_v[0]) + mm(high, fwd_v[1])

    wait(krcv, r3.at[0])
    whole(krcv)
    turned()
    for h in range(RADIX):
        spec[h] = spectrum(h)
    wait(grcv, r3.at[1])
    whole(grcv)
    turned()
    for h in range(RADIX):
        g, k = spectrum(h), spec[h]
        gr, gi, kr, ki = g[:, :LANES], g[:, LANES:], k[:, :LANES], k[:, LANES:]
        high, low = split(jnp.concatenate([gr * kr - gi * ki, gr * ki + gi * kr], axis=1))
        z = mm(high, inv_v[0]) + mm(low, inv_v[0]) + mm(high, inv_v[1])
        zr, zi = z[:, :LANES], z[:, LANES:]
        cs = twid_v[0, :, h * LANES : (h + 1) * LANES]
        sn = twid_v[1, :, h * LANES : (h + 1) * LANES]
        back[h, 0] = zr * cs - zi * sn
        back[h, 1] = zi * cs + zr * sn

    def behind(step, carry):
        lo = pl.multiple_of(step * 32, 32)
        rows = pl.ds(lo, 32)
        rows_im = pl.ds(pl.multiple_of(D + lo, 32), 32)
        re = [back[h, 0, rows, :] for h in range(RADIX)]
        im = [back[h, 1, rows, :] for h in range(RADIX)]
        e0r, e0i, e1r, e1i = re[0] + re[2], im[0] + im[2], re[0] - re[2], im[0] - im[2]
        o0r, o0i, o1r, o1i = re[1] + re[3], im[1] + im[3], re[1] - re[3], im[1] - im[3]
        outs = [
            (e0r + o0r, e0i + o0i),
            (e1r - o1i, e1i + o1r),
            (e0r - o0r, e0i - o0i),
            (e1r + o1i, e1i - o1r),
        ]
        for r, (a, b) in enumerate(outs):
            if r:
                cs, sn = spins[r - 1, rows, :], spins[r + 2, rows, :]
                a, b = a * cs - b * sn, b * cs + a * sn
            lanes = slice(r * LANES, (r + 1) * LANES)
            high, low = split(a)
            dhi[rows, lanes] = high
            dlo[rows, lanes] = low
            high, low = split(b)
            dhi[rows_im, lanes] = high
            dlo[rows_im, lanes] = low
        return carry

    lax.fori_loop(0, D // 32, behind, 0)
    last_hi, last_lo = last_v[0:D, :], last_v[D : 2 * D, :]
    def settle(h, carry):
        lanes_h = pl.ds(pl.multiple_of(h * HALF, HALF), HALF)
        high, low = dhi[:, lanes_h], dlo[:, lanes_h]
        settled = mm(last_hi, high) + mm(last_lo, high) + mm(last_hi, low)
        for r in range(PAIR):
            stage2[:, r, :] = settled[:, r * LANES : (r + 1) * LANES]
        ysnd[h] = stage2[...].astype(BF16)
        to_row = c * SEQ + s
        for i, j, l in spots:
            si = at_x[i] + at_y[j] + at_k[l]
            for far in FAR + (0,):
                if (i, j, l, far) != (0, 0, 0, 0):
                    cj = lax.rem(c + far, CH)
                    put(
                        ysnd.at[h, si * CH + cj],
                        yrcv.at[h, to_row],
                        s3.at[3 + h],
                        r3.at[3 + h],
                        (si, cj),
                    )
        pltpu.make_async_copy(ysnd.at[h, me], yrcv.at[h, to_row], r3.at[3 + h]).start()
        return carry

    lax.fori_loop(0, 2, settle, 0)

    def mix(h):
        wait(yrcv.at[h], r3.at[3 + h])
        cols_h = slice(h * HALF, (h + 1) * HALF)
        stage2[...] = yrcv[h].astype(F32)
        convolved = jnp.concatenate([stage2[:, r, :] for r in range(PAIR)], axis=1)
        convolved = convolved + pflat[:, DIRECT : DIRECT + 1] * keepg[:, cols_h]
        mixed = (keep0[:, cols_h] * convolved).astype(BF16)
        osnd[h] = (mm(wout_v[...], mixed) + pflat[:, OUTB : OUTB + 1]).astype(BF16)
        o_dst = out_ref.at[:, pl.ds(pl.multiple_of(c * CHUNK + h * HALF, HALF), HALF)]
        for i in FAR:
            j = lax.rem(c + i, CH)
            put(
                osnd.at[h, pl.ds(pl.multiple_of(j * OWN, OWN), OWN), :],
                o_dst,
                s6.at[h],
                r6.at[h],
                (s, j),
            )
        pltpu.make_async_copy(osnd.at[h, rows_own, :], o_dst, r6.at[h]).start()

    mix(0)
    mix(1)

    for h in range(2):
        wait(out_ref.at[:, pl.ds(0, SPAN // 2)], r6.at[h])
    most = pl.ds(0, CH - 1)
    wait(pbuf.at[most, 0], s1.at[0])
    wait(wbuf.at[:, most, 0, :, pl.ds(0, LANES)], s1.at[1])
    wait(wbuf.at[:, pl.ds(0, 6), pl.ds(0, 2)], s1.at[5])
    wait(wbuf.at[:, :, pl.ds(0, 2)], s1.at[6])
    wait(xc.at[pl.ds(0, D - OWN), pl.ds(HALO, CHUNK)], s1.at[2])
    tails = pl.ds(0, OWN)
    wait(xc.at[pl.ds(0, 6 * OWN), pl.ds(0, HALO)], s1.at[3])

    @pl.when(c == 0)
    def _():
        wait(xc.at[tails, pl.ds(0, HALO)], s1.at[3])

    @pl.when(s < SEQ - 1)
    def _():
        wait(xc.at[tails, pl.ds(0, HALO)], s1.at[3])

    wait(pbuf.at[pl.ds(0, 6)], s1.at[4])
    wait(ksnd.at[pl.ds(0, SEQ - 1)], s3.at[0])
    wait(gsnd.at[pl.ds(0, DEV - 1)], s3.at[1])
    for h in range(2):
        wait(ysnd.at[h, pl.ds(0, DEV - 1)], s3.at[3 + h])
        wait(osnd.at[h, pl.ds(0, D - OWN), :], s6.at[h])


def body(
    inputs,
    w_in,
    b_in,
    short_kernel,
    positional,
    filter_in,
    filter_bias,
    filter_freq,
    filter_hidden,
    filter_out,
    decay,
    conv_bias,
    w_out,
    b_out,
):
    dma = pltpu.SemaphoreType.DMA
    hbm = pl.BlockSpec(memory_space=pl.ANY)
    vmem = pltpu.VMEM
    return pl.pallas_call(
        kernel,
        out_shape=pltpu.VMEM((OWN, SPAN), BF16),
        in_specs=[hbm] * 21,
        out_specs=pl.BlockSpec(memory_space=pltpu.VMEM),
        scratch_shapes=[
            vmem((3, OWN), F32),
            vmem((3, 3, OWN), F32),
            vmem((OWN, ORDER), F32),
            vmem((1, OWN), F32),
            vmem((1, OWN), F32),
            vmem((1, OWN), F32),
            vmem((5, SPAN), F32),
            vmem((5, ORDER), F32),
            vmem((3, ORDER), F32),
            vmem((3, ORDER), F32),
            vmem((2, ORDER, ORDER), F32),
            vmem((D, D), BF16),
            vmem((16, OWN), F32),
            vmem((16, ORDER), F32),
            vmem((OWN, LANES), F32),
            vmem((4, 8, LANES), BF16),
            vmem((D, HALO + CHUNK), BF16),
            vmem((3, CH, 4, 8, D), BF16),
            vmem((CH, 4, 8, LANES), BF16),
            vmem((D, LANES), F32),
            vmem((2, D, CHUNK), BF16),
            vmem((21, D, LANES), F32),
            vmem((6, D, LANES), F32),
            vmem((DEV, RADIX, LANES), F32),
            vmem((DEV, PAIR, LANES), F32),
            vmem((D, CHUNK), F32),
            vmem((D, CHUNK), F32),
            vmem((3, D, D), F32),
            vmem((3, 2 * D, D), BF16),
            vmem((2, D, WIDE), BF16),
            vmem((D, WIDE), F32),
            vmem((OWN, CH, RADIX, LANES), F32),
            vmem((OWN, CH, RADIX, LANES), BF16),
            vmem((DEV, RADIX, LANES), BF16),
            vmem((DEV, RADIX, LANES), BF16),
            vmem((DEV, RADIX, LANES), BF16),
            vmem((4 * D, D), BF16),
            vmem((2 * D, 2 * D), BF16),
            vmem((2, D, D), BF16),
            vmem((2, D, D), BF16),
            vmem((2, D, LANES), F32),
            vmem((2 * RADIX, LANES), F32),
            vmem((D, LANES), F32),
            vmem((2, D, CHUNK), F32),
            vmem((2, D, CHUNK), F32),
            vmem((RADIX, D, 2 * LANES), BF16),
            vmem((RADIX, D, 2 * LANES), BF16),
            vmem((RADIX, D, 2 * LANES), F32),
            vmem((RADIX, 2, D, LANES), F32),
            vmem((2 * D, CHUNK), BF16),
            vmem((2 * D, CHUNK), BF16),
            vmem((2, DEV, PAIR, LANES), BF16),
            vmem((2, DEV, PAIR, LANES), BF16),
            vmem((2, D, HALF), BF16),
            dma((12,)),
            dma((7,)),
            dma((3,)),
            pltpu.SemaphoreType.REGULAR,
            dma((8,)),
            dma((8,)),
            dma((5,)),
            dma((5,)),
            dma((2,)),
            dma((2,)),
        ],
        compiler_params=pltpu.CompilerParams(collective_id=0, has_side_effects=True),
    )(
        inputs,
        w_in,
        b_in,
        short_kernel.transpose(0, 2, 1),
        filter_out,
        decay.reshape(1, OWN),
        conv_bias.reshape(1, OWN),
        b_out.reshape(1, OWN),
        positional,
        filter_in.T,
        filter_bias,
        filter_freq,
        filter_hidden,
        w_out,
        *tables(),
    )


def solution(mesh):
    in_specs = (
        P("ch", "seq"),
        P(None, "ch", None),
        P(None, "ch"),
        P(None, "ch", None),
        P(None, "seq"),
        P(),
        P(),
        P(),
        P(),
        P("ch", None),
        P("ch"),
        P("ch"),
        P(),
        P("ch"),
    )
    return jax.shard_map(
        body, mesh=mesh, in_specs=in_specs, out_specs=P("ch", "seq"), check_vma=False
    )
```
